32 devices in a mesh: dp: 4 (over x, core), expert: 8 (over z, y).
Axes of the slice: x: 2, y: 2, z: 4, core: 2. Of those that a mesh axis runs over, the one named last changes fastest.
Arguments:
- tokens: bfloat16 [16384, 768], P(('dp', 'expert')), may hold values from -6 to 6
- cotangent: bfloat16 [16384, 768], P(('dp', 'expert')), may hold values from -6 to 6
- chosen: int32 [16384, 2], P(('dp', 'expert')), may hold values from 0 to 9, all different within a row; in each aligned block of 512 rows (0 to 511, 512 to 1023, ...) at most 128 rows name the same one
- gates: float32 [16384, 2], P(('dp', 'expert')), may hold values from 0.2 to 0.8
- lengths: int32 [32, 8], P(('dp', 'expert')), may hold values from 1 to 256, 512 in all within a row
- keep_mask: int32 [16384], P(('dp', 'expert')), may hold values 0 or 1
- gain1: float32 [768], replicated, may hold values from 0.5 to 1.5
- w_qkv: bfloat16 [768, 2304], replicated, may hold values from -0.21875 to 0.21875
- w_o: bfloat16 [768, 768], replicated, may hold values from -0.875 to 0.875
- gain2: float32 [768], replicated, may hold values from 0.5 to 1.5
- frozen_in: bfloat16 [2, 3072, 768], replicated, may hold values from -0.21875 to 0.21875
- frozen_out: bfloat16 [2, 3072, 768], replicated, may hold values from -0.109375 to 0.109375
- w_in: bfloat16 [8, 3072, 768], P('expert', 'dp'), may hold values from -0.21875 to 0.21875
- w_out: bfloat16 [8, 3072, 768], P('expert', 'dp'), may hold values from -0.109375 to 0.109375
Outputs:
- output: bfloat16 [16384, 768], P(('dp', 'expert'))
- d_tokens: bfloat16 [16384, 768], P(('dp', 'expert'))
- d_gain1: float32 [768], replicated
- d_w_qkv: float32 [768, 2304], replicated
- d_w_o: float32 [768, 768], replicated
- d_gain2: float32 [768], replicated
- d_w_in: float32 [8, 3072, 768], P('expert', 'dp')
- d_w_out: float32 [8, 3072, 768], P('expert', 'dp')
- counts: float32 [10], replicated
The draws below stay inside these ranges and needn't reach their ends.
Inputs may be any that keep to these rules, and one draw needn't show every extreme that they name: `chosen`: each token names two different experts; among the 512 tokens of one device no expert is named more than 128 times, a bound that some block reaches. The 8 lengths of a device sum to 512; the longest is exactly 256.
All inputs are finite; a program needn't handle non-finite values. No bound on the sum of `keep_mask` on one device may be relied on, other than what follows from the above.
Results may differ from the reference program's by a relative error of at most 0.012.
Values may be sent and summed in bfloat16 or wider, within the bound.
A program may use at most 256 MiB of HBM per device.

```python
import math
import jax
import jax.numpy as jnp
import numpy as np
from jax import lax

D = 768
HEADS = 12
HEAD_DIM = 64
FF = 3072
FROZEN = 2
TOK_DEV = 512
DOCS = 8
EXPERTS = 8
NEXP = 10
CAP = 128
TOKENS = 16384
GROUPS = 32
N_DP = 4
N_EXPERT = 8


def set_ends(values, own_key, smallest, top_value):
    shape = values.shape
    place = [jax.random.randint(jax.random.fold_in(own_key, axis), (), 0, shape[axis]) for axis in range(len(shape))]
    values = values.at[tuple(place)].set(smallest)
    longest = shape.index(max(shape))
    place[longest] = (place[longest] + 1) % shape[longest]
    return values.at[tuple(place)].set(top_value)


def levels(rng, extent, shards, smallest, largest):
    gain = 1.0
    for position, blocks in shards:
        draws = jax.random.uniform(jax.random.fold_in(jax.random.fold_in(rng, 6), position), (blocks,), jnp.float32, smallest / len(shards), largest / len(shards))
        gain = gain * jnp.repeat(jnp.exp(draws), extent[position] // blocks).reshape((-1,) + (1,) * (len(extent) - 1 - position))
    return gain


def profile(number_of, total, limit, slope):
    loads = [(1 << 20) // math.isqrt(standing ** slope) + 1 for standing in range(2, number_of + 1)]
    spare, given = total - limit - (number_of - 1), [1] * (number_of - 1)
    while spare > 0:
        candidates = [i for i in range(number_of - 1) if given[i] < limit]
        whole, remaining = sum([loads[i] for i in candidates]), spare
        for i in candidates:
            more = min(limit - given[i], max(1, remaining * loads[i] // whole), spare)
            given[i] = given[i] + more
            spare = spare - more
    return np.array([limit] + given)


def uneven(key, count, total, limit, slope):
    if count == 2:
        one = jax.random.randint(key, (), max(1, total - limit), min(limit, total - 1) + 1)
        return jnp.stack([one, total - one])
    sizes = jnp.asarray(profile(count, total, limit, slope), jnp.int32)
    twos = (count - 1) // 2
    source_of, sink = sizes[1:1 + 2 * twos:2], sizes[2:2 + 2 * twos:2]
    room = jnp.minimum(source_of - 1, limit - sink)
    shifted = jax.random.randint(jax.random.fold_in(key, 1), (twos,), 0, 1 << 20) % (room + 1)
    sizes = sizes.at[1:1 + 2 * twos:2].set(source_of - shifted).at[2:2 + 2 * twos:2].set(sink + shifted)
    return sizes[jax.random.permutation(jax.random.fold_in(key, 2), count)]


def shared_out(key, own, number, rows, amount, top, most, lean):
    ranking = jax.random.permutation(key, amount)
    crowded, common = shares(amount, rows * top, most, lean, True), shares(amount, rows * top, most, lean, False)
    places = jnp.arange(amount)

    def named(sizes, turn):
        used = int((sizes > 0).sum())
        fixed = max(1, used // 4)
        moved = fixed + (places - fixed + turn * (used - fixed)) % max(1, amount - fixed)
        return jnp.zeros((amount,), jnp.int32).at[ranking[jnp.where(places < fixed, places, moved)]].set(jnp.asarray(sizes, jnp.int32))

    sizes = jnp.where(number % 4 == 0, named(crowded, number // 4), named(common, number - number // 4 - 1))
    mixed = jax.random.permutation(jax.random.fold_in(own, 3), amount)
    donor, taker = mixed[0:amount // 2 * 2:2], mixed[1:amount // 2 * 2:2]
    room = jnp.minimum(sizes[donor] - 1, most - sizes[taker]) // 2
    room = jnp.where((donor == ranking[0]) | (taker == ranking[0]) | (sizes[taker] == 0), 0, jnp.maximum(room, 0))
    moved = jax.random.randint(jax.random.fold_in(own, 4), (amount // 2,), 0, 1 << 20) % (room + 1)
    sizes = sizes.at[donor].add(-moved).at[taker].add(moved)
    labels = jnp.searchsorted(jnp.cumsum(sizes), jnp.arange(rows * top), side="right").astype(jnp.int32)
    listing = labels.reshape(top, rows).T
    listing = listing[jax.random.permutation(jax.random.fold_in(own, 1), rows)]
    turn = jax.random.randint(jax.random.fold_in(own, 2), (rows, 1), 0, top)
    return jnp.take_along_axis(listing, (jnp.arange(top)[None, :] + turn) % top, axis=1)


def shares(number_of, total, reach, lean, full):
    loads = [(1 << 20) // math.isqrt(standing ** lean) + 1 for standing in range(1, number_of + 1)]
    largest = reach if full else min(reach, max(-(-total // number_of), total * loads[0] // sum(loads)))
    least = 1 if total - largest >= number_of - 1 else 0
    holding, rest = [largest] + [least] * (number_of - 1), total - largest - least * (number_of - 1)
    while rest > 0:
        free = [i for i in range(1, number_of) if holding[i] < largest] or [i for i in range(1, number_of) if holding[i] < reach]
        mass, left = sum([loads[i] for i in free]), rest
        for i in free:
            extra = min(reach - holding[i], max(1, left * loads[i] // mass), rest)
            holding[i] = holding[i] + extra
            rest = rest - extra
    return np.array(holding)


def gaussian(rng, dims, deviation, reach, cuts=(), kind=jnp.bfloat16):
    entries = jax.random.normal(rng, dims, jnp.float32) * deviation
    if len(cuts) > 0:
        entries = levels(rng, dims, cuts, -0.22, 0.18) * entries
    return jnp.clip(entries, min=-reach, max=reach).astype(kind)


def setup_inputs(seed: int = 0) -> dict:
    seeds = jax.random.split(jax.random.key(seed), 15)
    tokens = gaussian(seeds[0], (TOKENS, D), 1.0, 6.0, ((0, 32),))
    cotangent = gaussian(seeds[1], (TOKENS, D), 1.0, 6.0, ((0, 32),))
    chosen_keys = jax.random.split(jax.random.fold_in(seeds[2], 1), TOKENS // TOK_DEV)
    chosen_turns = jax.random.permutation(jax.random.fold_in(seeds[2], 3), TOKENS // TOK_DEV)
    chosen = jax.vmap(lambda own, number: shared_out(jax.random.fold_in(seeds[2], 2), own, number, TOK_DEV, NEXP, 2, CAP, 1))(chosen_keys, chosen_turns).reshape((TOKENS, 2))
    gates = jnp.clip(0.2 + 0.6 * jax.random.uniform(seeds[3], (TOKENS, 2), jnp.float32) ** levels(seeds[3], (TOKENS, 2), ((0, 32),), -0.2, 0.2), 0.2, 0.8)
    lengths = jax.vmap(lambda own: uneven(own, DOCS, TOK_DEV, TOK_DEV // 2, 2))(jax.random.split(seeds[4], GROUPS)).reshape((GROUPS, DOCS)).astype(jnp.int32)
    keep_mask = set_ends((jax.random.randint(seeds[5], (TOKENS,), 0, 8) < 7).astype(jnp.int32), jax.random.fold_in(seeds[5], 1), 0, 1)
    gain1 = jnp.clip(1.0 + 0.1 * jax.random.normal(seeds[6], (D,), jnp.float32), 0.5, 1.5)
    w_qkv = gaussian(seeds[7], (D, 3 * D), D ** -0.5, 0.21875)
    w_o = gaussian(seeds[8], (D, D), (D // 16) ** -0.5, 0.875)
    gain2 = jnp.clip(1.0 + 0.1 * jax.random.normal(seeds[9], (D,), jnp.float32), 0.5, 1.5)
    frozen_in = gaussian(seeds[10], (FROZEN, FF, D), D ** -0.5, 0.21875)
    frozen_out = gaussian(seeds[11], (FROZEN, FF, D), FF ** -0.5, 0.109375)
    w_in = gaussian(seeds[12], (EXPERTS, FF, D), D ** -0.5, 0.21875, ((0, 8), (1, 4)))
    w_out = gaussian(seeds[13], (EXPERTS, FF, D), FF ** -0.5, 0.109375, ((0, 8), (1, 4)))
    return dict(tokens=tokens, cotangent=cotangent, chosen=chosen, gates=gates, lengths=lengths, keep_mask=keep_mask, gain1=gain1, w_qkv=w_qkv, w_o=w_o, gain2=gain2, frozen_in=frozen_in, frozen_out=frozen_out, w_in=w_in, w_out=w_out)


@jax.custom_vjp
def low(v):
    return lax.optimization_barrier(v.astype(jnp.bfloat16)).astype(jnp.float32)

@jax.custom_vjp
def low_back(v):
    return v

def low_keep(v):
    return (low(v), None)

def low_pass(kept, grad):
    return (grad,)

def back_keep(v):
    return (v, None)

def back_low(kept, grad):
    return (low(grad),)
low.defvjp(low_keep, low_pass)
low_back.defvjp(back_keep, back_low)
HIGHEST_MODE = lax.Precision.HIGHEST

def layer_norm(values_in, gain_vec):
    row_mean = lax.optimization_barrier(jnp.mean(values_in, axis=-1, keepdims=True))
    centred = values_in - row_mean
    variance = lax.optimization_barrier(jnp.mean(centred * centred, axis=-1, keepdims=True))
    return centred * lax.rsqrt(variance + 1e-05) * gain_vec

def slot_positions(chosen_ids):
    flat_ids = chosen_ids.reshape(-1)
    one_hot = (flat_ids[:, None] == jnp.arange(NEXP, dtype=jnp.int32)[None, :]).astype(jnp.int32)
    slot_ranks = lax.optimization_barrier(jnp.sum(jnp.cumsum(one_hot, axis=0) * one_hot, axis=1)) - 1
    return (flat_ids * CAP + slot_ranks).astype(jnp.int32)

def device_layer(params, inputs):
    gain_one, qkv_weight, out_weight, gain_two, up_all, down_all = params
    rows_in, chosen_ids, gate_vals, doc_lengths, keep_flags = inputs
    normed_one = low(layer_norm(rows_in, gain_one))
    projected = low_back(low(jnp.dot(normed_one, qkv_weight, precision=HIGHEST_MODE)))
    queries = projected[:, :D].reshape(TOK_DEV, HEADS, HEAD_DIM)
    key_heads = projected[:, D:2 * D].reshape(TOK_DEV, HEADS, HEAD_DIM)
    value_heads = projected[:, 2 * D:].reshape(TOK_DEV, HEADS, HEAD_DIM)
    places = jnp.arange(TOK_DEV, dtype=jnp.int32)
    doc_ends = jnp.cumsum(doc_lengths)
    documents = lax.optimization_barrier(jnp.sum((places[:, None] >= doc_ends[None, :]).astype(jnp.int32), axis=1))
    allowed = (documents[:, None] == documents[None, :]) & (places[None, :] <= places[:, None]) & ((keep_flags[None, :] > 0) | (places[None, :] == places[:, None]))
    scores = low_back(jnp.einsum('qhd,khd->hqk', queries, key_heads, precision=HIGHEST_MODE) * 0.125)
    scores = jnp.where(allowed[None], scores, -1e+30)
    peak_score = lax.optimization_barrier(jnp.max(scores, axis=-1, keepdims=True))
    exp_scores = jnp.exp(scores - peak_score)
    probabilities = low(exp_scores / lax.optimization_barrier(jnp.sum(exp_scores, axis=-1, keepdims=True)))
    attended = jnp.einsum('hqk,khd->qhd', probabilities, value_heads, precision=HIGHEST_MODE).reshape(TOK_DEV, D)
    attended = low_back(low(attended))
    mixed_rows = rows_in + low_back(jnp.dot(attended, out_weight, precision=HIGHEST_MODE))
    normed_two = low(layer_norm(mixed_rows, gain_two))
    positions = slot_positions(chosen_ids)
    buffer_rows = jnp.zeros((NEXP * CAP, D), jnp.float32).at[positions].set(jnp.repeat(normed_two, 2, axis=0))
    buffer_rows = low_back(buffer_rows).reshape(NEXP, CAP, D)
    hidden = low_back(jnp.einsum('gcd,gfd->gcf', buffer_rows, up_all, precision=HIGHEST_MODE))
    active = low(jax.nn.gelu(hidden))
    results = low_back(low(jnp.einsum('gcf,gfd->gcd', active, down_all, precision=HIGHEST_MODE))).reshape(NEXP * CAP, D)
    picked = results[positions].reshape(TOK_DEV, 2, D)
    return mixed_rows + lax.optimization_barrier(jnp.sum(picked * gate_vals[:, :, None], axis=1))

def reference(tokens, cotangent, chosen, gates, lengths, keep_mask, gain1, w_qkv, w_o, gain2, frozen_in, frozen_out, w_in, w_out):
    groups = N_DP * N_EXPERT
    frozen_up = frozen_in.astype(jnp.float32)
    frozen_down = frozen_out.astype(jnp.float32)
    inputs_rest = (chosen.reshape(groups, TOK_DEV, 2), gates.astype(jnp.float32).reshape(groups, TOK_DEV, 2), lengths, keep_mask.reshape(groups, TOK_DEV))

    def forward(gain_one, qkv_weight, out_weight, gain_two, up_new, down_new, rows_all):
        params = (gain_one, qkv_weight, out_weight, gain_two, jnp.concatenate([frozen_up, up_new], axis=0), jnp.concatenate([frozen_down, down_new], axis=0))
        stepper = jax.checkpoint(device_layer)

        def scan_step(carry_in, per_device):
            return (carry_in, stepper(params, per_device))
        _, stacked = lax.scan(scan_step, jnp.zeros((), jnp.float32), (rows_all.reshape(groups, TOK_DEV, D),) + inputs_rest)
        return stacked.reshape(groups * TOK_DEV, D)
    result_all, pullback = jax.vjp(forward, gain1.astype(jnp.float32), w_qkv.astype(jnp.float32), w_o.astype(jnp.float32), gain2.astype(jnp.float32), w_in.astype(jnp.float32), w_out.astype(jnp.float32), tokens.astype(jnp.float32))
    grads = pullback(cotangent.astype(jnp.float32))
    counts = lax.optimization_barrier(jnp.sum((chosen.reshape(-1)[:, None] == jnp.arange(NEXP, dtype=jnp.int32)[None, :]).astype(jnp.float32), axis=0))
    return (result_all.astype(jnp.bfloat16), grads[6].astype(jnp.bfloat16), grads[0], grads[1], grads[2], grads[3], grads[4], grads[5], counts)
```

```python
import functools
import jax
import jax.numpy as jnp
from jax import lax
from jax.experimental import pallas as pl
from jax.experimental.pallas import tpu as pltpu
from jax.sharding import PartitionSpec as P

MESH = pl.DeviceIdType.MESH


def butterfly(dp_size, ex_size):
    core = ("dp", 1)
    xs = [("dp", 2 << k) for k in range((dp_size // 2).bit_length() - 1)]
    depth = 4 if ex_size % 4 == 0 else 1
    wide = ex_size // depth
    ys = [("expert", 1 << k) for k in range(wide.bit_length() - 1)]
    zs = [("expert", wide << k) for k in range(depth.bit_length() - 1)]
    return core, xs, ys, zs


def partner_of(step):
    axis, mask = step
    place = {"dp": lax.axis_index("dp"), "expert": lax.axis_index("expert")}
    bit = lax.rem(place[axis] // mask, 2)
    place[axis] = place[axis] + mask - 2 * mask * bit
    return bit, (place["dp"], place["expert"])


def reduce_kernel(dp_size, ex_size, w_ref, s_ref, out_ref, sum_ref, acc, got, small, ssem, rsem, gsem, hsem, tsem, usem):
    core, xs, ys, zs = butterfly(dp_size, ex_size)
    orders = [[core] + xs + ys + zs, [core] + ys + zs + xs, [core] + zs + xs + ys]
    count = len(orders[0])
    parts = len(orders)
    rows = w_ref.shape[0] // parts
    barrier = pltpu.get_barrier_semaphore()
    for step in orders[0]:
        _, peer = partner_of(step)
        pl.semaphore_signal(barrier, inc=1, device_id=peer, device_id_type=MESH)
    pl.semaphore_wait(barrier, count)

    offs = [[p * rows] for p in range(parts)]
    land = [[p * rows] for p in range(parts)]

    def scatter_send(p, i):
        bit, peer = partner_of(orders[p][i])
        half = rows >> (i + 1)
        source = w_ref if i == 0 else acc
        give = pl.multiple_of(offs[p][i] + (1 - bit) * half, half)
        copy = pltpu.make_async_remote_copy(
            src_ref=source.at[pl.ds(give, half)],
            dst_ref=got.at[pl.ds(land[p][i], half)],
            send_sem=ssem.at[p, i], recv_sem=rsem.at[p, i],
            device_id=peer, device_id_type=MESH)
        copy.start()
        offs[p].append(offs[p][i] + bit * half)
        land[p].append(land[p][i] + half)
        return copy

    def small_send(i):
        _, peer = partner_of(orders[0][i])
        copy = pltpu.make_async_remote_copy(
            src_ref=s_ref if i == 0 else small.at[count + i], dst_ref=small.at[i],
            send_sem=tsem.at[i], recv_sem=usem.at[i], device_id=peer, device_id_type=MESH)
        copy.start()
        return copy

    live = [scatter_send(p, 0) for p in range(parts)]
    tiny = small_send(0)
    for i in range(count):
        half = rows >> (i + 1)
        for p in range(parts):
            live[p].wait()
            source = w_ref if i == 0 else acc
            target = acc if i + 1 < count else out_ref
            keep = offs[p][i + 1]
            tile = min(half, 128)

            def add(j, _, keep=keep, start=land[p][i], source=source, target=target, tile=tile):
                at = pl.ds(pl.multiple_of(keep + j * tile, tile), tile)
                other = got[pl.ds(pl.multiple_of(start + j * tile, tile), tile), :]
                target[at, :] = (source[at, :].astype(jnp.float32) + other.astype(jnp.float32)).astype(jnp.bfloat16)
                return 0

            lax.fori_loop(0, half // tile, add, 0)
            if i + 1 < count:
                live[p] = scatter_send(p, i + 1)
        tiny.wait()
        mine = s_ref[...] if i == 0 else small[count + i]
        total = mine + small[i]
        if i + 1 < count:
            small[count + i + 1] = total
            tiny = small_send(i + 1)
        else:
            sum_ref[...] = total

    def gather_send(p, i):
        _, peer = partner_of(orders[p][i])
        half = rows >> (i + 1)
        at = pl.ds(pl.multiple_of(offs[p][i + 1], half), half)
        copy = pltpu.make_async_remote_copy(
            src_ref=out_ref.at[at], dst_ref=out_ref.at[at],
            send_sem=gsem.at[p, i], recv_sem=hsem.at[p, i], device_id=peer, device_id_type=MESH)
        copy.start()
        return copy

    for i in reversed(range(count)):
        live = [gather_send(p, i) for p in range(parts)]
        for p in range(parts):
            live[p].wait()


def all_reduce(blocks, small, dp_size, ex_size):
    steps = (dp_size * ex_size).bit_length() - 1
    rows, width = blocks.shape
    vmem = pl.BlockSpec(memory_space=pltpu.VMEM)
    dma = pltpu.SemaphoreType.DMA
    return pl.pallas_call(
        functools.partial(reduce_kernel, dp_size, ex_size),
        out_shape=(jax.ShapeDtypeStruct(blocks.shape, jnp.bfloat16), jax.ShapeDtypeStruct(small.shape, jnp.float32)),
        in_specs=[vmem, vmem],
        out_specs=(vmem, vmem),
        scratch_shapes=[
            pltpu.VMEM((rows, width), jnp.bfloat16),
            pltpu.VMEM((rows, width), jnp.bfloat16),
            pltpu.VMEM((2 * steps,) + small.shape, jnp.float32),
            dma((3, steps)), dma((3, steps)), dma((3, steps)), dma((3, steps)), dma((steps,)), dma((steps,)),
        ],
        compiler_params=pltpu.CompilerParams(collective_id=3, has_side_effects=True, vmem_limit_bytes=48 << 20),
        name="reduce_gradients",
    )(blocks, small)


HEADS = 12
HEAD_DIM = 64
FROZEN = 2


def layer_norm(values_in, gain_vec):
    row_mean = jnp.mean(values_in, axis=-1, keepdims=True)
    centred = values_in - row_mean
    variance = jnp.mean(centred * centred, axis=-1, keepdims=True)
    return centred * lax.rsqrt(variance + 1e-05) * gain_vec


def expert_forward(rows_low, up_weights, down_weights):
    hidden = jnp.einsum("gcd,gfd->gcf", rows_low, up_weights, preferred_element_type=jnp.float32)
    active = jax.nn.gelu(hidden).astype(jnp.bfloat16)
    result_rows = jnp.einsum(
        "gcf,gfd->gcd", active, down_weights, preferred_element_type=jnp.float32
    ).astype(jnp.bfloat16)
    return (result_rows, hidden)


def expert_backward(result_grad, hidden, up_weights, down_weights):
    active_grad = jnp.einsum(
        "gcd,gfd->gcf", result_grad, down_weights, preferred_element_type=jnp.float32
    )
    active, gelu_back = jax.vjp(jax.nn.gelu, hidden)
    hidden_grad = gelu_back(active_grad)[0].astype(jnp.bfloat16)
    input_grad = jnp.einsum(
        "gcf,gfd->gcd", hidden_grad, up_weights, preferred_element_type=jnp.float32
    ).astype(jnp.bfloat16)
    return (input_grad, hidden_grad, active.astype(jnp.bfloat16))


def block_scores(query_part, key_heads, allowed):
    scores = (
        jnp.einsum("qhd,khd->hqk", query_part, key_heads, preferred_element_type=jnp.float32)
        * 0.125
    )
    return jnp.where(allowed[None], scores, -1e30)


def body(
    tokens,
    cotangent,
    chosen,
    gates,
    lengths,
    keep_mask,
    gain1,
    w_qkv,
    w_o,
    gain2,
    frozen_in,
    frozen_out,
    w_in,
    w_out,
):
    row_count = tokens.shape[0]
    feat_width = tokens.shape[1]
    owners = lax.axis_size("expert")
    kind_count = FROZEN + owners
    slot_count = (2 * row_count * 5 // (4 * kind_count) + 7) // 8 * 8
    block_rows = min(512, row_count)
    weights_in, weights_out = (
        lax.all_gather(w_in, "dp", axis=1, tiled=True),
        lax.all_gather(w_out, "dp", axis=1, tiled=True),
    )
    tokens_full = tokens.astype(jnp.float32)
    normed_one, norm_one_back = jax.vjp(layer_norm, tokens_full, gain1)
    normed_one_low = normed_one.astype(jnp.bfloat16)
    projected = jnp.dot(normed_one_low, w_qkv, preferred_element_type=jnp.float32).astype(
        jnp.bfloat16
    )
    queries = projected[:, :feat_width].reshape(row_count, HEADS, HEAD_DIM)
    key_heads = projected[:, feat_width : 2 * feat_width].reshape(row_count, HEADS, HEAD_DIM)
    value_heads = projected[:, 2 * feat_width :].reshape(row_count, HEADS, HEAD_DIM)
    places = jnp.arange(row_count, dtype=jnp.int32)
    doc_ends = jnp.cumsum(lengths[0])
    documents = jnp.sum((places[:, None] >= doc_ends[None, :]).astype(jnp.int32), axis=1)

    def permitted():
        return (
            (documents[:, None] == documents[None, :])
            & (places[None, :] <= places[:, None])
            & ((keep_mask[None, :] > 0) | (places[None, :] == places[:, None]))
        )

    scores = block_scores(queries, key_heads, permitted())
    peak_score = jnp.max(scores, axis=-1, keepdims=True)
    exp_scores = jnp.exp(scores - peak_score)
    exp_total = jnp.sum(exp_scores, axis=-1, keepdims=True)
    probs_low = (exp_scores / exp_total).astype(jnp.bfloat16)
    block_out = jnp.einsum(
        "hqk,khd->qhd", probs_low, value_heads, preferred_element_type=jnp.float32
    )
    out_blocks = block_out.reshape(block_rows, feat_width).astype(jnp.bfloat16)
    lse_blocks = [peak_score + jnp.log(exp_total)]
    mixed_rows = tokens_full + jnp.dot(out_blocks, w_o, preferred_element_type=jnp.float32)
    normed_two, norm_two_back = jax.vjp(layer_norm, mixed_rows, gain2)
    normed_two_low = normed_two.astype(jnp.bfloat16)
    flat_ids = chosen.reshape(-1)
    one_hot = (flat_ids[:, None] == jnp.arange(kind_count, dtype=jnp.int32)[None, :]).astype(
        jnp.int32
    )
    slot_ranks = jnp.sum(jnp.cumsum(one_hot, axis=0) * one_hot, axis=1) - 1
    positions = flat_ids * slot_count + slot_ranks
    buffer_rows = (
        jnp.zeros((kind_count * slot_count, feat_width), jnp.bfloat16)
        .at[positions]
        .set(jnp.repeat(normed_two_low, 2, axis=0))
    )
    local_rows = buffer_rows[: FROZEN * slot_count].reshape(FROZEN, slot_count, feat_width)
    routed_rows = buffer_rows[FROZEN * slot_count :].reshape(owners, slot_count, feat_width)
    arrived_rows = lax.all_to_all(routed_rows, "expert", split_axis=0, concat_axis=0, tiled=True)
    result_rows, _ = expert_forward(
        arrived_rows.reshape(1, -1, feat_width), weights_in, weights_out
    )
    served = result_rows.reshape(arrived_rows.shape)
    frozen_result, frozen_hidden = expert_forward(local_rows, frozen_in, frozen_out)
    returned = lax.all_to_all(served, "expert", split_axis=0, concat_axis=0, tiled=True)
    results = jnp.concatenate(
        [frozen_result.reshape(-1, feat_width), returned.reshape(-1, feat_width)], axis=0
    )
    picked = results[positions].astype(jnp.float32).reshape(row_count, 2, feat_width)
    output = mixed_rows + jnp.sum(picked * gates[:, :, None], axis=1)
    grad_out = cotangent.astype(jnp.float32)
    weighted = (jnp.repeat(grad_out, 2, axis=0) * gates.reshape(-1, 1)).astype(jnp.bfloat16)
    grad_buffer = (
        jnp.zeros((kind_count * slot_count, feat_width), jnp.bfloat16).at[positions].set(weighted)
    )
    frozen_grad_rows = grad_buffer[: FROZEN * slot_count].reshape(FROZEN, slot_count, feat_width)
    routed_grad = grad_buffer[FROZEN * slot_count :].reshape(owners, slot_count, feat_width)
    arrived_grad = lax.all_to_all(routed_grad, "expert", split_axis=0, concat_axis=0, tiled=True)
    flat_rows = arrived_rows.reshape(1, -1, feat_width)
    flat_grad = arrived_grad.reshape(1, -1, feat_width)
    hidden_all = jnp.einsum(
        "gcd,gfd->gcf", flat_rows, weights_in, preferred_element_type=jnp.float32
    )
    row_input_grad, hidden_grad, active = expert_backward(
        flat_grad, hidden_all, weights_in, weights_out
    )
    sent_back = lax.all_to_all(
        row_input_grad.reshape(owners, slot_count, feat_width),
        "expert",
        split_axis=0,
        concat_axis=0,
        tiled=True,
    )
    frozen_input_grad, _, _ = expert_backward(
        frozen_grad_rows, frozen_hidden, frozen_in, frozen_out
    )
    hidden_rows = hidden_grad[0]
    active_rows = active[0]
    input_rows = flat_rows[0]
    output_rows = flat_grad[0]
    term_in = lax.dot_general(
        hidden_rows, input_rows, (((0,), (0,)), ((), ())), preferred_element_type=jnp.float32
    )
    term_out = lax.dot_general(
        active_rows, output_rows, (((0,), (0,)), ((), ())), preferred_element_type=jnp.float32
    )
    summed = lax.psum_scatter(
        jnp.concatenate([term_in, term_out], axis=1).astype(jnp.bfloat16),
        "dp", scatter_dimension=0, tiled=True
    ).astype(jnp.float32)
    d_w_in = summed[:, :feat_width][None]
    d_w_out = summed[:, feat_width:][None]
    row_grads = jnp.concatenate(
        [frozen_input_grad.reshape(-1, feat_width), sent_back.reshape(-1, feat_width)], axis=0
    )
    normed_two_grad = jnp.sum(
        row_grads[positions].astype(jnp.float32).reshape(row_count, 2, feat_width), axis=1
    )
    mixed_part, gain2_grad = norm_two_back(normed_two_grad)
    mixed_grad = grad_out + mixed_part
    branch_grad = mixed_grad.astype(jnp.bfloat16)
    w_o_grad = lax.dot_general(
        out_blocks, branch_grad, (((0,), (0,)), ((), ())), preferred_element_type=jnp.float32
    )
    attended_grad = lax.dot_general(
        branch_grad, w_o, (((1,), (1,)), ((), ())), preferred_element_type=jnp.float32
    ).astype(jnp.bfloat16)
    attended_heads = attended_grad.reshape(row_count, HEADS, HEAD_DIM)
    key_grad = jnp.zeros((row_count, HEADS, HEAD_DIM), jnp.float32)
    value_grad = jnp.zeros((row_count, HEADS, HEAD_DIM), jnp.float32)
    query_grads = []
    for block_index, row_start in enumerate(range(0, row_count, block_rows)):
        scores = block_scores(queries, key_heads, permitted())
        probs_full = jnp.exp(scores - lse_blocks[block_index])
        probs_low = probs_full.astype(jnp.bfloat16)
        prob_grad = jnp.einsum(
            "qhd,khd->hqk", attended_heads, value_heads, preferred_element_type=jnp.float32
        )
        row_delta = jnp.sum(probs_full * prob_grad, axis=-1, keepdims=True)
        score_grad = (probs_full * (prob_grad - row_delta)).astype(jnp.bfloat16)
        query_grads.append(
            jnp.einsum("hqk,khd->qhd", score_grad, key_heads, preferred_element_type=jnp.float32)
            * 0.125
        )
        key_grad = (
            jnp.einsum("hqk,qhd->khd", score_grad, queries, preferred_element_type=jnp.float32)
            * 0.125
        )
        value_grad = jnp.einsum(
            "hqk,qhd->khd", probs_low, attended_heads, preferred_element_type=jnp.float32
        )
    projected_grad = jnp.concatenate(
        [
            query_grads[0].reshape(row_count, feat_width),
            key_grad.reshape(row_count, feat_width),
            value_grad.reshape(row_count, feat_width),
        ],
        axis=1,
    ).astype(jnp.bfloat16)
    w_qkv_grad = lax.dot_general(
        normed_one_low, projected_grad, (((0,), (0,)), ((), ())), preferred_element_type=jnp.float32
    )
    normed_one_grad = lax.dot_general(
        projected_grad, w_qkv, (((1,), (1,)), ((), ())), preferred_element_type=jnp.float32
    )
    tokens_part, gain1_grad = norm_one_back(normed_one_grad)
    tokens_grad = (mixed_grad + tokens_part).astype(jnp.bfloat16)
    local_counts = jnp.sum(one_hot, axis=0).astype(jnp.float32)
    both = jnp.concatenate([w_qkv_grad, w_o_grad], axis=1).astype(jnp.bfloat16)
    half = feat_width // 2
    blocks = both.reshape(feat_width, 8, half).transpose(1, 0, 2).reshape(8 * feat_width, half)
    padded_counts = jnp.pad(local_counts, (0, feat_width - kind_count))
    small = jnp.concatenate(
        [gain1_grad[None], gain2_grad[None], padded_counts[None], jnp.zeros((5, feat_width), jnp.float32)])
    total, small_sum = all_reduce(blocks, small, lax.axis_size("dp"), owners)
    both_sum = total.reshape(8, feat_width, half).transpose(1, 0, 2).reshape(feat_width, 8 * half)
    w_qkv_sum = both_sum[:, : 3 * feat_width].astype(jnp.float32)
    w_o_sum = both_sum[:, 3 * feat_width :].astype(jnp.float32)
    gain1_sum, gain2_sum, counts = small_sum[0], small_sum[1], small_sum[2, :kind_count]
    return (
        output.astype(jnp.bfloat16),
        tokens_grad,
        gain1_sum,
        w_qkv_sum,
        w_o_sum,
        gain2_sum,
        d_w_in,
        d_w_out,
        counts,
    )


def solution(mesh):
    placed = (
        P(("dp", "expert"), None),
        P(("dp", "expert"), None),
        P(("dp", "expert"), None),
        P(("dp", "expert"), None),
        P(("dp", "expert"), None),
        P(("dp", "expert")),
        P(),
        P(),
        P(),
        P(),
        P(),
        P(),
        P("expert", "dp", None),
        P("expert", "dp", None),
    )
    return jax.shard_map(
        body,
        mesh=mesh,
        in_specs=placed,
        out_specs=(
            P(("dp", "expert"), None),
            P(("dp", "expert"), None),
            P(),
            P(),
            P(),
            P(),
            P("expert", "dp", None),
            P("expert", "dp", None),
            P(),
        ),
        check_vma=False,
    )
```

```python
import functools
import jax
import jax.numpy as jnp
from jax import lax
from jax.experimental import pallas as pl
from jax.experimental.pallas import tpu as pltpu
from jax.sharding import PartitionSpec as P

MESH = pl.DeviceIdType.MESH


def butterfly(dp_size, ex_size):
    core = ("dp", 1)
    xs = [("dp", 2 << k) for k in range((dp_size // 2).bit_length() - 1)]
    depth = 4 if ex_size % 4 == 0 else 1
    wide = ex_size // depth
    ys = [("expert", 1 << k) for k in range(wide.bit_length() - 1)]
    zs = [("expert", wide << k) for k in range(depth.bit_length() - 1)]
    return core, xs, ys, zs


def partner_of(step):
    axis, mask = step
    place = {"dp": lax.axis_index("dp"), "expert": lax.axis_index("expert")}
    bit = lax.rem(place[axis] // mask, 2)
    place[axis] = place[axis] + mask - 2 * mask * bit
    return bit, (place["dp"], place["expert"])


def reduce_kernel(dp_size, ex_size, w_ref, s_ref, out_ref, sum_ref, acc, got, small, ssem, rsem, gsem, hsem, tsem, usem):
    core, xs, ys, zs = butterfly(dp_size, ex_size)
    orders = [[core] + xs + ys + zs, [core] + ys + zs + xs, [core] + zs + xs + ys]
    count = len(orders[0])
    parts = len(orders)
    rows = w_ref.shape[0] // parts
    barrier = pltpu.get_barrier_semaphore()
    for step in orders[0]:
        _, peer = partner_of(step)
        pl.semaphore_signal(barrier, inc=1, device_id=peer, device_id_type=MESH)
    pl.semaphore_wait(barrier, count)

    offs = [[p * rows] for p in range(parts)]
    land = [[p * rows] for p in range(parts)]

    def scatter_send(p, i):
        bit, peer = partner_of(orders[p][i])
        half = rows >> (i + 1)
        source = w_ref if i == 0 else acc
        give = pl.multiple_of(offs[p][i] + (1 - bit) * half, half)
        copy = pltpu.make_async_remote_copy(
            src_ref=source.at[pl.ds(give, half)],
            dst_ref=got.at[pl.ds(land[p][i], half)],
            send_sem=ssem.at[p, i], recv_sem=rsem.at[p, i],
            device_id=peer, device_id_type=MESH)
        copy.start()
        offs[p].append(offs[p][i] + bit * half)
        land[p].append(land[p][i] + half)
        return copy

    def small_send(i):
        _, peer = partner_of(orders[0][i])
        copy = pltpu.make_async_remote_copy(
            src_ref=s_ref if i == 0 else small.at[count + i], dst_ref=small.at[i],
            send_sem=tsem.at[i], recv_sem=usem.at[i], device_id=peer, device_id_type=MESH)
        copy.start()
        return copy

    live = [scatter_send(p, 0) for p in range(parts)]
    tiny = small_send(0)
    for i in range(count):
        half = rows >> (i + 1)
        for p in range(parts):
            live[p].wait()
            source = w_ref if i == 0 else acc
            target = acc if i + 1 < count else out_ref
            keep = offs[p][i + 1]
            tile = min(half, 128)

            def add(j, _, keep=keep, start=land[p][i], source=source, target=target, tile=tile):
                at = pl.ds(pl.multiple_of(keep + j * tile, tile), tile)
                other = got[pl.ds(pl.multiple_of(start + j * tile, tile), tile), :]
                target[at, :] = (source[at, :].astype(jnp.float32) + other.astype(jnp.float32)).astype(jnp.bfloat16)
                return 0

            lax.fori_loop(0, half // tile, add, 0)
            if i + 1 < count:
                live[p] = scatter_send(p, i + 1)
        tiny.wait()
        mine = s_ref[...] if i == 0 else small[count + i]
        total = mine + small[i]
        if i + 1 < count:
            small[count + i + 1] = total
            tiny = small_send(i + 1)
        else:
            sum_ref[...] = total

    def gather_send(p, i):
        _, peer = partner_of(orders[p][i])
        half = rows >> (i + 1)
        at = pl.ds(pl.multiple_of(offs[p][i + 1], half), half)
        copy = pltpu.make_async_remote_copy(
            src_ref=out_ref.at[at], dst_ref=out_ref.at[at],
            send_sem=gsem.at[p, i], recv_sem=hsem.at[p, i], device_id=peer, device_id_type=MESH)
        copy.start()
        return copy

    for i in reversed(range(count)):
        live = [gather_send(p, i) for p in range(parts)]
        for p in range(parts):
            live[p].wait()


def all_reduce(blocks, small, dp_size, ex_size):
    steps = (dp_size * ex_size).bit_length() - 1
    rows, width = blocks.shape
    vmem = pl.BlockSpec(memory_space=pltpu.VMEM)
    dma = pltpu.SemaphoreType.DMA
    return pl.pallas_call(
        functools.partial(reduce_kernel, dp_size, ex_size),
        out_shape=(jax.ShapeDtypeStruct(blocks.shape, jnp.bfloat16), jax.ShapeDtypeStruct(small.shape, jnp.float32)),
        in_specs=[vmem, vmem],
        out_specs=(vmem, vmem),
        scratch_shapes=[
            pltpu.VMEM((rows, width), jnp.bfloat16),
            pltpu.VMEM((rows, width), jnp.bfloat16),
            pltpu.VMEM((2 * steps,) + small.shape, jnp.float32),
            dma((3, steps)), dma((3, steps)), dma((3, steps)), dma((3, steps)), dma((steps,)), dma((steps,)),
        ],
        compiler_params=pltpu.CompilerParams(collective_id=3, has_side_effects=True, vmem_limit_bytes=48 << 20),
        name="reduce_gradients",
    )(blocks, small)


def dot_nn(a, b):
    return jnp.dot(a, b, preferred_element_type=jnp.float32)


def dot_nt(a, b):
    return lax.dot_general(a, b, (((1,), (1,)), ((), ())), preferred_element_type=jnp.float32)


def dot_tn(a, b):
    return lax.dot_general(a, b, (((0,), (0,)), ((), ())), preferred_element_type=jnp.float32)


GELU_A = 0.7978845608028654
GELU_B = GELU_A * 0.044715


def gelu_pair(h):
    square = h * h
    bend = jnp.tanh(h * (GELU_B * square + GELU_A))
    share = 0.5 * bend + 0.5
    slope = share + (0.5 * h) * (1.0 - bend * bend) * ((3.0 * GELU_B) * square + GELU_A)
    return h * share, slope


def expert_kernel(dp_size, ex_size, cap, rows_hbm, fgrad_hbm, agrad_hbm, win_hbm, shard_hbm, fin_hbm, fout_hbm,
                  back_hbm, res_hbm, dw_hbm,
                  rows_v, grad_v, win_v, wout_v, act_v, hg_v, fin_v, fout_v, frow_v, fgrad_v, facc_v, fout_st,
                  rg_v, dw_st, send_row, recv_row, send_back, recv_back, send_w, recv_w, fwd_w, got_w,
                  load_sem, frozen_sem, fload_sem, store_sem, dw_sem):
    dp = lax.axis_index("dp")
    ex = lax.axis_index("expert")
    shard = shard_hbm.shape[0]
    feat = shard_hbm.shape[1]
    slots = ex_size * cap
    far = dp_size // 2
    tiles = win_hbm.shape[0] // 256
    span = fin_v.shape[1]
    steps = fin_hbm.shape[0]

    barrier = pltpu.get_barrier_semaphore()
    for r in range(1, ex_size):
        pl.semaphore_signal(barrier, inc=1, device_id=(dp, ex ^ r), device_id_type=MESH)
    pl.semaphore_signal(barrier, inc=1, device_id=(dp ^ 1, ex), device_id_type=MESH)
    for k in range(1, far):
        pl.semaphore_signal(barrier, inc=1, device_id=(dp ^ (2 * k), ex), device_id_type=MESH)
    local = [
        pltpu.make_async_copy(rows_hbm.at[pl.ds(0, 2)], frow_v, load_sem.at[0]),
        pltpu.make_async_copy(fgrad_hbm, fgrad_v, load_sem.at[1]),
    ]
    for copy in local:
        copy.start()

    def frozen_load(i, slot):
        return (pltpu.make_async_copy(fin_hbm.at[i], fin_v.at[slot], frozen_sem.at[0, slot]),
                pltpu.make_async_copy(fout_hbm.at[i], fout_v.at[slot], frozen_sem.at[1, slot]))

    for copy in frozen_load(0, 0):
        copy.start()
    pl.semaphore_wait(barrier, ex_size - 1 + 1 + far - 1)

    row_copies = []
    for r in reversed(range(1, ex_size)):
        copy = pltpu.make_async_remote_copy(
            src_ref=rows_hbm.at[2 + (ex ^ r)], dst_ref=rows_v.at[pl.ds(r * cap, cap)],
            send_sem=send_row.at[r], recv_sem=recv_row.at[r], device_id=(dp, ex ^ r), device_id_type=MESH)
        copy.start()
        row_copies.append(copy)
    own = [pltpu.make_async_copy(rows_hbm.at[2 + ex], rows_v.at[pl.ds(0, cap)], load_sem.at[2]),
           pltpu.make_async_copy(win_hbm, win_v, load_sem.at[3]),
           pltpu.make_async_copy(shard_hbm, wout_v.at[pl.ds(pl.multiple_of(dp * shard, shard), shard)], load_sem.at[4])]
    for copy in own:
        copy.start()

    mine = wout_v.at[pl.ds(pl.multiple_of(dp * shard, shard), shard)]
    weight_copies = []
    for k in range(1, far):
        copy = pltpu.make_async_remote_copy(
            src_ref=shard_hbm, dst_ref=mine, send_sem=send_w.at[k], recv_sem=recv_w.at[k],
            device_id=(dp ^ (2 * k), ex), device_id_type=MESH)
        copy.start()
        weight_copies.append(copy)
    beside = pltpu.make_async_remote_copy(
        src_ref=shard_hbm, dst_ref=mine, send_sem=send_w.at[0], recv_sem=recv_w.at[0],
        device_id=(dp ^ 1, ex), device_id_type=MESH)
    beside.start()
    grad_copies = []
    for r in range(ex_size):
        copy = pltpu.make_async_copy(agrad_hbm.at[ex ^ r], grad_v.at[pl.ds(r * cap, cap)], fload_sem.at[r])
        copy.start()
        grad_copies.append(copy)

    for copy in local:
        copy.wait()
    per = steps // 2

    def frozen(i, _):
        slot = lax.rem(i, 2)
        for copy in frozen_load(i, slot):
            copy.wait()

        @pl.when(i + 1 < steps)
        def _():
            for copy in frozen_load(i + 1, 1 - slot):
                copy.start()
        which = i // per
        up = fin_v[slot]
        down = fout_v[slot]
        hidden = dot_nt(frow_v[which], up)
        slope_in = dot_nt(fgrad_v[which], down)
        active, slope = gelu_pair(hidden)
        result = dot_nn(active.astype(jnp.bfloat16), down)
        back = dot_nn((slope_in * slope).astype(jnp.bfloat16), up)
        first = lax.rem(i, per) == 0

        @pl.when(first)
        def _():
            facc_v[0, which] = result
            facc_v[1, which] = back

        @pl.when(jnp.logical_not(first))
        def _():
            facc_v[0, which] += result
            facc_v[1, which] += back
        return 0

    lax.fori_loop(0, steps, frozen, 0)
    fout_st[...] = facc_v[...].astype(jnp.bfloat16)
    stores = [pltpu.make_async_copy(fout_st.at[0], res_hbm.at[pl.ds(0, 2)], store_sem.at[0]),
              pltpu.make_async_copy(fout_st.at[1], back_hbm.at[pl.ds(0, 2)], store_sem.at[1])]
    for copy in stores:
        copy.start()

    passed = []
    for k in range(1, far):
        weight_copies[k - 1].wait_recv()
        theirs = wout_v.at[pl.ds(pl.multiple_of((dp ^ (2 * k)) * shard, shard), shard)]
        copy = pltpu.make_async_remote_copy(
            src_ref=theirs, dst_ref=theirs, send_sem=fwd_w.at[k], recv_sem=got_w.at[k],
            device_id=(dp ^ 1, ex), device_id_type=MESH)
        copy.start()
        passed.append(copy)
    beside.wait_recv()
    for copy in passed:
        copy.wait_recv()
    for copy in grad_copies:
        copy.wait()
    for copy in own:
        copy.wait()

    def slope_tile(t, _):
        at = pl.ds(pl.multiple_of(t * 256, 256), 256)
        hg_v[:, at] = dot_nt(grad_v[...], wout_v[at, :]).astype(jnp.bfloat16)
        return 0

    lax.fori_loop(0, tiles, slope_tile, 0)
    back_copies = []
    half = slots // 2
    for part in (1, 0):
        here = pl.ds(part * half, half)
        group = range(part * (ex_size // 2), (part + 1) * (ex_size // 2))
        for r in group:
            if r:
                row_copies[ex_size - 1 - r].wait_recv()

        def hidden_tile(t, _, here=here):
            at = pl.ds(pl.multiple_of(t * 256, 256), 256)
            active, slope = gelu_pair(dot_nt(rows_v[here, :], win_v[at, :]))
            act_v[here, at] = active.astype(jnp.bfloat16)
            hg_v[here, at] = (hg_v[here, at].astype(jnp.float32) * slope).astype(jnp.bfloat16)
            return 0

        lax.fori_loop(0, tiles, hidden_tile, 0)

        def back_tile(n, _, here=here):
            at = pl.ds(pl.multiple_of(n * 256, 256), 256)
            rg_v[here, at] = dot_nn(hg_v[here, :], win_v[:, at]).astype(jnp.bfloat16)
            return 0

        lax.fori_loop(0, feat // 256, back_tile, 0)
        for r in reversed(group):
            source = rg_v.at[pl.ds(r * cap, cap)]
            if r:
                copy = pltpu.make_async_remote_copy(
                    src_ref=source, dst_ref=back_hbm.at[2 + ex], send_sem=send_back.at[r], recv_sem=recv_back.at[r],
                    device_id=(dp, ex ^ r), device_id_type=MESH)
            else:
                copy = pltpu.make_async_copy(source, back_hbm.at[2 + ex], store_sem.at[2])
            copy.start()
            back_copies.append(copy)

    def result_tile(n, _):
        at = pl.ds(pl.multiple_of(n * 256, 256), 256)
        grad_st[:, at] = dot_nn(act_v[...], wout_v[:, at]).astype(jnp.bfloat16)
        return 0

    def weight_tile(t, _):
        at = pl.ds(pl.multiple_of(t * 256, 256), 256)
        slot = lax.rem(t, 2)

        @pl.when(t >= 2)
        def _():
            pltpu.make_async_copy(dw_st.at[slot], dw_hbm.at[at], dw_sem.at[slot]).wait()
        dw_st[slot, :, 0:feat] = dot_tn(hg_v[:, at], rows_v[...]).astype(jnp.bfloat16)
        dw_st[slot, :, feat:] = dot_tn(act_v[:, at], grad_v[...]).astype(jnp.bfloat16)
        pltpu.make_async_copy(dw_st.at[slot], dw_hbm.at[at], dw_sem.at[slot]).start()
        return 0

    lax.fori_loop(0, tiles, weight_tile, 0)
    grad_st = grad_v
    lax.fori_loop(0, feat // 256, result_tile, 0)
    res_copies = []
    for r in range(ex_size):
        copy = pltpu.make_async_copy(grad_st.at[pl.ds(r * cap, cap)], res_hbm.at[2 + (ex ^ r)], fload_sem.at[r])
        copy.start()
        res_copies.append(copy)
    for slot in range(2):
        pltpu.make_async_copy(dw_st.at[slot], dw_hbm.at[pl.ds(0, 256)], dw_sem.at[slot]).wait()
    for copy in res_copies + stores:
        copy.wait()
    for copy in weight_copies:
        copy.wait_send()
    beside.wait_send()
    for copy in passed:
        copy.wait_send()
    for copy in row_copies:
        copy.wait_send()
    for copy in back_copies:
        copy.wait()


def experts(rows, fgrad, agrad, win, shard, fin, fout, dp_size, ex_size):
    kinds, cap, feat = rows.shape
    hidden = win.shape[0]
    slots = ex_size * cap
    far = dp_size // 2
    span = 768 if hidden % 768 == 0 else hidden
    steps = 2 * hidden // span
    anyspace = pl.BlockSpec(memory_space=pl.ANY)
    dma = pltpu.SemaphoreType.DMA
    low = jnp.bfloat16
    return pl.pallas_call(
        functools.partial(expert_kernel, dp_size, ex_size, cap),
        out_shape=(jax.ShapeDtypeStruct((kinds, cap, feat), low), jax.ShapeDtypeStruct((kinds, cap, feat), low),
                   jax.ShapeDtypeStruct((hidden, 2 * feat), low)),
        in_specs=[anyspace] * 7,
        out_specs=(anyspace,) * 3,
        scratch_shapes=[
            pltpu.VMEM((slots, feat), low), pltpu.VMEM((slots, feat), low),
            pltpu.VMEM((hidden, feat), low), pltpu.VMEM((hidden, feat), low),
            pltpu.VMEM((slots, hidden), low), pltpu.VMEM((slots, hidden), low),
            pltpu.VMEM((2, span, feat), low), pltpu.VMEM((2, span, feat), low),
            pltpu.VMEM((2, cap, feat), low), pltpu.VMEM((2, cap, feat), low),
            pltpu.VMEM((2, 2, cap, feat), jnp.float32), pltpu.VMEM((2, 2, cap, feat), low),
            pltpu.VMEM((slots, feat), low), pltpu.VMEM((2, 256, 2 * feat), low),
            dma((ex_size,)), dma((ex_size,)), dma((ex_size,)), dma((ex_size,)),
            dma((far,)), dma((far,)), dma((far,)), dma((far,)),
            dma((5,)), dma((2, 2)), dma((ex_size,)), dma((3,)), dma((2,)),
        ],
        compiler_params=pltpu.CompilerParams(collective_id=1, has_side_effects=True, vmem_limit_bytes=60 << 20),
        name="experts",
    )(rows, fgrad, agrad, win, shard, fin.reshape(steps, span, feat), fout.reshape(steps, span, feat))


HEADS = 12
HEAD_DIM = 64
FROZEN = 2


def layer_norm(values_in, gain_vec):
    row_mean = jnp.mean(values_in, axis=-1, keepdims=True)
    centred = values_in - row_mean
    variance = jnp.mean(centred * centred, axis=-1, keepdims=True)
    return centred * lax.rsqrt(variance + 1e-05) * gain_vec


def block_scores(query_part, key_heads, allowed):
    scores = (
        jnp.einsum("qhd,khd->hqk", query_part, key_heads, preferred_element_type=jnp.float32)
        * 0.125
    )
    return jnp.where(allowed[None], scores, -1e30)


def body(
    tokens,
    cotangent,
    chosen,
    gates,
    lengths,
    keep_mask,
    gain1,
    w_qkv,
    w_o,
    gain2,
    frozen_in,
    frozen_out,
    w_in,
    w_out,
):
    row_count = tokens.shape[0]
    feat_width = tokens.shape[1]
    owners = lax.axis_size("expert")
    kind_count = FROZEN + owners
    slot_count = ((2 * row_count * 5 // (4 * kind_count) + 7) // 8 * 8 + 15) // 16 * 16
    block_rows = min(512, row_count)
    weights_in = lax.all_gather(w_in, "dp", axis=1, tiled=True)[0]
    tokens_full = tokens.astype(jnp.float32)
    normed_one, norm_one_back = jax.vjp(layer_norm, tokens_full, gain1)
    normed_one_low = normed_one.astype(jnp.bfloat16)
    projected = jnp.dot(normed_one_low, w_qkv, preferred_element_type=jnp.float32).astype(
        jnp.bfloat16
    )
    queries = projected[:, :feat_width].reshape(row_count, HEADS, HEAD_DIM)
    key_heads = projected[:, feat_width : 2 * feat_width].reshape(row_count, HEADS, HEAD_DIM)
    value_heads = projected[:, 2 * feat_width :].reshape(row_count, HEADS, HEAD_DIM)
    places = jnp.arange(row_count, dtype=jnp.int32)
    doc_ends = jnp.cumsum(lengths[0])
    documents = jnp.sum((places[:, None] >= doc_ends[None, :]).astype(jnp.int32), axis=1)

    def permitted():
        return (
            (documents[:, None] == documents[None, :])
            & (places[None, :] <= places[:, None])
            & ((keep_mask[None, :] > 0) | (places[None, :] == places[:, None]))
        )

    scores = block_scores(queries, key_heads, permitted())
    peak_score = jnp.max(scores, axis=-1, keepdims=True)
    exp_scores = jnp.exp(scores - peak_score)
    exp_total = jnp.sum(exp_scores, axis=-1, keepdims=True)
    probs_low = (exp_scores / exp_total).astype(jnp.bfloat16)
    block_out = jnp.einsum(
        "hqk,khd->qhd", probs_low, value_heads, preferred_element_type=jnp.float32
    )
    out_blocks = block_out.reshape(block_rows, feat_width).astype(jnp.bfloat16)
    lse_blocks = [peak_score + jnp.log(exp_total)]
    mixed_rows = tokens_full + jnp.dot(out_blocks, w_o, preferred_element_type=jnp.float32)
    normed_two, norm_two_back = jax.vjp(layer_norm, mixed_rows, gain2)
    normed_two_low = normed_two.astype(jnp.bfloat16)
    flat_ids = chosen.reshape(-1)
    one_hot = (flat_ids[:, None] == jnp.arange(kind_count, dtype=jnp.int32)[None, :]).astype(
        jnp.int32
    )
    slot_ranks = jnp.sum(jnp.cumsum(one_hot, axis=0) * one_hot, axis=1) - 1
    positions = flat_ids * slot_count + slot_ranks
    buffer_rows = (
        jnp.zeros((kind_count * slot_count, feat_width), jnp.bfloat16)
        .at[positions]
        .set(jnp.repeat(normed_two_low, 2, axis=0))
    )
    grad_out = cotangent.astype(jnp.float32)
    weighted = (jnp.repeat(grad_out, 2, axis=0) * gates.reshape(-1, 1)).astype(jnp.bfloat16)
    grad_buffer = (
        jnp.zeros((kind_count * slot_count, feat_width), jnp.bfloat16).at[positions].set(weighted)
    )
    dp_size = lax.axis_size("dp")
    grad_slots = grad_buffer.reshape(kind_count, slot_count, feat_width)
    arrived_grad = lax.all_to_all(grad_slots[FROZEN:], "expert", split_axis=0, concat_axis=0, tiled=True)
    row_grads, served, weight_grads = experts(
        buffer_rows.reshape(kind_count, slot_count, feat_width), grad_slots[:FROZEN], arrived_grad,
        weights_in, w_out[0], frozen_in, frozen_out, dp_size, owners)
    returned = lax.all_to_all(served[FROZEN:], "expert", split_axis=0, concat_axis=0, tiled=True)
    results = jnp.concatenate([served[:FROZEN], returned], axis=0).reshape(-1, feat_width)
    picked = results[positions].astype(jnp.float32).reshape(row_count, 2, feat_width)
    output = mixed_rows + jnp.sum(picked * gates[:, :, None], axis=1)
    summed = lax.psum_scatter(
        weight_grads, "dp", scatter_dimension=0, tiled=True
    ).astype(jnp.float32)
    d_w_in = summed[:, :feat_width][None]
    d_w_out = summed[:, feat_width:][None]
    row_grads = row_grads.reshape(-1, feat_width)
    normed_two_grad = jnp.sum(
        row_grads[positions].astype(jnp.float32).reshape(row_count, 2, feat_width), axis=1
    )
    mixed_part, gain2_grad = norm_two_back(normed_two_grad)
    mixed_grad = grad_out + mixed_part
    branch_grad = mixed_grad.astype(jnp.bfloat16)
    w_o_grad = lax.dot_general(
        out_blocks, branch_grad, (((0,), (0,)), ((), ())), preferred_element_type=jnp.float32
    )
    attended_grad = lax.dot_general(
        branch_grad, w_o, (((1,), (1,)), ((), ())), preferred_element_type=jnp.float32
    ).astype(jnp.bfloat16)
    attended_heads = attended_grad.reshape(row_count, HEADS, HEAD_DIM)
    key_grad = jnp.zeros((row_count, HEADS, HEAD_DIM), jnp.float32)
    value_grad = jnp.zeros((row_count, HEADS, HEAD_DIM), jnp.float32)
    query_grads = []
    for block_index, row_start in enumerate(range(0, row_count, block_rows)):
        scores = block_scores(queries, key_heads, permitted())
        probs_full = jnp.exp(scores - lse_blocks[block_index])
        probs_low = probs_full.astype(jnp.bfloat16)
        prob_grad = jnp.einsum(
            "qhd,khd->hqk", attended_heads, value_heads, preferred_element_type=jnp.float32
        )
        row_delta = jnp.sum(probs_full * prob_grad, axis=-1, keepdims=True)
        score_grad = (probs_full * (prob_grad - row_delta)).astype(jnp.bfloat16)
        query_grads.append(
            jnp.einsum("hqk,khd->qhd", score_grad, key_heads, preferred_element_type=jnp.float32)
            * 0.125
        )
        key_grad = (
            jnp.einsum("hqk,qhd->khd", score_grad, queries, preferred_element_type=jnp.float32)
            * 0.125
        )
        value_grad = jnp.einsum(
            "hqk,qhd->khd", probs_low, attended_heads, preferred_element_type=jnp.float32
        )
    projected_grad = jnp.concatenate(
        [
            query_grads[0].reshape(row_count, feat_width),
            key_grad.reshape(row_count, feat_width),
            value_grad.reshape(row_count, feat_width),
        ],
        axis=1,
    ).astype(jnp.bfloat16)
    w_qkv_grad = lax.dot_general(
        normed_one_low, projected_grad, (((0,), (0,)), ((), ())), preferred_element_type=jnp.float32
    )
    normed_one_grad = lax.dot_general(
        projected_grad, w_qkv, (((1,), (1,)), ((), ())), preferred_element_type=jnp.float32
    )
    tokens_part, gain1_grad = norm_one_back(normed_one_grad)
    tokens_grad = (mixed_grad + tokens_part).astype(jnp.bfloat16)
    local_counts = jnp.sum(one_hot, axis=0).astype(jnp.float32)
    both = jnp.concatenate([w_qkv_grad, w_o_grad], axis=1).astype(jnp.bfloat16)
    half = feat_width // 2
    blocks = both.reshape(feat_width, 8, half).transpose(1, 0, 2).reshape(8 * feat_width, half)
    padded_counts = jnp.pad(local_counts, (0, feat_width - kind_count))
    small = jnp.concatenate(
        [gain1_grad[None], gain2_grad[None], padded_counts[None], jnp.zeros((5, feat_width), jnp.float32)])
    total, small_sum = all_reduce(blocks, small, lax.axis_size("dp"), owners)
    both_sum = total.reshape(8, feat_width, half).transpose(1, 0, 2).reshape(feat_width, 8 * half)
    w_qkv_sum = both_sum[:, : 3 * feat_width].astype(jnp.float32)
    w_o_sum = both_sum[:, 3 * feat_width :].astype(jnp.float32)
    gain1_sum, gain2_sum, counts = small_sum[0], small_sum[1], small_sum[2, :kind_count]
    return (
        output.astype(jnp.bfloat16),
        tokens_grad,
        gain1_sum,
        w_qkv_sum,
        w_o_sum,
        gain2_sum,
        d_w_in,
        d_w_out,
        counts,
    )


def solution(mesh):
    placed = (
        P(("dp", "expert"), None),
        P(("dp", "expert"), None),
        P(("dp", "expert"), None),
        P(("dp", "expert"), None),
        P(("dp", "expert"), None),
        P(("dp", "expert")),
        P(),
        P(),
        P(),
        P(),
        P(),
        P(),
        P("expert", "dp", None),
        P("expert", "dp", None),
    )
    return jax.shard_map(
        body,
        mesh=mesh,
        in_specs=placed,
        out_specs=(
            P(("dp", "expert"), None),
            P(("dp", "expert"), None),
            P(),
            P(),
            P(),
            P(),
            P("expert", "dp", None),
            P("expert", "dp", None),
            P(),
        ),
        check_vma=False,
    )
```

```python
import functools
import jax
import jax.numpy as jnp
from jax import lax
from jax.experimental import pallas as pl
from jax.experimental.pallas import tpu as pltpu
from jax.sharding import PartitionSpec as P

MESH = pl.DeviceIdType.MESH


def butterfly(dp_size, ex_size):
    core = ("dp", 1)
    xs = [("dp", 2 << k) for k in range((dp_size // 2).bit_length() - 1)]
    depth = 4 if ex_size % 4 == 0 else 1
    wide = ex_size // depth
    ys = [("expert", 1 << k) for k in range(wide.bit_length() - 1)]
    zs = [("expert", wide << k) for k in range(depth.bit_length() - 1)]
    return core, xs, ys, zs


def partner_of(step):
    axis, mask = step
    place = {"dp": lax.axis_index("dp"), "expert": lax.axis_index("expert")}
    bit = lax.rem(place[axis] // mask, 2)
    place[axis] = place[axis] + mask - 2 * mask * bit
    return bit, (place["dp"], place["expert"])


def dot_nn(a, b):
    return jnp.dot(a, b, preferred_element_type=jnp.float32)


def dot_nt(a, b):
    return lax.dot_general(a, b, (((1,), (1,)), ((), ())), preferred_element_type=jnp.float32)


def dot_tn(a, b):
    return lax.dot_general(a, b, (((0,), (0,)), ((), ())), preferred_element_type=jnp.float32)


GELU_A = 0.7978845608028654
GELU_B = GELU_A * 0.044715


def gelu_pair(h):
    square = h * h
    bend = jnp.tanh(h * (GELU_B * square + GELU_A))
    share = 0.5 * bend + 0.5
    slope = share + (0.5 * h) * (1.0 - bend * bend) * ((3.0 * GELU_B) * square + GELU_A)
    return h * share, slope


def expert_kernel(dp_size, ex_size, cap, rows_hbm, fgrad_hbm, agrad_hbm, win_hbm, shard_hbm, fin_hbm, fout_hbm,
                  back_hbm, res_hbm, dw_hbm,
                  rows_v, grad_v, win_v, wout_v, act_v, hg_v, fin_v, fout_v, frow_v, fgrad_v, facc_v, fout_st,
                  rg_v, dw_st, send_row, recv_row, send_back, recv_back, send_w, recv_w, fwd_w, got_w,
                  load_sem, frozen_sem, fload_sem, store_sem, dw_sem):
    dp = lax.axis_index("dp")
    ex = lax.axis_index("expert")
    shard = shard_hbm.shape[0]
    feat = shard_hbm.shape[1]
    slots = ex_size * cap
    far = dp_size // 2
    tiles = win_hbm.shape[0] // 256
    span = fin_v.shape[1]
    steps = fin_hbm.shape[0]

    barrier = pltpu.get_barrier_semaphore()
    for r in range(1, ex_size):
        pl.semaphore_signal(barrier, inc=1, device_id=(dp, ex ^ r), device_id_type=MESH)
    pl.semaphore_signal(barrier, inc=1, device_id=(dp ^ 1, ex), device_id_type=MESH)
    for k in range(1, far):
        pl.semaphore_signal(barrier, inc=1, device_id=(dp ^ (2 * k), ex), device_id_type=MESH)
    local = [
        pltpu.make_async_copy(rows_hbm.at[pl.ds(0, 2)], frow_v, load_sem.at[0]),
        pltpu.make_async_copy(fgrad_hbm, fgrad_v, load_sem.at[1]),
    ]
    for copy in local:
        copy.start()

    def frozen_load(i, slot):
        return (pltpu.make_async_copy(fin_hbm.at[i], fin_v.at[slot], frozen_sem.at[0, slot]),
                pltpu.make_async_copy(fout_hbm.at[i], fout_v.at[slot], frozen_sem.at[1, slot]))

    for copy in frozen_load(0, 0):
        copy.start()
    pl.semaphore_wait(barrier, ex_size - 1 + 1 + far - 1)

    row_copies = []
    for r in reversed(range(1, ex_size)):
        copy = pltpu.make_async_remote_copy(
            src_ref=rows_hbm.at[2 + (ex ^ r)], dst_ref=rows_v.at[pl.ds(r * cap, cap)],
            send_sem=send_row.at[r], recv_sem=recv_row.at[r], device_id=(dp, ex ^ r), device_id_type=MESH)
        copy.start()
        row_copies.append(copy)
    own = [pltpu.make_async_copy(rows_hbm.at[2 + ex], rows_v.at[pl.ds(0, cap)], load_sem.at[2]),
           pltpu.make_async_copy(win_hbm, win_v, load_sem.at[3]),
           pltpu.make_async_copy(shard_hbm, wout_v.at[pl.ds(pl.multiple_of(dp * shard, shard), shard)], load_sem.at[4])]
    for copy in own:
        copy.start()

    mine = wout_v.at[pl.ds(pl.multiple_of(dp * shard, shard), shard)]
    weight_copies = []
    for k in range(1, far):
        copy = pltpu.make_async_remote_copy(
            src_ref=shard_hbm, dst_ref=mine, send_sem=send_w.at[k], recv_sem=recv_w.at[k],
            device_id=(dp ^ (2 * k), ex), device_id_type=MESH)
        copy.start()
        weight_copies.append(copy)
    beside = pltpu.make_async_remote_copy(
        src_ref=shard_hbm, dst_ref=mine, send_sem=send_w.at[0], recv_sem=recv_w.at[0],
        device_id=(dp ^ 1, ex), device_id_type=MESH)
    beside.start()
    grad_copies = []
    for r in range(ex_size):
        copy = pltpu.make_async_copy(agrad_hbm.at[ex ^ r], grad_v.at[pl.ds(r * cap, cap)], fload_sem.at[r])
        copy.start()
        grad_copies.append(copy)

    for copy in local:
        copy.wait()
    per = steps // 2

    def frozen(i, _):
        slot = lax.rem(i, 2)
        for copy in frozen_load(i, slot):
            copy.wait()

        @pl.when(i + 1 < steps)
        def _():
            for copy in frozen_load(i + 1, 1 - slot):
                copy.start()
        which = i // per
        up = fin_v[slot]
        down = fout_v[slot]
        hidden = dot_nt(frow_v[which], up)
        slope_in = dot_nt(fgrad_v[which], down)
        active, slope = gelu_pair(hidden)
        result = dot_nn(active.astype(jnp.bfloat16), down)
        back = dot_nn((slope_in * slope).astype(jnp.bfloat16), up)
        first = lax.rem(i, per) == 0

        @pl.when(first)
        def _():
            facc_v[0, which] = result
            facc_v[1, which] = back

        @pl.when(jnp.logical_not(first))
        def _():
            facc_v[0, which] += result
            facc_v[1, which] += back
        return 0

    lax.fori_loop(0, steps, frozen, 0)
    fout_st[...] = facc_v[...].astype(jnp.bfloat16)
    stores = [pltpu.make_async_copy(fout_st.at[0], res_hbm.at[pl.ds(0, 2)], store_sem.at[0]),
              pltpu.make_async_copy(fout_st.at[1], back_hbm.at[pl.ds(0, 2)], store_sem.at[1])]
    for copy in stores:
        copy.start()

    passed = []
    for k in range(1, far):
        weight_copies[k - 1].wait_recv()
        theirs = wout_v.at[pl.ds(pl.multiple_of((dp ^ (2 * k)) * shard, shard), shard)]
        copy = pltpu.make_async_remote_copy(
            src_ref=theirs, dst_ref=theirs, send_sem=fwd_w.at[k], recv_sem=got_w.at[k],
            device_id=(dp ^ 1, ex), device_id_type=MESH)
        copy.start()
        passed.append(copy)
    beside.wait_recv()
    for copy in passed:
        copy.wait_recv()
    for copy in grad_copies:
        copy.wait()
    for copy in own:
        copy.wait()

    def slope_tile(t, _):
        at = pl.ds(pl.multiple_of(t * 256, 256), 256)
        hg_v[:, at] = dot_nt(grad_v[...], wout_v[at, :]).astype(jnp.bfloat16)
        return 0

    lax.fori_loop(0, tiles, slope_tile, 0)
    back_copies = []
    half = slots // 2
    for part in (1, 0):
        here = pl.ds(part * half, half)
        group = range(part * (ex_size // 2), (part + 1) * (ex_size // 2))
        for r in group:
            if r:
                row_copies[ex_size - 1 - r].wait_recv()

        def hidden_tile(t, _, here=here):
            at = pl.ds(pl.multiple_of(t * 256, 256), 256)
            active, slope = gelu_pair(dot_nt(rows_v[here, :], win_v[at, :]))
            act_v[here, at] = active.astype(jnp.bfloat16)
            hg_v[here, at] = (hg_v[here, at].astype(jnp.float32) * slope).astype(jnp.bfloat16)
            return 0

        lax.fori_loop(0, tiles, hidden_tile, 0)

        def back_tile(n, _, here=here):
            at = pl.ds(pl.multiple_of(n * 256, 256), 256)
            rg_v[here, at] = dot_nn(hg_v[here, :], win_v[:, at]).astype(jnp.bfloat16)
            return 0

        lax.fori_loop(0, feat // 256, back_tile, 0)
        for r in reversed(group):
            source = rg_v.at[pl.ds(r * cap, cap)]
            if r:
                copy = pltpu.make_async_remote_copy(
                    src_ref=source, dst_ref=back_hbm.at[2 + ex], send_sem=send_back.at[r], recv_sem=recv_back.at[r],
                    device_id=(dp, ex ^ r), device_id_type=MESH)
            else:
                copy = pltpu.make_async_copy(source, back_hbm.at[2 + ex], store_sem.at[2])
            copy.start()
            back_copies.append(copy)

    def result_tile(n, _):
        at = pl.ds(pl.multiple_of(n * 256, 256), 256)
        grad_st[:, at] = dot_nn(act_v[...], wout_v[:, at]).astype(jnp.bfloat16)
        return 0

    def weight_tile(t, _):
        at = pl.ds(pl.multiple_of(t * 256, 256), 256)
        slot = lax.rem(t, 2)

        @pl.when(t >= 2)
        def _():
            pltpu.make_async_copy(dw_st.at[slot], dw_hbm.at[at], dw_sem.at[slot]).wait()
        dw_st[slot, :, 0:feat] = dot_tn(hg_v[:, at], rows_v[...]).astype(jnp.bfloat16)
        dw_st[slot, :, feat:] = dot_tn(act_v[:, at], grad_v[...]).astype(jnp.bfloat16)
        pltpu.make_async_copy(dw_st.at[slot], dw_hbm.at[at], dw_sem.at[slot]).start()
        return 0

    lax.fori_loop(0, tiles, weight_tile, 0)
    grad_st = grad_v
    lax.fori_loop(0, feat // 256, result_tile, 0)
    res_copies = []
    for r in range(ex_size):
        copy = pltpu.make_async_copy(grad_st.at[pl.ds(r * cap, cap)], res_hbm.at[2 + (ex ^ r)], fload_sem.at[r])
        copy.start()
        res_copies.append(copy)
    for slot in range(2):
        pltpu.make_async_copy(dw_st.at[slot], dw_hbm.at[pl.ds(0, 256)], dw_sem.at[slot]).wait()
    for copy in res_copies + stores:
        copy.wait()
    for copy in weight_copies:
        copy.wait_send()
    beside.wait_send()
    for copy in passed:
        copy.wait_send()
    for copy in row_copies:
        copy.wait_send()
    for copy in back_copies:
        copy.wait()


def experts(rows, fgrad, agrad, win, shard, fin, fout, dp_size, ex_size):
    kinds, cap, feat = rows.shape
    hidden = win.shape[0]
    slots = ex_size * cap
    far = dp_size // 2
    span = 768 if hidden % 768 == 0 else hidden
    steps = 2 * hidden // span
    anyspace = pl.BlockSpec(memory_space=pl.ANY)
    dma = pltpu.SemaphoreType.DMA
    low = jnp.bfloat16
    return pl.pallas_call(
        functools.partial(expert_kernel, dp_size, ex_size, cap),
        out_shape=(jax.ShapeDtypeStruct((kinds, cap, feat), low), jax.ShapeDtypeStruct((kinds, cap, feat), low),
                   jax.ShapeDtypeStruct((hidden, 2 * feat), low)),
        in_specs=[anyspace] * 7,
        out_specs=(anyspace,) * 3,
        scratch_shapes=[
            pltpu.VMEM((slots, feat), low), pltpu.VMEM((slots, feat), low),
            pltpu.VMEM((hidden, feat), low), pltpu.VMEM((hidden, feat), low),
            pltpu.VMEM((slots, hidden), low), pltpu.VMEM((slots, hidden), low),
            pltpu.VMEM((2, span, feat), low), pltpu.VMEM((2, span, feat), low),
            pltpu.VMEM((2, cap, feat), low), pltpu.VMEM((2, cap, feat), low),
            pltpu.VMEM((2, 2, cap, feat), jnp.float32), pltpu.VMEM((2, 2, cap, feat), low),
            pltpu.VMEM((slots, feat), low), pltpu.VMEM((2, 256, 2 * feat), low),
            dma((ex_size,)), dma((ex_size,)), dma((ex_size,)), dma((ex_size,)),
            dma((far,)), dma((far,)), dma((far,)), dma((far,)),
            dma((5,)), dma((2, 2)), dma((ex_size,)), dma((3,)), dma((2,)),
        ],
        compiler_params=pltpu.CompilerParams(collective_id=1, has_side_effects=True, vmem_limit_bytes=60 << 20),
        name="experts",
    )(rows, fgrad, agrad, win, shard, fin.reshape(steps, span, feat), fout.reshape(steps, span, feat))


def attend_kernel(dp_size, ex_size, kinds, cap, lengths_s, chosen_ref, gates_ref, keep_ref, tok_ref, cot_ref, gain1_ref,
                  gain2_ref, wqkv_hbm, wo_hbm, shard_hbm,
                  rows_hbm, fgrad_hbm, agrad_hbm, win_hbm, proj_hbm, prob_hbm, attt_hbm, normt_hbm, mixed_ref, place_ref,
                  count_ref,
                  wqkv_v, wo_v, norm_v, normt_v, proj_v, prob_v, attt_v, att_v, bias_v, grad_v, rows_v, place_v,
                  send_g, recv_g, send_w, recv_w, fwd_w, got_w, load_sem, store_sem, prob_sem):
    dp = lax.axis_index("dp")
    ex = lax.axis_index("expert")
    count, feat = tok_ref.shape
    shard = shard_hbm.shape[0]
    far = dp_size // 2
    low = jnp.bfloat16

    barrier = pltpu.get_barrier_semaphore()
    for r in range(1, ex_size):
        pl.semaphore_signal(barrier, inc=1, device_id=(dp, ex ^ r), device_id_type=MESH)
    pl.semaphore_signal(barrier, inc=1, device_id=(dp ^ 1, ex), device_id_type=MESH)
    for k in range(1, far):
        pl.semaphore_signal(barrier, inc=1, device_id=(dp ^ (2 * k), ex), device_id_type=MESH)
    mine = win_hbm.at[pl.ds(pl.multiple_of(dp * shard, shard), shard)]
    loads = [pltpu.make_async_copy(wqkv_hbm, wqkv_v, load_sem.at[0]),
             pltpu.make_async_copy(wo_hbm, wo_v, load_sem.at[1]),
             pltpu.make_async_copy(shard_hbm, mine, load_sem.at[2])]
    for copy in loads:
        copy.start()

    kind = lax.broadcasted_iota(jnp.int32, (128, count), 0)
    first = chosen_ref[0:1, :]
    second = chosen_ref[1:2, :]
    hit_first = jnp.where(kind == first, 1.0, 0.0)
    hit_second = jnp.where(kind == second, 1.0, 0.0)
    hits = (hit_first + hit_second).astype(low)
    before = jnp.where(lax.broadcasted_iota(jnp.int32, (count, count), 0)
                       < lax.broadcasted_iota(jnp.int32, (count, count), 1), 1.0, 0.0).astype(low)
    ahead = dot_nn(hits, before)
    count_ref[...] = dot_nt(jnp.ones((8, count), low), hits)
    place_first = first.astype(jnp.float32) * cap + jnp.sum(hit_first * ahead, axis=0, keepdims=True)
    place_second = second.astype(jnp.float32) * cap + jnp.sum(hit_second * ahead, axis=0, keepdims=True)
    place_v[0:1, :] = place_first
    place_v[1:2, :] = place_second

    spot = lax.broadcasted_iota(jnp.int32, (1, count), 1)
    document = jnp.zeros((1, count), jnp.float32)
    end = lengths_s[0, 0]
    for j in range(1, lengths_s.shape[1] + 1):
        document = document + jnp.where(spot >= end, 1.0, 0.0)
        if j < lengths_s.shape[1]:
            end = end + lengths_s[0, j]
    place_v[2:3, :] = document
    place_v[3:4, :] = keep_ref[...].astype(jnp.float32)
    place_v[4:8, :] = jnp.zeros((4, count), jnp.float32)
    columns = place_v[...].T
    place_ref[...] = columns

    def chosen_rows(e):
        slot = (e * cap + lax.broadcasted_iota(jnp.int32, (cap, count), 0)).astype(jnp.float32)
        return slot == place_v[0:1, :], slot == place_v[1:2, :]

    def grad_rows(e, _):
        one, two = chosen_rows(e)
        gate = jnp.sum(jnp.where(one, gates_ref[0:1, :], jnp.where(two, gates_ref[1:2, :], 0.0)), axis=1, keepdims=True)
        pick = jnp.where(one | two, 1.0, 0.0).astype(low)
        grad_v[e] = (dot_nn(pick, cot_ref[...]) * gate).astype(low)
        return 0

    lax.fori_loop(0, kinds, grad_rows, 0)
    pl.semaphore_wait(barrier, ex_size - 1 + 1 + far - 1)
    grad_copies = []
    for r in reversed(range(1, ex_size)):
        copy = pltpu.make_async_remote_copy(
            src_ref=grad_v.at[2 + (ex ^ r)], dst_ref=agrad_hbm.at[ex],
            send_sem=send_g.at[r], recv_sem=recv_g.at[r], device_id=(dp, ex ^ r), device_id_type=MESH)
        copy.start()
        grad_copies.append(copy)
    weight_copies = []
    for k in range(1, far):
        copy = pltpu.make_async_remote_copy(
            src_ref=shard_hbm, dst_ref=mine, send_sem=send_w.at[k], recv_sem=recv_w.at[k],
            device_id=(dp ^ (2 * k), ex), device_id_type=MESH)
        copy.start()
        weight_copies.append(copy)
    beside = pltpu.make_async_remote_copy(
        src_ref=shard_hbm, dst_ref=mine, send_sem=send_w.at[0], recv_sem=recv_w.at[0],
        device_id=(dp ^ 1, ex), device_id_type=MESH)
    beside.start()
    stores = [pltpu.make_async_copy(grad_v.at[2 + ex], agrad_hbm.at[ex], store_sem.at[0]),
              pltpu.make_async_copy(grad_v.at[pl.ds(0, 2)], fgrad_hbm, store_sem.at[1])]
    for copy in stores:
        copy.start()

    whole = tok_ref[...].astype(jnp.float32)
    centred = whole - jnp.mean(whole, axis=1, keepdims=True)
    scale = lax.rsqrt(jnp.mean(centred * centred, axis=1, keepdims=True) + 1e-05)
    norm_v[...] = (centred * scale * gain1_ref[...][None]).astype(low)
    loads[0].wait()

    def project(n, _):
        at = pl.ds(pl.multiple_of(n * 256, 256), 256)
        proj_v[:, at] = dot_nn(norm_v[...], wqkv_v[:, at]).astype(low)
        return 0

    lax.fori_loop(0, 3 * feat // 256, project, 0)
    stores.append(pltpu.make_async_copy(proj_v, proj_hbm, store_sem.at[2]))
    stores[-1].start()

    key = lax.broadcasted_iota(jnp.int32, (count, count), 0)
    query = lax.broadcasted_iota(jnp.int32, (count, count), 1)
    allowed = (columns[:, 2:3] == document) & (key <= query) & ((columns[:, 3:4] > 0.0) | (key == query))
    bias_v[...] = jnp.where(allowed, 0.0, -1e30)
    half = count // 2
    lower = lax.broadcasted_iota(jnp.int32, (count, 128), 1) < 64

    def head_pair(p, _):
        at = pl.multiple_of(p * 128, 128)
        q = proj_v[:, pl.ds(at, 128)]
        k = proj_v[:, pl.ds(pl.multiple_of(feat + p * 128, 128), 128)]
        vt = proj_v[:, pl.ds(pl.multiple_of(2 * feat + p * 128, 128), 128)].T
        for j in range(2):
            one = jnp.where(lower if j == 0 else jnp.logical_not(lower), k, jnp.zeros_like(k))
            for b in range(2):
                reach = (b + 1) * half
                scores = dot_nt(one[0:reach], q[b * half:(b + 1) * half]) * 0.125 + bias_v[0:reach, b * half:(b + 1) * half]
                powers = jnp.exp(scores - jnp.max(scores, axis=0, keepdims=True))
                probs = (powers * (1.0 / jnp.sum(powers, axis=0, keepdims=True))).astype(low)
                prob_v[2 * p + j, b * half:b * half + reach, :] = probs
                attt_v[pl.ds(at + 64 * j, 64), b * half:(b + 1) * half] = dot_nn(
                    vt[64 * j:64 * j + 64, 0:reach], probs).astype(low)
        pltpu.make_async_copy(prob_v.at[pl.ds(2 * p, 2)], prob_hbm.at[pl.ds(2 * p, 2)], prob_sem.at[p]).start()
        return 0

    lax.fori_loop(0, feat // 128, head_pair, 0)
    stores.append(pltpu.make_async_copy(attt_v, attt_hbm, store_sem.at[3]))
    stores[-1].start()

    def turn(n, _):
        at = pl.ds(pl.multiple_of(n * 128, 128), 128)
        att_v[:, at] = attt_v[at, :].T
        return 0

    lax.fori_loop(0, feat // 128, turn, 0)
    loads[1].wait()

    def mix(n, _):
        at = pl.ds(pl.multiple_of(n * 256, 256), 256)
        mixed_ref[:, at] = tok_ref[:, at].astype(jnp.float32) + dot_nn(att_v[...], wo_v[:, at])
        return 0

    lax.fori_loop(0, feat // 256, mix, 0)
    mixed = mixed_ref[...]
    centred = mixed - jnp.mean(mixed, axis=1, keepdims=True)
    scale = lax.rsqrt(jnp.mean(centred * centred, axis=1, keepdims=True) + 1e-05)
    att_v[...] = (centred * scale * gain2_ref[...][None]).astype(low)

    def token_rows(e, _):
        one, two = chosen_rows(e)
        pick = jnp.where(one | two, 1.0, 0.0).astype(low)
        rows_v[e] = dot_nn(pick, att_v[...]).astype(low)
        return 0

    lax.fori_loop(0, kinds, token_rows, 0)
    stores.append(pltpu.make_async_copy(rows_v, rows_hbm, store_sem.at[4]))
    stores[-1].start()

    def turn_norm(n, _):
        at = pl.ds(pl.multiple_of(n * 128, 128), 128)
        normt_v[at, :] = norm_v[:, at].T
        return 0

    lax.fori_loop(0, feat // 128, turn_norm, 0)
    stores.append(pltpu.make_async_copy(normt_v, normt_hbm, store_sem.at[5]))
    stores[-1].start()

    passed = []
    for k in range(1, far):
        weight_copies[k - 1].wait_recv()
        theirs = win_hbm.at[pl.ds(pl.multiple_of((dp ^ (2 * k)) * shard, shard), shard)]
        copy = pltpu.make_async_remote_copy(
            src_ref=theirs, dst_ref=theirs, send_sem=fwd_w.at[k], recv_sem=got_w.at[k],
            device_id=(dp ^ 1, ex), device_id_type=MESH)
        copy.start()
        passed.append(copy)
    for p in range(feat // 128):
        pltpu.make_async_copy(prob_v.at[pl.ds(2 * p, 2)], prob_hbm.at[pl.ds(2 * p, 2)], prob_sem.at[p]).wait()
    for copy in stores:
        copy.wait()
    loads[2].wait()
    for copy in weight_copies:
        copy.wait_send()
    beside.wait()
    for copy in passed:
        copy.wait()
    for copy in grad_copies:
        copy.wait()


def attend(tokens, cotangent, chosen, gates, lengths, keep, gain1, gain2, wqkv, wo, shard, kinds, cap, dp_size, ex_size):
    count, feat = tokens.shape
    heads = feat // 64
    anyspace = pl.BlockSpec(memory_space=pl.ANY)
    vmem = pl.BlockSpec(memory_space=pltpu.VMEM)
    dma = pltpu.SemaphoreType.DMA
    low = jnp.bfloat16
    shape = jax.ShapeDtypeStruct
    far = dp_size // 2
    return pl.pallas_call(
        functools.partial(attend_kernel, dp_size, ex_size, kinds, cap),
        out_shape=(shape((kinds, cap, feat), low), shape((2, cap, feat), low), shape((ex_size, cap, feat), low),
                   shape((dp_size * shard.shape[0], feat), low), shape((count, 3 * feat), low),
                   shape((heads, count + count // 2, count // 2), low), shape((feat, count), low),
                   shape((feat, count), low), shape((count, feat), jnp.float32), shape((count, 8), jnp.float32),
                   shape((8, 128), jnp.float32)),
        in_specs=[pl.BlockSpec(memory_space=pltpu.SMEM)] + [vmem] * 7 + [anyspace] * 3,
        out_specs=(anyspace,) * 8 + (vmem,) * 3,
        scratch_shapes=[
            pltpu.VMEM((feat, 3 * feat), low), pltpu.VMEM((feat, feat), low), pltpu.VMEM((count, feat), low),
            pltpu.VMEM((feat, count), low), pltpu.VMEM((count, 3 * feat), low),
            pltpu.VMEM((heads, count + count // 2, count // 2), low), pltpu.VMEM((feat, count), low),
            pltpu.VMEM((count, feat), low), pltpu.VMEM((count, count), jnp.float32),
            pltpu.VMEM((kinds, cap, feat), low), pltpu.VMEM((kinds, cap, feat), low), pltpu.VMEM((8, count), jnp.float32),
            dma((ex_size,)), dma((ex_size,)), dma((far,)), dma((far,)), dma((far,)), dma((far,)),
            dma((3,)), dma((6,)), dma((feat // 128,)),
        ],
        compiler_params=pltpu.CompilerParams(collective_id=0, has_side_effects=True, vmem_limit_bytes=56 << 20),
        name="attend",
    )(lengths, chosen.T, gates.T, keep[None], tokens, cotangent, gain1, gain2, wqkv, wo, shard)


class Sums:

    def __init__(self, chunks, blocks, acc, got, out, ssem, rsem, gsem, hsem):
        self.chunks, self.blocks, self.acc, self.got, self.out = chunks, blocks, acc, got, out
        self.sems = (ssem, rsem, gsem, hsem)
        self.offs = [[base] for base, _, _, _ in chunks]
        self.land = [[base] for base, _, _, _ in chunks]
        self.copies = [None] * len(chunks)
        self.stage = [0] * len(chunks)
        self.sent = []

    def scatter(self, c, i):
        base, rows, order, _ = self.chunks[c]
        bit, peer = partner_of(order[i])
        half = rows >> (i + 1)
        source = self.blocks if i == 0 else self.acc
        give = pl.multiple_of(self.offs[c][i] + (1 - bit) * half, 16)
        copy = pltpu.make_async_remote_copy(
            src_ref=source.at[pl.ds(give, half)], dst_ref=self.got.at[pl.ds(self.land[c][i], half)],
            send_sem=self.sems[0].at[c, i], recv_sem=self.sems[1].at[c, i], device_id=peer, device_id_type=MESH)
        copy.start()
        self.offs[c].append(self.offs[c][i] + bit * half)
        self.land[c].append(self.land[c][i] + half)
        self.copies[c] = copy

    def gather(self, c, i):
        base, rows, order, _ = self.chunks[c]
        _, peer = partner_of(order[i])
        at = pl.ds(pl.multiple_of(self.offs[c][i + 1], 16), rows >> (i + 1))
        copy = pltpu.make_async_remote_copy(
            src_ref=self.out.at[at], dst_ref=self.out.at[at],
            send_sem=self.sems[2].at[c, i], recv_sem=self.sems[3].at[c, i], device_id=peer, device_id_type=MESH)
        copy.start()
        self.copies[c] = copy

    def start(self, phase):
        for c, chunk in enumerate(self.chunks):
            if chunk[3] == phase:
                self.scatter(c, 0)

    def advance(self, c):
        if self.copies[c] is None:
            return
        base, rows, order, _ = self.chunks[c]
        steps, s = len(order), self.stage[c]
        self.copies[c].wait()
        self.stage[c] += 1
        if s >= steps:
            i = 2 * steps - 1 - s
            if i > 0:
                self.gather(c, i - 1)
            else:
                self.copies[c] = None
            return
        half = rows >> (s + 1)
        source = self.blocks if s == 0 else self.acc
        target = self.acc if s + 1 < steps else self.out
        keep, begin = self.offs[c][s + 1], self.land[c][s]
        tile = half
        while tile > 128 or half % tile or tile % 16:
            tile -= 16

        def add(j, _):
            at = pl.ds(pl.multiple_of(keep + j * tile, 16), tile)
            other = self.got[pl.ds(pl.multiple_of(begin + j * tile, 16), tile), :]
            target[at, :] = (source[at, :].astype(jnp.float32) + other.astype(jnp.float32)).astype(jnp.bfloat16)
            return 0

        lax.fori_loop(0, half // tile, add, 0)
        if s + 1 < steps:
            self.scatter(c, s + 1)
        else:
            self.gather(c, s)

    def tick(self):
        for c in range(len(self.chunks)):
            self.advance(c)

    def finish(self):
        while any(copy is not None for copy in self.copies):
            self.tick()


def sum_chunks(dp_size, ex_size, rows):
    core, xs, ys, zs = butterfly(dp_size, ex_size)
    yxz, yzx, xyz = [core] + ys + xs + zs, [core] + ys + zs + xs, [core] + xs + ys + zs
    if dp_size * ex_size * 16 <= 512:
        return [(0, 1536, yxz, 0), (1536, 2048, yzx, 1), (3584, 1024, xyz, 2), (4608, 1536, yxz, 2)]
    third = rows // 3
    return [(0, third, yxz, 2), (third, third, yzx, 2), (2 * third, third, xyz, 2)]


def unwind_kernel(dp_size, ex_size, kinds, cap, back_hbm, res_hbm, proj_hbm, prob_hbm, attt_hbm, normt_hbm, wqkv_hbm, wo_hbm,
                  mixed_ref, tok_ref, cot_ref, place_ref, gates_ref, count_ref, gain1_ref, gain2_ref,
                  out_ref, dtok_ref, total_ref, sum_ref,
                  back_v, ret_v, pick_v, other_v, g_v, mg_v, branch_v, da_v, dqt_v, proj_v, prob_v, attt_v, normt_v, wqkv_v,
                  wo_v, pg_v, blocks_v, acc_v, got_v, gain_v, small_v, send_res, recv_res, ssem, rsem, gsem, hsem, tsem, usem,
                  load_sem):
    dp = lax.axis_index("dp")
    ex = lax.axis_index("expert")
    count, feat = tok_ref.shape
    slots = kinds * cap
    padded = back_v.shape[0]
    low = jnp.bfloat16
    steps = (dp_size * ex_size).bit_length() - 1
    bits = dp_size.bit_length() - 1

    barrier = pltpu.get_barrier_semaphore()
    for r in range(1, ex_size):
        pl.semaphore_signal(barrier, inc=1, device_id=(dp, ex ^ r), device_id_type=MESH)
    for k in range(bits):
        pl.semaphore_signal(barrier, inc=1, device_id=(dp ^ (1 << k), ex), device_id_type=MESH)
    loads = [pltpu.make_async_copy(source, target, load_sem.at[i]) for i, (source, target) in enumerate([
        (back_hbm, back_v.at[pl.ds(0, slots)]), (attt_hbm, attt_v), (wo_hbm, wo_v), (prob_hbm, prob_v), (proj_hbm, proj_v),
        (normt_hbm, normt_v), (wqkv_hbm, wqkv_v)])]
    for copy in loads:
        copy.start()
    pl.semaphore_wait(barrier, ex_size - 1 + bits)
    results = []
    for r in reversed(range(1, ex_size)):
        copy = pltpu.make_async_remote_copy(
            src_ref=res_hbm.at[pl.ds(pl.multiple_of((2 + (ex ^ r)) * cap, 16), cap)],
            dst_ref=ret_v.at[pl.ds(pl.multiple_of((2 + ex) * cap, 16), cap)],
            send_sem=send_res.at[r], recv_sem=recv_res.at[r], device_id=(dp, ex ^ r), device_id_type=MESH)
        copy.start()
        results.append(copy)
    own = pl.ds(pl.multiple_of((2 + ex) * cap, 16), cap)
    results.append(pltpu.make_async_copy(res_hbm.at[own], ret_v.at[own], load_sem.at[7]))
    results.append(pltpu.make_async_copy(res_hbm.at[pl.ds(0, 2 * cap)], ret_v.at[pl.ds(0, 2 * cap)], load_sem.at[8]))
    for copy in results[-2:]:
        copy.start()
    if padded > slots:
        ret_v[slots:, :] = jnp.zeros((padded - slots, feat), low)
        back_v[slots:, :] = jnp.zeros((padded - slots, feat), low)
    sums = Sums(sum_chunks(dp_size, ex_size, blocks_v.shape[0]), blocks_v, acc_v, got_v, total_ref, ssem, rsem, gsem, hsem)

    def place_tile(n):
        at = pl.ds(pl.multiple_of(n * 128, 128), 128)
        slot = (n * 128 + lax.broadcasted_iota(jnp.int32, (count, 128), 1)).astype(jnp.float32)
        return at, slot == place_ref[:, 0:1], slot == place_ref[:, 1:2]

    def pick_both(n, _):
        at, one, two = place_tile(n)
        pick_v[:, at] = jnp.where(one | two, 1.0, 0.0).astype(low)
        return 0

    lax.fori_loop(0, padded // 128, pick_both, 0)
    loads[0].wait()

    def collect(n, _):
        at = pl.ds(pl.multiple_of(n * 256, 256), 256)
        g_v[:, at] = dot_nn(pick_v[...], back_v[:, at])
        return 0

    lax.fori_loop(0, feat // 256, collect, 0)
    gain_v[...] = jnp.zeros_like(gain_v)
    gain_v[16:24, 0:128] = count_ref[...]

    def norm_back(i, whole, gain, target):
        at = pl.ds(pl.multiple_of(i * 64, 64), 64)
        centred = whole - jnp.mean(whole, axis=1, keepdims=True)
        scale = lax.rsqrt(jnp.mean(centred * centred, axis=1, keepdims=True) + 1e-05)
        unit = centred * scale
        grad = g_v[at, :]
        weighted = grad * unit
        gain_v[target:target + 8, :] += jnp.sum(weighted.reshape(8, 8, feat), axis=0)
        scaled = grad * gain
        return at, scale * (scaled - jnp.mean(scaled, axis=1, keepdims=True)
                            - unit * jnp.mean(scaled * unit, axis=1, keepdims=True))

    def second_norm(i, _):
        at, part = norm_back(i, mixed_ref[pl.ds(pl.multiple_of(i * 64, 64), 64), :], gain2_ref[...][None], 8)
        grad = cot_ref[at, :].astype(jnp.float32) + part
        mg_v[at, :] = grad
        branch_v[at, :] = grad.astype(low)
        return 0

    lax.fori_loop(0, count // 64, second_norm, 0)
    loads[1].wait()
    wide = feat // 2

    def out_weight(b, _):
        at = pl.ds(pl.multiple_of(b * wide, 128), wide)
        blocks_v[pl.ds(pl.multiple_of(b * feat, 16), feat), :] = dot_nn(attt_v[...], branch_v[:, at]).astype(low)
        return 0

    lax.fori_loop(0, 2, out_weight, 0)
    sums.start(0)
    loads[2].wait()

    def attended_grad(n, _):
        at = pl.ds(pl.multiple_of(n * 256, 256), 256)
        da_v[:, at] = dot_nt(branch_v[...], wo_v[at, :]).astype(low)
        return 0

    lax.fori_loop(0, feat // 256, attended_grad, 0)
    loads[3].wait()
    loads[4].wait()
    half = count // 2
    lower = lax.broadcasted_iota(jnp.int32, (count, 128), 1) < 64

    def head_pair(p, _):
        at_q = pl.ds(pl.multiple_of(p * 128, 128), 128)
        at_k = pl.ds(pl.multiple_of(feat + p * 128, 128), 128)
        at_v = pl.ds(pl.multiple_of(2 * feat + p * 128, 128), 128)
        q, k, v, da = proj_v[:, at_q], proj_v[:, at_k], proj_v[:, at_v], da_v[:, at_q]
        kt = k.T
        key_near = key_far = value_near = value_far = 0.0
        for j in range(2):
            mask = lower if j == 0 else jnp.logical_not(lower)
            qj, vj, daj = [jnp.where(mask, w, jnp.zeros_like(w)) for w in (q, v, da)]
            for b in range(2):
                reach, here = (b + 1) * half, slice(b * half, (b + 1) * half)
                prob = prob_v[2 * p + j, b * half:b * half + reach, :]
                full = prob.astype(jnp.float32)
                grad = dot_nt(vj[0:reach], da[here])
                score = (full * (grad - jnp.sum(full * grad, axis=0, keepdims=True))).astype(low)
                dqt_v[64 * j:64 * j + 64, here] = dot_nn(kt[64 * j:64 * j + 64, 0:reach], score)
                key_near += dot_nn(score[0:half], qj[here])
                value_near += dot_nn(prob[0:half], daj[here])
                if b:
                    key_far += dot_nn(score[half:], qj[here])
                    value_far += dot_nn(prob[half:], daj[here])
        pg_v[:, at_q] = (dqt_v[...].T * 0.125).astype(low)
        pg_v[0:half, at_k] = (key_near * 0.125).astype(low)
        pg_v[half:, at_k] = (key_far * 0.125).astype(low)
        pg_v[0:half, at_v] = value_near.astype(low)
        pg_v[half:, at_v] = value_far.astype(low)
        return 0

    pairs = feat // 128
    for turn in range(2):
        lax.fori_loop(turn * pairs // 2, (turn + 1) * pairs // 2, head_pair, 0)
        if turn == 0:
            loads[5].wait()
        sums.tick()

        def weight_block(c, _, turn=turn):
            at = pl.ds(pl.multiple_of(c * feat + turn * wide, 128), wide)
            into = pl.ds(pl.multiple_of(2 * feat + (3 * turn + c) * feat, 16), feat)
            blocks_v[into, :] = dot_nn(normt_v[...], pg_v[:, at]).astype(low)
            return 0

        lax.fori_loop(0, 3, weight_block, 0)
        sums.start(1 + turn)
    loads[6].wait()
    sums.tick()

    def norm_grad(n, _):
        at = pl.ds(pl.multiple_of(n * 256, 256), 256)
        g_v[:, at] = dot_nt(pg_v[...], wqkv_v[at, :])
        return 0

    lax.fori_loop(0, feat // 256, norm_grad, 0)
    sums.tick()

    def first_norm(i, _):
        here = pl.ds(pl.multiple_of(i * 64, 64), 64)
        at, part = norm_back(i, tok_ref[here, :].astype(jnp.float32), gain1_ref[...][None], 0)
        dtok_ref[at, :] = (mg_v[at, :] + part).astype(low)
        return 0

    lax.fori_loop(0, count // 64, first_norm, 0)
    for i in range(3):
        small_v[steps, i:i + 1, :] = jnp.sum(gain_v[8 * i:8 * i + 8, :], axis=0, keepdims=True)
    small_v[steps, 2:3, :] = gain_v[16:17, :]
    small_v[steps, 3:8, :] = jnp.zeros((5, feat), jnp.float32)
    order = sums.chunks[0][2]

    def small_send(i):
        _, peer = partner_of(order[i])
        copy = pltpu.make_async_remote_copy(
            src_ref=small_v.at[steps + i], dst_ref=small_v.at[i], send_sem=tsem.at[i], recv_sem=usem.at[i],
            device_id=peer, device_id_type=MESH)
        copy.start()
        return copy

    def small_add(i, copy):
        copy.wait()
        total = small_v[steps + i] + small_v[i]
        if i + 1 < steps:
            small_v[steps + i + 1] = total
            return small_send(i + 1)
        sum_ref[...] = total

    tiny = small_send(0)
    sums.tick()
    for copy in results:
        copy.wait()

    def pick_each(n, _):
        at, one, two = place_tile(n)
        pick_v[:, at] = jnp.where(one, 1.0, 0.0).astype(low)
        other_v[:, at] = jnp.where(two, 1.0, 0.0).astype(low)
        return 0

    lax.fori_loop(0, padded // 128, pick_each, 0)

    def deliver(n, _):
        at = pl.ds(pl.multiple_of(n * 256, 256), 256)
        one = dot_nn(pick_v[...], ret_v[:, at]) * gates_ref[:, 0:1]
        two = dot_nn(other_v[...], ret_v[:, at]) * gates_ref[:, 1:2]
        out_ref[:, at] = (mixed_ref[:, at] + (one + two)).astype(low)
        return 0

    lax.fori_loop(0, feat // 256, deliver, 0)
    for i in range(steps):
        sums.tick()
        tiny = small_add(i, tiny)
    sums.finish()


def unwind(back, res, proj, prob, attt, normt, wqkv, wo, mixed, tokens, cotangent, place, gates, tally, gain1, gain2,
           dp_size, ex_size):
    kinds, cap, feat = back.shape
    count = tokens.shape[0]
    slots = kinds * cap
    padded = (slots + 127) // 128 * 128
    heads = feat // 64
    steps = (dp_size * ex_size).bit_length() - 1
    rows, wide = 8 * feat, feat // 2
    anyspace = pl.BlockSpec(memory_space=pl.ANY)
    vmem = pl.BlockSpec(memory_space=pltpu.VMEM)
    dma = pltpu.SemaphoreType.DMA
    low, full = jnp.bfloat16, jnp.float32
    shape = jax.ShapeDtypeStruct
    chunks = len(sum_chunks(dp_size, ex_size, rows))
    return pl.pallas_call(
        functools.partial(unwind_kernel, dp_size, ex_size, kinds, cap),
        out_shape=(shape((count, feat), low), shape((count, feat), low), shape((rows, wide), low), shape((8, feat), full)),
        in_specs=[anyspace] * 8 + [vmem] * 8,
        out_specs=(vmem,) * 4,
        scratch_shapes=[
            pltpu.VMEM((padded, feat), low), pltpu.VMEM((padded, feat), low), pltpu.VMEM((count, padded), low),
            pltpu.VMEM((count, padded), low), pltpu.VMEM((count, feat), full), pltpu.VMEM((count, feat), full),
            pltpu.VMEM((count, feat), low), pltpu.VMEM((count, feat), low), pltpu.VMEM((128, count), full),
            pltpu.VMEM((count, 3 * feat), low), pltpu.VMEM((heads, count + count // 2, count // 2), low),
            pltpu.VMEM((feat, count), low), pltpu.VMEM((feat, count), low), pltpu.VMEM((feat, 3 * feat), low),
            pltpu.VMEM((feat, feat), low), pltpu.VMEM((count, 3 * feat), low), pltpu.VMEM((rows, wide), low),
            pltpu.VMEM((rows, wide), low), pltpu.VMEM((rows, wide), low), pltpu.VMEM((24, feat), full),
            pltpu.VMEM((2 * steps, 8, feat), full),
            dma((ex_size,)), dma((ex_size,)), dma((chunks, steps)), dma((chunks, steps)), dma((chunks, steps)),
            dma((chunks, steps)), dma((steps,)), dma((steps,)), dma((9,)),
        ],
        compiler_params=pltpu.CompilerParams(collective_id=2, has_side_effects=True, vmem_limit_bytes=62 << 20),
        name="unwind",
    )(back.reshape(slots, feat), res.reshape(slots, feat), proj, prob, attt, normt, wqkv, wo, mixed, tokens, cotangent,
      place, gates, tally, gain1, gain2)


FROZEN = 2


def body(
    tokens,
    cotangent,
    chosen,
    gates,
    lengths,
    keep_mask,
    gain1,
    w_qkv,
    w_o,
    gain2,
    frozen_in,
    frozen_out,
    w_in,
    w_out,
):
    row_count, feat_width = tokens.shape
    owners = lax.axis_size("expert")
    dp_size = lax.axis_size("dp")
    kind_count = FROZEN + owners
    slot_count = ((2 * row_count * 5 // (4 * kind_count) + 7) // 8 * 8 + 15) // 16 * 16
    rows, fgrad, agrad, weights_in, projected, probs_t, attended_t, norm_t, mixed_rows, place, tally = attend(
        tokens, cotangent, chosen, gates, lengths, keep_mask, gain1, gain2, w_qkv, w_o, w_in[0], kind_count, slot_count,
        dp_size, owners)
    row_grads, served, weight_grads = experts(
        rows, fgrad, agrad, weights_in, w_out[0], frozen_in, frozen_out, dp_size, owners)
    summed = lax.psum_scatter(weight_grads, "dp", scatter_dimension=0, tiled=True).astype(jnp.float32)
    d_w_in = summed[:, :feat_width][None]
    d_w_out = summed[:, feat_width:][None]
    output, tokens_grad, total, small_sum = unwind(
        row_grads, served, projected, probs_t, attended_t, norm_t, w_qkv, w_o, mixed_rows, tokens, cotangent, place, gates,
        tally, gain1, gain2, dp_size, owners)
    blocks = total.reshape(8, feat_width, feat_width // 2).astype(jnp.float32)
    w_o_sum = jnp.concatenate([blocks[0], blocks[1]], axis=1)
    w_qkv_sum = jnp.concatenate([blocks[i] for i in (2, 5, 3, 6, 4, 7)], axis=1)
    return (
        output,
        tokens_grad,
        small_sum[0],
        w_qkv_sum,
        w_o_sum,
        small_sum[1],
        d_w_in,
        d_w_out,
        small_sum[2, :kind_count],
    )


def solution(mesh):
    placed = (
        P(("dp", "expert"), None),
        P(("dp", "expert"), None),
        P(("dp", "expert"), None),
        P(("dp", "expert"), None),
        P(("dp", "expert"), None),
        P(("dp", "expert")),
        P(),
        P(),
        P(),
        P(),
        P(),
        P(),
        P("expert", "dp", None),
        P("expert", "dp", None),
    )
    return jax.shard_map(
        body,
        mesh=mesh,
        in_specs=placed,
        out_specs=(
            P(("dp", "expert"), None),
            P(("dp", "expert"), None),
            P(),
            P(),
            P(),
            P(),
            P("expert", "dp", None),
            P("expert", "dp", None),
            P(),
        ),
        check_vma=False,
    )
```

```python
import functools
import jax
import jax.numpy as jnp
from jax import lax
from jax.experimental import pallas as pl
from jax.experimental.pallas import tpu as pltpu
from jax.sharding import PartitionSpec as P

MESH = pl.DeviceIdType.MESH


def butterfly(dp_size, ex_size):
    core = ("dp", 1)
    xs = [("dp", 2 << k) for k in range((dp_size // 2).bit_length() - 1)]
    depth = 4 if ex_size % 4 == 0 else 1
    wide = ex_size // depth
    ys = [("expert", 1 << k) for k in range(wide.bit_length() - 1)]
    zs = [("expert", wide << k) for k in range(depth.bit_length() - 1)]
    return core, xs, ys, zs


def group_of(stage):
    place = {"dp": lax.axis_index("dp"), "expert": lax.axis_index("expert")}
    mine = sum(lax.rem(place[axis] // mask, 2) << j for j, (axis, mask) in enumerate(stage))
    peers = []
    for m in range(1, 1 << len(stage)):
        peer = dict(place)
        for j, (axis, mask) in enumerate(stage):
            if m >> j & 1:
                peer[axis] = peer[axis] ^ mask
        peers.append((peer["dp"], peer["expert"]))
    return mine, peers


def dot_nn(a, b):
    return jnp.dot(a, b, preferred_element_type=jnp.float32)


def dot_nt(a, b):
    return lax.dot_general(a, b, (((1,), (1,)), ((), ())), preferred_element_type=jnp.float32)


def dot_tn(a, b):
    return lax.dot_general(a, b, (((0,), (0,)), ((), ())), preferred_element_type=jnp.float32)


GELU_A = 0.7978845608028654
GELU_B = GELU_A * 0.044715


def gelu_pair(h):
    square = h * h
    bend = jnp.tanh(h * (GELU_B * square + GELU_A))
    share = 0.5 * bend + 0.5
    slope = share + (0.5 * h) * (1.0 - bend * bend) * ((3.0 * GELU_B) * square + GELU_A)
    return h * share, slope


class Scatter:

    def __init__(self, dp, ex, far, core_v, pre_v, chip_v, sems):
        self.dp, self.ex, self.far = dp, ex, far
        self.core_v, self.pre_v, self.chip_v, self.sems = core_v, pre_v, chip_v, sems
        self.cores, self.chips = {}, {}

    def to_core(self, k, source):
        self.cores[k] = pltpu.make_async_remote_copy(
            src_ref=source, dst_ref=self.core_v.at[k], send_sem=self.sems[0].at[k], recv_sem=self.sems[1].at[k],
            device_id=(self.dp ^ 1, self.ex), device_id_type=MESH)
        self.cores[k].start()

    def to_chip(self, k, source):
        self.cores[k].wait_recv()

        def add(j, _):
            at = pl.ds(pl.multiple_of(j * 128, 128), 128)
            total = source[at, :].astype(jnp.float32) + self.core_v[k, at, :].astype(jnp.float32)
            self.pre_v[k, at, :] = total.astype(jnp.bfloat16)
            return 0

        lax.fori_loop(0, self.core_v.shape[1] // 128, add, 0)
        self.chips[k] = pltpu.make_async_remote_copy(
            src_ref=self.pre_v.at[k], dst_ref=self.chip_v.at[k], send_sem=self.sems[2].at[k], recv_sem=self.sems[3].at[k],
            device_id=(self.dp ^ (2 * k), self.ex), device_id_type=MESH)
        self.chips[k].start()

    def total(self, source, target):
        self.cores[0].wait_recv()
        for k in range(1, self.far):
            self.chips[k].wait_recv()

        def add(j, _):
            at = pl.ds(pl.multiple_of(j * 128, 128), 128)
            total = source[at, :].astype(jnp.float32) + self.core_v[0, at, :].astype(jnp.float32)
            for k in range(1, self.far):
                total = total + self.chip_v[k, at, :].astype(jnp.float32)
            target[at, :] = total
            return 0

        lax.fori_loop(0, self.core_v.shape[1] // 128, add, 0)
        for copy in list(self.cores.values()) + list(self.chips.values()):
            copy.wait_send()


def expert_kernel(dp_size, ex_size, cap, rows_hbm, fgrad_hbm, agrad_hbm, win_hbm, shard_hbm, fin_hbm, fout_hbm,
                  back_hbm, res_hbm, dwo_hbm, dwin_ref,
                  rows_v, grad_v, win_v, wout_v, act_v, hg_v, fin_v, fout_v, frow_v, fgrad_v, facc_v, fout_st,
                  rg_v, dwi_v, dwo_v, core_v, pre_v, chip_v, send_row, recv_row, send_back, recv_back, send_w, recv_w, fwd_w, got_w,
                  load_sem, frozen_sem, fload_sem, store_sem, dw_sem, *scatter_sems):
    dp = lax.axis_index("dp")
    ex = lax.axis_index("expert")
    shard = shard_hbm.shape[0]
    feat = shard_hbm.shape[1]
    slots = ex_size * cap
    far = dp_size // 2
    tiles = win_hbm.shape[0] // 256
    span = fin_v.shape[1]
    steps = fin_hbm.shape[0]

    barrier = pltpu.get_barrier_semaphore()
    for r in range(1, ex_size):
        pl.semaphore_signal(barrier, inc=1, device_id=(dp, ex ^ r), device_id_type=MESH)
    pl.semaphore_signal(barrier, inc=1, device_id=(dp ^ 1, ex), device_id_type=MESH)
    for k in range(1, far):
        pl.semaphore_signal(barrier, inc=1, device_id=(dp ^ (2 * k), ex), device_id_type=MESH)
    local = [
        pltpu.make_async_copy(rows_hbm.at[pl.ds(0, 2)], frow_v, load_sem.at[0]),
        pltpu.make_async_copy(fgrad_hbm, fgrad_v, load_sem.at[1]),
    ]
    for copy in local:
        copy.start()

    def frozen_load(i, slot):
        return (pltpu.make_async_copy(fin_hbm.at[i], fin_v.at[slot], frozen_sem.at[0, slot]),
                pltpu.make_async_copy(fout_hbm.at[i], fout_v.at[slot], frozen_sem.at[1, slot]))

    for copy in frozen_load(0, 0):
        copy.start()
    pl.semaphore_wait(barrier, ex_size - 1 + 1 + far - 1)

    row_copies = []
    for r in reversed(range(1, ex_size)):
        copy = pltpu.make_async_remote_copy(
            src_ref=rows_hbm.at[2 + (ex ^ r)], dst_ref=rows_v.at[pl.ds(r * cap, cap)],
            send_sem=send_row.at[r], recv_sem=recv_row.at[r], device_id=(dp, ex ^ r), device_id_type=MESH)
        copy.start()
        row_copies.append(copy)
    own = [pltpu.make_async_copy(rows_hbm.at[2 + ex], rows_v.at[pl.ds(0, cap)], load_sem.at[2]),
           pltpu.make_async_copy(win_hbm, win_v, load_sem.at[3]),
           pltpu.make_async_copy(shard_hbm, wout_v.at[pl.ds(pl.multiple_of(dp * shard, shard), shard)], load_sem.at[4])]
    for copy in own:
        copy.start()

    mine = wout_v.at[pl.ds(pl.multiple_of(dp * shard, shard), shard)]
    weight_copies = []
    for k in range(1, far):
        copy = pltpu.make_async_remote_copy(
            src_ref=shard_hbm, dst_ref=mine, send_sem=send_w.at[k], recv_sem=recv_w.at[k],
            device_id=(dp ^ (2 * k), ex), device_id_type=MESH)
        copy.start()
        weight_copies.append(copy)
    beside = pltpu.make_async_remote_copy(
        src_ref=shard_hbm, dst_ref=mine, send_sem=send_w.at[0], recv_sem=recv_w.at[0],
        device_id=(dp ^ 1, ex), device_id_type=MESH)
    beside.start()
    grad_copies = []
    for r in range(ex_size):
        copy = pltpu.make_async_copy(agrad_hbm.at[ex ^ r], grad_v.at[pl.ds(r * cap, cap)], fload_sem.at[r])
        copy.start()
        grad_copies.append(copy)

    for copy in local:
        copy.wait()
    per = steps // 2

    def frozen(i, _):
        slot = lax.rem(i, 2)
        for copy in frozen_load(i, slot):
            copy.wait()

        @pl.when(i + 1 < steps)
        def _():
            for copy in frozen_load(i + 1, 1 - slot):
                copy.start()
        which = i // per
        up = fin_v[slot]
        down = fout_v[slot]
        hidden = dot_nt(frow_v[which], up)
        slope_in = dot_nt(fgrad_v[which], down)
        active, slope = gelu_pair(hidden)
        result = dot_nn(active.astype(jnp.bfloat16), down)
        back = dot_nn((slope_in * slope).astype(jnp.bfloat16), up)
        first = lax.rem(i, per) == 0

        @pl.when(first)
        def _():
            facc_v[0, which] = result
            facc_v[1, which] = back

        @pl.when(jnp.logical_not(first))
        def _():
            facc_v[0, which] += result
            facc_v[1, which] += back
        return 0

    lax.fori_loop(0, steps, frozen, 0)
    fout_st[...] = facc_v[...].astype(jnp.bfloat16)
    stores = [pltpu.make_async_copy(fout_st.at[0], res_hbm.at[pl.ds(0, 2)], store_sem.at[0]),
              pltpu.make_async_copy(fout_st.at[1], back_hbm.at[pl.ds(0, 2)], store_sem.at[1])]
    for copy in stores:
        copy.start()

    passed = []
    for k in range(1, far):
        weight_copies[k - 1].wait_recv()
        theirs = wout_v.at[pl.ds(pl.multiple_of((dp ^ (2 * k)) * shard, shard), shard)]
        copy = pltpu.make_async_remote_copy(
            src_ref=theirs, dst_ref=theirs, send_sem=fwd_w.at[k], recv_sem=got_w.at[k],
            device_id=(dp ^ 1, ex), device_id_type=MESH)
        copy.start()
        passed.append(copy)
    beside.wait_recv()
    for copy in passed:
        copy.wait_recv()
    for copy in grad_copies:
        copy.wait()
    for copy in own:
        copy.wait()

    def slope_tile(t, _):
        at = pl.ds(pl.multiple_of(t * 256, 256), 256)
        hg_v[:, at] = dot_nt(grad_v[...], wout_v[at, :]).astype(jnp.bfloat16)
        return 0

    lax.fori_loop(0, tiles, slope_tile, 0)
    back_copies = []
    whole = list(reversed(range(ex_size)))
    groups = [whole[:ex_size // 4], whole[ex_size // 4:ex_size // 2], whole[ex_size // 2:]]
    for group in groups:
        here = pl.ds(group[-1] * cap, len(group) * cap)
        for r in group:
            if r:
                row_copies[ex_size - 1 - r].wait_recv()

        def hidden_tile(t, _, here=here):
            at = pl.ds(pl.multiple_of(t * 256, 256), 256)
            active, slope = gelu_pair(dot_nt(rows_v[here, :], win_v[at, :]))
            act_v[here, at] = active.astype(jnp.bfloat16)
            hg_v[here, at] = (hg_v[here, at].astype(jnp.float32) * slope).astype(jnp.bfloat16)
            return 0

        lax.fori_loop(0, tiles, hidden_tile, 0)

        def back_tile(n, _, here=here):
            at = pl.ds(pl.multiple_of(n * 256, 256), 256)
            rg_v[here, at] = dot_nn(hg_v[here, :], win_v[:, at]).astype(jnp.bfloat16)
            return 0

        lax.fori_loop(0, feat // 256, back_tile, 0)
        for r in group:
            source = rg_v.at[pl.ds(r * cap, cap)]
            if r:
                copy = pltpu.make_async_remote_copy(
                    src_ref=source, dst_ref=back_hbm.at[2 + ex], send_sem=send_back.at[r], recv_sem=recv_back.at[r],
                    device_id=(dp, ex ^ r), device_id_type=MESH)
            else:
                copy = pltpu.make_async_copy(source, back_hbm.at[2 + ex], store_sem.at[2])
            copy.start()
            back_copies.append(copy)

    width = 256 if shard % 256 == 0 else 128

    def shard_at(which):
        return pl.ds(pl.multiple_of(which * shard, shard), shard)

    def in_shard(which):
        def in_tile(j, _):
            at = pl.ds(pl.multiple_of(which * shard + j * width, width), width)
            dwi_v[at, :] = dot_tn(hg_v[:, at], rows_v[...]).astype(jnp.bfloat16)
            return 0

        lax.fori_loop(0, shard // width, in_tile, 0)

    scatter = Scatter(dp, ex, far, core_v, pre_v, chip_v, scatter_sems)
    for k in range(1, far):
        in_shard(dp ^ (2 * k + 1))
        scatter.to_core(k, dwi_v.at[shard_at(dp ^ (2 * k + 1))])
        in_shard(dp ^ (2 * k))
        scatter.to_chip(k, dwi_v.at[shard_at(dp ^ (2 * k))])
    in_shard(dp ^ 1)
    scatter.to_core(0, dwi_v.at[shard_at(dp ^ 1)])
    in_shard(dp)

    def out_tile(t, _):
        at = pl.ds(pl.multiple_of(t * 256, 256), 256)
        dwo_v[at, :] = dot_tn(act_v[:, at], grad_v[...]).astype(jnp.bfloat16)
        return 0

    lax.fori_loop(0, tiles, out_tile, 0)
    stores.append(pltpu.make_async_copy(dwo_v, dwo_hbm, dw_sem.at[0]))
    stores[-1].start()

    def result_tile(n, _):
        at = pl.ds(pl.multiple_of(n * 256, 256), 256)
        grad_v[:, at] = dot_nn(act_v[...], wout_v[:, at]).astype(jnp.bfloat16)
        return 0

    lax.fori_loop(0, feat // 256, result_tile, 0)
    for r in range(ex_size):
        stores.append(pltpu.make_async_copy(grad_v.at[pl.ds(r * cap, cap)], res_hbm.at[2 + (ex ^ r)], fload_sem.at[r]))
        stores[-1].start()
    scatter.total(dwi_v.at[shard_at(dp)], dwin_ref)
    for copy in stores:
        copy.wait()
    for copy in weight_copies:
        copy.wait_send()
    beside.wait_send()
    for copy in passed:
        copy.wait_send()
    for copy in row_copies:
        copy.wait_send()
    for copy in back_copies:
        copy.wait()


def experts(rows, fgrad, agrad, win, shard, fin, fout, dp_size, ex_size):
    kinds, cap, feat = rows.shape
    hidden = win.shape[0]
    slots = ex_size * cap
    far = dp_size // 2
    span = 768 if hidden % 768 == 0 else hidden
    steps = 2 * hidden // span
    anyspace = pl.BlockSpec(memory_space=pl.ANY)
    dma = pltpu.SemaphoreType.DMA
    low = jnp.bfloat16
    return pl.pallas_call(
        functools.partial(expert_kernel, dp_size, ex_size, cap),
        out_shape=(jax.ShapeDtypeStruct((kinds, cap, feat), low), jax.ShapeDtypeStruct((kinds, cap, feat), low),
                   jax.ShapeDtypeStruct((hidden, feat), low), jax.ShapeDtypeStruct(shard.shape, jnp.float32)),
        in_specs=[anyspace] * 7,
        out_specs=(anyspace,) * 3 + (pl.BlockSpec(memory_space=pltpu.VMEM),),
        scratch_shapes=[
            pltpu.VMEM((slots, feat), low), pltpu.VMEM((slots, feat), low),
            pltpu.VMEM((hidden, feat), low), pltpu.VMEM((hidden, feat), low),
            pltpu.VMEM((slots, hidden), low), pltpu.VMEM((slots, hidden), low),
            pltpu.VMEM((2, span, feat), low), pltpu.VMEM((2, span, feat), low),
            pltpu.VMEM((2, cap, feat), low), pltpu.VMEM((2, cap, feat), low),
            pltpu.VMEM((2, 2, cap, feat), jnp.float32), pltpu.VMEM((2, 2, cap, feat), low),
            pltpu.VMEM((slots, feat), low), pltpu.VMEM((hidden, feat), low), pltpu.VMEM((hidden, feat), low),
            pltpu.VMEM((far,) + shard.shape, low), pltpu.VMEM((far,) + shard.shape, low), pltpu.VMEM((far,) + shard.shape, low),
            dma((ex_size,)), dma((ex_size,)), dma((ex_size,)), dma((ex_size,)),
            dma((far,)), dma((far,)), dma((far,)), dma((far,)),
            dma((5,)), dma((2, 2)), dma((ex_size,)), dma((3,)), dma((1,)),
            dma((far,)), dma((far,)), dma((far,)), dma((far,)),
        ],
        compiler_params=pltpu.CompilerParams(collective_id=1, has_side_effects=True, vmem_limit_bytes=60 << 20),
        name="experts",
    )(rows, fgrad, agrad, win, shard, fin.reshape(steps, span, feat), fout.reshape(steps, span, feat))


def attend_kernel(dp_size, ex_size, kinds, cap, lengths_s, chosen_ref, gates_ref, keep_ref, tok_ref, cot_ref, gain1_ref,
                  gain2_ref, wqkv_hbm, wo_hbm, shard_hbm,
                  rows_hbm, fgrad_hbm, agrad_hbm, win_hbm, proj_hbm, prob_hbm, attt_hbm, normt_hbm, mixed_ref, place_ref,
                  count_ref,
                  wqkv_v, wo_v, norm_v, normt_v, proj_v, prob_v, attt_v, att_v, bias_v, grad_v, rows_v, place_v, shard_v,
                  send_g, recv_g, send_w, recv_w, fwd_w, got_w, load_sem, store_sem, prob_sem):
    dp = lax.axis_index("dp")
    ex = lax.axis_index("expert")
    count, feat = tok_ref.shape
    shard = shard_hbm.shape[0]
    far = dp_size // 2
    low = jnp.bfloat16

    barrier = pltpu.get_barrier_semaphore()
    for r in range(1, ex_size):
        pl.semaphore_signal(barrier, inc=1, device_id=(dp, ex ^ r), device_id_type=MESH)
    pl.semaphore_signal(barrier, inc=1, device_id=(dp ^ 1, ex), device_id_type=MESH)
    for k in range(1, far):
        pl.semaphore_signal(barrier, inc=1, device_id=(dp ^ (2 * k), ex), device_id_type=MESH)
    mine = win_hbm.at[pl.ds(pl.multiple_of(dp * shard, shard), shard)]
    loads = [pltpu.make_async_copy(wqkv_hbm, wqkv_v, load_sem.at[0]),
             pltpu.make_async_copy(wo_hbm, wo_v, load_sem.at[1]),
             pltpu.make_async_copy(shard_hbm, shard_v, load_sem.at[2])]
    for copy in loads:
        copy.start()

    kind = lax.broadcasted_iota(jnp.int32, (128, count), 0)
    first = chosen_ref[0:1, :]
    second = chosen_ref[1:2, :]
    hit_first = jnp.where(kind == first, 1.0, 0.0)
    hit_second = jnp.where(kind == second, 1.0, 0.0)
    hits = (hit_first + hit_second).astype(low)
    before = jnp.where(lax.broadcasted_iota(jnp.int32, (count, count), 0)
                       < lax.broadcasted_iota(jnp.int32, (count, count), 1), 1.0, 0.0).astype(low)
    ahead = dot_nn(hits, before)
    count_ref[...] = dot_nt(jnp.ones((8, count), low), hits)
    place_first = first.astype(jnp.float32) * cap + jnp.sum(hit_first * ahead, axis=0, keepdims=True)
    place_second = second.astype(jnp.float32) * cap + jnp.sum(hit_second * ahead, axis=0, keepdims=True)
    place_v[0:1, :] = place_first
    place_v[1:2, :] = place_second

    spot = lax.broadcasted_iota(jnp.int32, (1, count), 1)
    document = jnp.zeros((1, count), jnp.float32)
    end = lengths_s[0, 0]
    for j in range(1, lengths_s.shape[1] + 1):
        document = document + jnp.where(spot >= end, 1.0, 0.0)
        if j < lengths_s.shape[1]:
            end = end + lengths_s[0, j]
    place_v[2:3, :] = document
    place_v[3:4, :] = keep_ref[...].astype(jnp.float32)
    place_v[4:8, :] = jnp.zeros((4, count), jnp.float32)
    columns = place_v[...].T
    place_ref[...] = columns

    def chosen_rows(e):
        slot = (e * cap + lax.broadcasted_iota(jnp.int32, (cap, count), 0)).astype(jnp.float32)
        return slot == place_v[0:1, :], slot == place_v[1:2, :]

    def grad_rows(e, _):
        one, two = chosen_rows(e)
        gate = jnp.sum(jnp.where(one, gates_ref[0:1, :], jnp.where(two, gates_ref[1:2, :], 0.0)), axis=1, keepdims=True)
        pick = jnp.where(one | two, 1.0, 0.0).astype(low)
        grad_v[e] = (dot_nn(pick, cot_ref[...]) * gate).astype(low)
        return 0

    lax.fori_loop(0, kinds, grad_rows, 0)
    pl.semaphore_wait(barrier, ex_size - 1 + 1 + far - 1)
    grad_copies = []
    for r in reversed(range(1, ex_size)):
        copy = pltpu.make_async_remote_copy(
            src_ref=grad_v.at[2 + (ex ^ r)], dst_ref=agrad_hbm.at[ex],
            send_sem=send_g.at[r], recv_sem=recv_g.at[r], device_id=(dp, ex ^ r), device_id_type=MESH)
        copy.start()
        grad_copies.append(copy)
    weight_copies = []
    for k in range(1, far):
        copy = pltpu.make_async_remote_copy(
            src_ref=shard_hbm, dst_ref=mine, send_sem=send_w.at[k], recv_sem=recv_w.at[k],
            device_id=(dp ^ (2 * k), ex), device_id_type=MESH)
        copy.start()
        weight_copies.append(copy)
    beside = pltpu.make_async_remote_copy(
        src_ref=shard_hbm, dst_ref=mine, send_sem=send_w.at[0], recv_sem=recv_w.at[0],
        device_id=(dp ^ 1, ex), device_id_type=MESH)
    beside.start()
    stores = [pltpu.make_async_copy(grad_v.at[2 + ex], agrad_hbm.at[ex], store_sem.at[0]),
              pltpu.make_async_copy(grad_v.at[pl.ds(0, 2)], fgrad_hbm, store_sem.at[1])]
    for copy in stores:
        copy.start()

    loads[2].wait()
    stores.append(pltpu.make_async_copy(shard_v, mine, store_sem.at[6]))
    stores[-1].start()
    whole = tok_ref[...].astype(jnp.float32)
    centred = whole - jnp.mean(whole, axis=1, keepdims=True)
    scale = lax.rsqrt(jnp.mean(centred * centred, axis=1, keepdims=True) + 1e-05)
    norm_v[...] = (centred * scale * gain1_ref[...][None]).astype(low)
    loads[0].wait()

    def project(n, _):
        at = pl.ds(pl.multiple_of(n * 256, 256), 256)
        proj_v[:, at] = dot_nn(norm_v[...], wqkv_v[:, at]).astype(low)
        return 0

    lax.fori_loop(0, 3 * feat // 256, project, 0)
    stores.append(pltpu.make_async_copy(proj_v, proj_hbm, store_sem.at[2]))
    stores[-1].start()

    key = lax.broadcasted_iota(jnp.int32, (count, count), 0)
    query = lax.broadcasted_iota(jnp.int32, (count, count), 1)
    allowed = (columns[:, 2:3] == document) & (key <= query) & ((columns[:, 3:4] > 0.0) | (key == query))
    bias_v[...] = jnp.where(allowed, 0.0, -1e30)
    half = count // 2
    lower = lax.broadcasted_iota(jnp.int32, (count, 128), 1) < 64

    def head_pair(p, _):
        at = pl.multiple_of(p * 128, 128)
        q = proj_v[:, pl.ds(at, 128)]
        k = proj_v[:, pl.ds(pl.multiple_of(feat + p * 128, 128), 128)]
        vt = proj_v[:, pl.ds(pl.multiple_of(2 * feat + p * 128, 128), 128)].T
        for j in range(2):
            one = jnp.where(lower if j == 0 else jnp.logical_not(lower), k, jnp.zeros_like(k))
            for b in range(2):
                reach = (b + 1) * half
                scores = dot_nt(one[0:reach], q[b * half:(b + 1) * half]) * 0.125 + bias_v[0:reach, b * half:(b + 1) * half]
                powers = jnp.exp(scores - jnp.max(scores, axis=0, keepdims=True))
                probs = (powers * (1.0 / jnp.sum(powers, axis=0, keepdims=True))).astype(low)
                prob_v[2 * p + j, b * half:b * half + reach, :] = probs
                attt_v[pl.ds(at + 64 * j, 64), b * half:(b + 1) * half] = dot_nn(
                    vt[64 * j:64 * j + 64, 0:reach], probs).astype(low)
        pltpu.make_async_copy(prob_v.at[pl.ds(2 * p, 2)], prob_hbm.at[pl.ds(2 * p, 2)], prob_sem.at[p]).start()
        return 0

    lax.fori_loop(0, feat // 128, head_pair, 0)
    stores.append(pltpu.make_async_copy(attt_v, attt_hbm, store_sem.at[3]))
    stores[-1].start()

    def turn(n, _):
        at = pl.ds(pl.multiple_of(n * 128, 128), 128)
        att_v[:, at] = attt_v[at, :].T
        return 0

    lax.fori_loop(0, feat // 128, turn, 0)
    loads[1].wait()

    def mix(n, _):
        at = pl.ds(pl.multiple_of(n * 256, 256), 256)
        mixed_ref[:, at] = tok_ref[:, at].astype(jnp.float32) + dot_nn(att_v[...], wo_v[:, at])
        return 0

    lax.fori_loop(0, feat // 256, mix, 0)
    mixed = mixed_ref[...]
    centred = mixed - jnp.mean(mixed, axis=1, keepdims=True)
    scale = lax.rsqrt(jnp.mean(centred * centred, axis=1, keepdims=True) + 1e-05)
    att_v[...] = (centred * scale * gain2_ref[...][None]).astype(low)

    def token_rows(e, _):
        one, two = chosen_rows(e)
        pick = jnp.where(one | two, 1.0, 0.0).astype(low)
        rows_v[e] = dot_nn(pick, att_v[...]).astype(low)
        return 0

    lax.fori_loop(0, kinds, token_rows, 0)
    stores.append(pltpu.make_async_copy(rows_v, rows_hbm, store_sem.at[4]))
    stores[-1].start()

    def turn_norm(n, _):
        at = pl.ds(pl.multiple_of(n * 128, 128), 128)
        normt_v[at, :] = norm_v[:, at].T
        return 0

    lax.fori_loop(0, feat // 128, turn_norm, 0)
    stores.append(pltpu.make_async_copy(normt_v, normt_hbm, store_sem.at[5]))
    stores[-1].start()

    passed = []
    for k in range(1, far):
        weight_copies[k - 1].wait_recv()
        theirs = win_hbm.at[pl.ds(pl.multiple_of((dp ^ (2 * k)) * shard, shard), shard)]
        copy = pltpu.make_async_remote_copy(
            src_ref=theirs, dst_ref=theirs, send_sem=fwd_w.at[k], recv_sem=got_w.at[k],
            device_id=(dp ^ 1, ex), device_id_type=MESH)
        copy.start()
        passed.append(copy)
    for p in range(feat // 128):
        pltpu.make_async_copy(prob_v.at[pl.ds(2 * p, 2)], prob_hbm.at[pl.ds(2 * p, 2)], prob_sem.at[p]).wait()
    for copy in stores:
        copy.wait()
    for copy in weight_copies:
        copy.wait_send()
    beside.wait()
    for copy in passed:
        copy.wait()
    for copy in grad_copies:
        copy.wait()


def attend(tokens, cotangent, chosen, gates, lengths, keep, gain1, gain2, wqkv, wo, shard, kinds, cap, dp_size, ex_size):
    count, feat = tokens.shape
    heads = feat // 64
    anyspace = pl.BlockSpec(memory_space=pl.ANY)
    vmem = pl.BlockSpec(memory_space=pltpu.VMEM)
    dma = pltpu.SemaphoreType.DMA
    low = jnp.bfloat16
    shape = jax.ShapeDtypeStruct
    far = dp_size // 2
    return pl.pallas_call(
        functools.partial(attend_kernel, dp_size, ex_size, kinds, cap),
        out_shape=(shape((kinds, cap, feat), low), shape((2, cap, feat), low), shape((ex_size, cap, feat), low),
                   shape((dp_size * shard.shape[0], feat), low), shape((count, 3 * feat), low),
                   shape((heads, count + count // 2, count // 2), low), shape((feat, count), low),
                   shape((feat, count), low), shape((count, feat), jnp.float32), shape((count, 8), jnp.float32),
                   shape((8, 128), jnp.float32)),
        in_specs=[pl.BlockSpec(memory_space=pltpu.SMEM)] + [vmem] * 7 + [anyspace] * 3,
        out_specs=(anyspace,) * 8 + (vmem,) * 3,
        scratch_shapes=[
            pltpu.VMEM((feat, 3 * feat), low), pltpu.VMEM((feat, feat), low), pltpu.VMEM((count, feat), low),
            pltpu.VMEM((feat, count), low), pltpu.VMEM((count, 3 * feat), low),
            pltpu.VMEM((heads, count + count // 2, count // 2), low), pltpu.VMEM((feat, count), low),
            pltpu.VMEM((count, feat), low), pltpu.VMEM((count, count), jnp.float32),
            pltpu.VMEM((kinds, cap, feat), low), pltpu.VMEM((kinds, cap, feat), low), pltpu.VMEM((8, count), jnp.float32),
            pltpu.VMEM(shard.shape, low),
            dma((ex_size,)), dma((ex_size,)), dma((far,)), dma((far,)), dma((far,)), dma((far,)),
            dma((3,)), dma((7,)), dma((feat // 128,)),
        ],
        compiler_params=pltpu.CompilerParams(collective_id=0, has_side_effects=True, vmem_limit_bytes=56 << 20),
        name="attend",
    )(lengths, chosen.T, gates.T, keep[None], tokens, cotangent, gain1, gain2, wqkv, wo, shard)


class Sums:

    def __init__(self, chunks, blocks, acc, got, out, ssem, rsem, gsem, hsem):
        self.chunks, self.blocks, self.acc, self.got, self.out = chunks, blocks, acc, got, out
        self.sems = (ssem, rsem, gsem, hsem)
        self.offs = [[base] for base, _, _, _ in chunks]
        self.lens = [[rows] for _, rows, _, _ in chunks]
        self.land = [[base] for base, _, _, _ in chunks]
        self.copies = [None] * len(chunks)
        self.shift = [0] * len(chunks)
        self.stage = [0] * len(chunks)

    def scatter(self, c, i):
        base, _, order, _ = self.chunks[c]
        mine, peers = group_of(order[i])
        part = self.lens[c][i] >> len(order[i])
        source = self.acc if i else self.blocks
        self.copies[c] = []
        for m, peer in enumerate(peers, 1):
            give = pl.multiple_of(self.offs[c][i] + (mine ^ m) * part + self.shift[c], 16)
            copy = pltpu.make_async_remote_copy(
                src_ref=source.at[pl.ds(give, part)], dst_ref=self.got.at[pl.ds(self.land[c][i] + (m - 1) * part, part)],
                send_sem=self.sems[0].at[c, i, m], recv_sem=self.sems[1].at[c, i, m], device_id=peer, device_id_type=MESH)
            copy.start()
            self.copies[c].append(copy)
        self.offs[c].append(self.offs[c][i] + mine * part)
        self.lens[c].append(part)
        self.land[c].append(self.land[c][i] + len(peers) * part)

    def gather(self, c, i):
        _, peers = group_of(self.chunks[c][2][i])
        at = pl.ds(pl.multiple_of(self.offs[c][i + 1], 16), self.lens[c][i + 1])
        self.copies[c] = []
        for m, peer in enumerate(peers, 1):
            copy = pltpu.make_async_remote_copy(
                src_ref=self.out.at[at], dst_ref=self.out.at[at],
                send_sem=self.sems[2].at[c, i, m], recv_sem=self.sems[3].at[c, i, m], device_id=peer, device_id_type=MESH)
            copy.start()
            self.copies[c].append(copy)

    def start(self, phase):
        for c, chunk in enumerate(self.chunks):
            if chunk[3] == phase:
                self.scatter(c, 0)

    def advance(self, c):
        if not self.copies[c]:
            return
        base, _, order, _ = self.chunks[c]
        stages, s = len(order), self.stage[c]
        for copy in self.copies[c]:
            copy.wait()
        self.stage[c] += 1
        if s >= stages:
            i = 2 * stages - 1 - s
            self.copies[c] = None
            if i > 0:
                self.gather(c, i - 1)
            return
        part = self.lens[c][s + 1]
        source = self.acc if s else self.blocks
        target = self.acc if s + 1 < stages else self.out
        keep, begin = self.offs[c][s + 1], self.land[c][s]
        count = (1 << len(order[s])) - 1
        tile = part
        while tile > 128 or part % tile or tile % 16:
            tile -= 16
        move_in = self.shift[c]
        if s == 0:
            self.shift[c] = base // 2 - keep
        move_out = self.shift[c] if s + 1 < stages else 0

        def add(j, _):
            at = pl.ds(pl.multiple_of(keep + move_out + j * tile, 16), tile)
            come = pl.ds(pl.multiple_of(keep + move_in + j * tile, 16), tile)
            total = source[come, :].astype(jnp.float32)
            for m in range(count):
                other = pl.ds(pl.multiple_of(begin + m * part + j * tile, 16), tile)
                total = total + self.got[other, :].astype(jnp.float32)
            target[at, :] = total.astype(jnp.bfloat16)
            return 0

        lax.fori_loop(0, part // tile, add, 0)
        if s + 1 < stages:
            self.scatter(c, s + 1)
        else:
            self.gather(c, s)

    def tick(self):
        for c in range(len(self.chunks)):
            self.advance(c)

    def finish(self):
        while any(self.copies):
            self.tick()


def sum_chunks(dp_size, ex_size, rows):
    core, xs, ys, zs = butterfly(dp_size, ex_size)
    yxz, xyz, zyx = [[core], ys, xs, zs], [[core], xs, ys, zs], [[core], zs, ys, xs]
    if dp_size * ex_size * 16 <= 512:
        return [(0, 1536, yxz, 0), (1536, 2048, yxz, 1), (3584, 1024, yxz, 2), (4608, 1024, xyz, 2), (5632, 512, zyx, 2)]
    third = rows // 3
    return [(0, third, yxz, 2), (third, third, xyz, 2), (2 * third, third, zyx, 2)]


def unwind_kernel(dp_size, ex_size, kinds, cap, dwo_hbm, back_hbm, res_hbm, proj_hbm, prob_hbm, attt_hbm, normt_hbm, wqkv_hbm, wo_hbm,
                  mixed_ref, tok_ref, cot_ref, place_ref, gates_ref, count_ref, gain1_ref, gain2_ref,
                  out_ref, dtok_ref, qkv_hbm, wide_hbm, sum_ref, dwout_ref,
                  back_v, ret_v, pick_v, other_v, g_v, mg_v, branch_v, da_v, dqt_v, proj_v, prob_v, attt_v, normt_v, wqkv_v,
                  wo_v, pg_v, blocks_v, acc_v, got_v, gain_v, small_v, total_ref, own_v, core_v, pre_v, chip_v, send_res, recv_res, ssem, rsem, gsem, hsem, tsem, usem,
                  load_sem, *scatter_sems):
    dp = lax.axis_index("dp")
    ex = lax.axis_index("expert")
    count, feat = tok_ref.shape
    slots = kinds * cap
    padded = back_v.shape[0]
    low = jnp.bfloat16
    steps = (dp_size * ex_size).bit_length() - 1

    barrier = pltpu.get_barrier_semaphore()
    for r in range(1, ex_size):
        pl.semaphore_signal(barrier, inc=1, device_id=(dp, ex ^ r), device_id_type=MESH)
    for k in range(1, dp_size):
        pl.semaphore_signal(barrier, inc=1, device_id=(dp ^ k, ex), device_id_type=MESH)
    loads = [pltpu.make_async_copy(source, target, load_sem.at[i]) for i, (source, target) in enumerate([
        (back_hbm, back_v.at[pl.ds(0, slots)]), (attt_hbm, attt_v), (wo_hbm, wo_v), (prob_hbm, prob_v), (proj_hbm, proj_v),
        (normt_hbm, normt_v), (wqkv_hbm, wqkv_v)])]
    for copy in loads:
        copy.start()
    pl.semaphore_wait(barrier, ex_size - 1 + dp_size - 1)
    results = []
    for r in reversed(range(1, ex_size)):
        copy = pltpu.make_async_remote_copy(
            src_ref=res_hbm.at[pl.ds(pl.multiple_of((2 + (ex ^ r)) * cap, 16), cap)],
            dst_ref=ret_v.at[pl.ds(pl.multiple_of((2 + ex) * cap, 16), cap)],
            send_sem=send_res.at[r], recv_sem=recv_res.at[r], device_id=(dp, ex ^ r), device_id_type=MESH)
        copy.start()
        results.append(copy)
    own = pl.ds(pl.multiple_of((2 + ex) * cap, 16), cap)
    results.append(pltpu.make_async_copy(res_hbm.at[own], ret_v.at[own], load_sem.at[7]))
    results.append(pltpu.make_async_copy(res_hbm.at[pl.ds(0, 2 * cap)], ret_v.at[pl.ds(0, 2 * cap)], load_sem.at[8]))
    for copy in results[-2:]:
        copy.start()
    far = dp_size // 2
    shard = dwout_ref.shape[0]
    scatter = Scatter(dp, ex, far, core_v, pre_v, chip_v, scatter_sems)

    def shard_at(which):
        return dwo_hbm.at[pl.ds(pl.multiple_of(which * shard, shard), shard)]

    for k in list(range(1, far)) + [0]:
        scatter.to_core(k, shard_at(dp ^ (2 * k + 1)))
    own_copies = [pltpu.make_async_copy(shard_at(dp ^ (2 * k)), own_v.at[k], load_sem.at[9 + k]) for k in range(far)]
    for copy in own_copies:
        copy.start()
    if padded > slots:
        ret_v[slots:, :] = jnp.zeros((padded - slots, feat), low)
        back_v[slots:, :] = jnp.zeros((padded - slots, feat), low)
    sums = Sums(sum_chunks(dp_size, ex_size, blocks_v.shape[0]), blocks_v, acc_v, got_v, total_ref, ssem, rsem, gsem, hsem)

    def place_tile(n):
        at = pl.ds(pl.multiple_of(n * 128, 128), 128)
        slot = (n * 128 + lax.broadcasted_iota(jnp.int32, (count, 128), 1)).astype(jnp.float32)
        return at, slot == place_ref[:, 0:1], slot == place_ref[:, 1:2]

    def pick_both(n, _):
        at, one, two = place_tile(n)
        pick_v[:, at] = jnp.where(one | two, 1.0, 0.0).astype(low)
        return 0

    lax.fori_loop(0, padded // 128, pick_both, 0)
    loads[0].wait()

    def collect(n, _):
        at = pl.ds(pl.multiple_of(n * 256, 256), 256)
        g_v[:, at] = dot_nn(pick_v[...], back_v[:, at])
        return 0

    lax.fori_loop(0, feat // 256, collect, 0)
    for copy in own_copies:
        copy.wait()
    for k in range(1, far):
        scatter.to_chip(k, own_v.at[k])
    gain_v[...] = jnp.zeros_like(gain_v)
    gain_v[16:24, 0:128] = count_ref[...]

    def norm_back(i, whole, gain, target):
        at = pl.ds(pl.multiple_of(i * 64, 64), 64)
        centred = whole - jnp.mean(whole, axis=1, keepdims=True)
        scale = lax.rsqrt(jnp.mean(centred * centred, axis=1, keepdims=True) + 1e-05)
        unit = centred * scale
        grad = g_v[at, :]
        weighted = grad * unit
        gain_v[target:target + 8, :] += jnp.sum(weighted.reshape(8, 8, feat), axis=0)
        scaled = grad * gain
        return at, scale * (scaled - jnp.mean(scaled, axis=1, keepdims=True)
                            - unit * jnp.mean(scaled * unit, axis=1, keepdims=True))

    def second_norm(i, _):
        at, part = norm_back(i, mixed_ref[pl.ds(pl.multiple_of(i * 64, 64), 64), :], gain2_ref[...][None], 8)
        grad = cot_ref[at, :].astype(jnp.float32) + part
        mg_v[at, :] = grad
        branch_v[at, :] = grad.astype(low)
        return 0

    lax.fori_loop(0, count // 64, second_norm, 0)
    loads[1].wait()
    wide = feat // 2

    def out_weight(b, _):
        at = pl.ds(pl.multiple_of(b * wide, 128), wide)
        blocks_v[pl.ds(pl.multiple_of(b * feat, 16), feat), :] = dot_nn(attt_v[...], branch_v[:, at]).astype(low)
        return 0

    lax.fori_loop(0, 2, out_weight, 0)
    sums.start(0)
    loads[2].wait()

    def attended_grad(n, _):
        at = pl.ds(pl.multiple_of(n * 256, 256), 256)
        da_v[:, at] = dot_nt(branch_v[...], wo_v[at, :]).astype(low)
        return 0

    lax.fori_loop(0, feat // 256, attended_grad, 0)
    loads[3].wait()
    loads[4].wait()
    half = count // 2
    lower = lax.broadcasted_iota(jnp.int32, (count, 128), 1) < 64

    def head_pair(p, _):
        at_q = pl.ds(pl.multiple_of(p * 128, 128), 128)
        at_k = pl.ds(pl.multiple_of(feat + p * 128, 128), 128)
        at_v = pl.ds(pl.multiple_of(2 * feat + p * 128, 128), 128)
        q, k, v, da = proj_v[:, at_q], proj_v[:, at_k], proj_v[:, at_v], da_v[:, at_q]
        kt = k.T
        key_near = key_far = value_near = value_far = 0.0
        for j in range(2):
            mask = lower if j == 0 else jnp.logical_not(lower)
            qj, vj, daj = [jnp.where(mask, w, jnp.zeros_like(w)) for w in (q, v, da)]
            for b in range(2):
                reach, here = (b + 1) * half, slice(b * half, (b + 1) * half)
                prob = prob_v[2 * p + j, b * half:b * half + reach, :]
                full = prob.astype(jnp.float32)
                grad = dot_nt(vj[0:reach], da[here])
                score = (full * (grad - jnp.sum(full * grad, axis=0, keepdims=True))).astype(low)
                dqt_v[64 * j:64 * j + 64, here] = dot_nn(kt[64 * j:64 * j + 64, 0:reach], score)
                key_near += dot_nn(score[0:half], qj[here])
                value_near += dot_nn(prob[0:half], daj[here])
                if b:
                    key_far += dot_nn(score[half:], qj[here])
                    value_far += dot_nn(prob[half:], daj[here])
        pg_v[:, at_q] = (dqt_v[...].T * 0.125).astype(low)
        pg_v[0:half, at_k] = (key_near * 0.125).astype(low)
        pg_v[half:, at_k] = (key_far * 0.125).astype(low)
        pg_v[0:half, at_v] = value_near.astype(low)
        pg_v[half:, at_v] = value_far.astype(low)
        return 0

    pairs = feat // 128
    for turn in range(2):
        lax.fori_loop(turn * pairs // 2, (turn + 1) * pairs // 2, head_pair, 0)
        if turn == 0:
            loads[5].wait()
        sums.tick()

        def weight_block(c, _, turn=turn):
            at = pl.ds(pl.multiple_of(c * feat + turn * wide, 128), wide)
            into = pl.ds(pl.multiple_of(2 * feat + (3 * turn + c) * feat, 16), feat)
            blocks_v[into, :] = dot_nn(normt_v[...], pg_v[:, at]).astype(low)
            return 0

        lax.fori_loop(0, 3, weight_block, 0)
        sums.start(1 + turn)
    loads[6].wait()
    sums.tick()

    def norm_grad(n, _):
        at = pl.ds(pl.multiple_of(n * 256, 256), 256)
        g_v[:, at] = dot_nt(pg_v[...], wqkv_v[at, :])
        return 0

    lax.fori_loop(0, feat // 256, norm_grad, 0)
    sums.tick()

    def first_norm(i, _):
        here = pl.ds(pl.multiple_of(i * 64, 64), 64)
        at, part = norm_back(i, tok_ref[here, :].astype(jnp.float32), gain1_ref[...][None], 0)
        dtok_ref[at, :] = (mg_v[at, :] + part).astype(low)
        return 0

    lax.fori_loop(0, count // 64, first_norm, 0)
    for i in range(3):
        small_v[steps, i:i + 1, :] = jnp.sum(gain_v[8 * i:8 * i + 8, :], axis=0, keepdims=True)
    small_v[steps, 2:3, :] = gain_v[16:17, :]
    small_v[steps, 3:8, :] = jnp.zeros((5, feat), jnp.float32)
    order = sums.chunks[0][2]

    def small_send(i):
        copies = []
        for m, peer in enumerate(group_of(order[i])[1], 1):
            copy = pltpu.make_async_remote_copy(
                src_ref=small_v.at[steps + i], dst_ref=small_v.at[slot_of[i] + m - 1], send_sem=tsem.at[i, m],
                recv_sem=usem.at[i, m], device_id=peer, device_id_type=MESH)
            copy.start()
            copies.append(copy)
        return copies

    def small_add(i, copies):
        for copy in copies:
            copy.wait()
        mine, peers = group_of(order[i])
        total = jnp.zeros_like(sum_ref[...])
        for n in range(len(peers) + 1):
            term = small_v[steps + i]
            for m in range(1, len(peers) + 1):
                term = jnp.where(mine == n ^ m, small_v[slot_of[i] + m - 1], term)
            total = total + term
        if i + 1 < len(order):
            small_v[steps + i + 1] = total
            return small_send(i + 1)
        sum_ref[...] = total

    slot_of = [steps + len(order) + sum((1 << len(stage)) - 1 for stage in order[:i]) for i in range(len(order))]
    tiny = small_send(0)
    sums.tick()
    for copy in results:
        copy.wait()

    def pick_each(n, _):
        at, one, two = place_tile(n)
        pick_v[:, at] = jnp.where(one, 1.0, 0.0).astype(low)
        other_v[:, at] = jnp.where(two, 1.0, 0.0).astype(low)
        return 0

    lax.fori_loop(0, padded // 128, pick_each, 0)

    def deliver(n, _):
        at = pl.ds(pl.multiple_of(n * 256, 256), 256)
        one = dot_nn(pick_v[...], ret_v[:, at]) * gates_ref[:, 0:1]
        two = dot_nn(other_v[...], ret_v[:, at]) * gates_ref[:, 1:2]
        out_ref[:, at] = (mixed_ref[:, at] + (one + two)).astype(low)
        return 0

    lax.fori_loop(0, feat // 256, deliver, 0)
    scatter.total(own_v.at[0], dwout_ref)
    for i in range(len(order)):
        sums.tick()
        tiny = small_add(i, tiny)
    sums.finish()
    finals = []
    for b in range(8):
        turn, c = (b - 2) // 3, (b - 2) % 3
        target = wide_hbm.at[:, pl.ds(b * wide, wide)] if b < 2 else qkv_hbm.at[:, pl.ds(c * feat + turn * wide, wide)]
        finals.append(pltpu.make_async_copy(total_ref.at[pl.ds(b * feat, feat)], target, load_sem.at[b]))
        finals[-1].start()
    for copy in finals:
        copy.wait()


def unwind(dwo, back, res, proj, prob, attt, normt, wqkv, wo, mixed, tokens, cotangent, place, gates, tally, gain1, gain2,
           dp_size, ex_size):
    kinds, cap, feat = back.shape
    count = tokens.shape[0]
    slots = kinds * cap
    padded = (slots + 127) // 128 * 128
    heads = feat // 64
    steps = (dp_size * ex_size).bit_length() - 1
    rows, wide = 8 * feat, feat // 2
    anyspace = pl.BlockSpec(memory_space=pl.ANY)
    vmem = pl.BlockSpec(memory_space=pltpu.VMEM)
    dma = pltpu.SemaphoreType.DMA
    low, full = jnp.bfloat16, jnp.float32
    shape = jax.ShapeDtypeStruct
    chunks = len(sum_chunks(dp_size, ex_size, rows))
    stages = 4
    shard, far = dwo.shape[0] // dp_size, dp_size // 2
    return pl.pallas_call(
        functools.partial(unwind_kernel, dp_size, ex_size, kinds, cap),
        out_shape=(shape((count, feat), low), shape((count, feat), low), shape((feat, 3 * feat), low), shape((feat, feat), low), shape((8, feat), full),
                   shape((shard, feat), full)),
        in_specs=[anyspace] * 9 + [vmem] * 8,
        out_specs=(vmem, vmem, anyspace, anyspace, vmem, vmem),
        scratch_shapes=[
            pltpu.VMEM((padded, feat), low), pltpu.VMEM((padded, feat), low), pltpu.VMEM((count, padded), low),
            pltpu.VMEM((count, padded), low), pltpu.VMEM((count, feat), full), pltpu.VMEM((count, feat), full),
            pltpu.VMEM((count, feat), low), pltpu.VMEM((count, feat), low), pltpu.VMEM((128, count), full),
            pltpu.VMEM((count, 3 * feat), low), pltpu.VMEM((heads, count + count // 2, count // 2), low),
            pltpu.VMEM((feat, count), low), pltpu.VMEM((feat, count), low), pltpu.VMEM((feat, 3 * feat), low),
            pltpu.VMEM((feat, feat), low), pltpu.VMEM((count, 3 * feat), low), pltpu.VMEM((rows, wide), low),
            pltpu.VMEM((rows // 2, wide), low), pltpu.VMEM((rows, wide), low), pltpu.VMEM((24, feat), full),
            pltpu.VMEM((steps + stages + 3 * stages, 8, feat), full), pltpu.VMEM((rows, wide), low), pltpu.VMEM((far, shard, feat), low), pltpu.VMEM((far, shard, feat), low),
            pltpu.VMEM((far, shard, feat), low), pltpu.VMEM((far, shard, feat), low),
            dma((ex_size,)), dma((ex_size,)), dma((chunks, stages, 4)), dma((chunks, stages, 4)),
            dma((chunks, stages, 4)), dma((chunks, stages, 4)), dma((stages, 4)), dma((stages, 4)), dma((9 + far,)),
            dma((far,)), dma((far,)), dma((far,)), dma((far,)),
        ],
        compiler_params=pltpu.CompilerParams(collective_id=2, has_side_effects=True, vmem_limit_bytes=62 << 20),
        name="unwind",
    )(dwo, back.reshape(slots, feat), res.reshape(slots, feat), proj, prob, attt, normt, wqkv, wo, mixed, tokens, cotangent,
      place, gates, tally, gain1, gain2)


FROZEN = 2


def body(
    tokens,
    cotangent,
    chosen,
    gates,
    lengths,
    keep_mask,
    gain1,
    w_qkv,
    w_o,
    gain2,
    frozen_in,
    frozen_out,
    w_in,
    w_out,
):
    row_count, feat_width = tokens.shape
    owners = lax.axis_size("expert")
    dp_size = lax.axis_size("dp")
    kind_count = FROZEN + owners
    slot_count = ((2 * row_count * 5 // (4 * kind_count) + 7) // 8 * 8 + 15) // 16 * 16
    rows, fgrad, agrad, weights_in, projected, probs_t, attended_t, norm_t, mixed_rows, place, tally = attend(
        tokens, cotangent, chosen, gates, lengths, keep_mask, gain1, gain2, w_qkv, w_o, w_in[0], kind_count, slot_count,
        dp_size, owners)
    row_grads, served, out_grads, d_w_in = experts(
        rows, fgrad, agrad, weights_in, w_out[0], frozen_in, frozen_out, dp_size, owners)
    output, tokens_grad, w_qkv_sum, w_o_sum, small_sum, d_w_out = unwind(
        out_grads, row_grads, served, projected, probs_t, attended_t, norm_t, w_qkv, w_o, mixed_rows, tokens, cotangent, place,
        gates, tally, gain1, gain2, dp_size, owners)
    return (
        output,
        tokens_grad,
        small_sum[0],
        w_qkv_sum.astype(jnp.float32),
        w_o_sum.astype(jnp.float32),
        small_sum[1],
        d_w_in[None],
        d_w_out[None],
        small_sum[2, :kind_count],
    )


def solution(mesh):
    placed = (
        P(("dp", "expert"), None),
        P(("dp", "expert"), None),
        P(("dp", "expert"), None),
        P(("dp", "expert"), None),
        P(("dp", "expert"), None),
        P(("dp", "expert")),
        P(),
        P(),
        P(),
        P(),
        P(),
        P(),
        P("expert", "dp", None),
        P("expert", "dp", None),
    )
    return jax.shard_map(
        body,
        mesh=mesh,
        in_specs=placed,
        out_specs=(
            P(("dp", "expert"), None),
            P(("dp", "expert"), None),
            P(),
            P(),
            P(),
            P(),
            P("expert", "dp", None),
            P("expert", "dp", None),
            P(),
        ),
        check_vma=False,
    )
```

```python
import functools
import jax
import jax.numpy as jnp
from jax import lax
from jax.experimental import pallas as pl
from jax.experimental.pallas import tpu as pltpu
from jax.sharding import PartitionSpec as P

MESH = pl.DeviceIdType.MESH


def butterfly(dp_size, ex_size):
    core = ("dp", 1)
    xs = [("dp", 2 << k) for k in range((dp_size // 2).bit_length() - 1)]
    depth = 4 if ex_size % 4 == 0 else 1
    wide = ex_size // depth
    ys = [("expert", 1 << k) for k in range(wide.bit_length() - 1)]
    zs = [("expert", wide << k) for k in range(depth.bit_length() - 1)]
    return core, xs, ys, zs


def group_of(stage):
    place = {"dp": lax.axis_index("dp"), "expert": lax.axis_index("expert")}
    mine = sum(lax.rem(place[axis] // mask, 2) << j for j, (axis, mask) in enumerate(stage))
    peers = []
    for m in range(1, 1 << len(stage)):
        peer = dict(place)
        for j, (axis, mask) in enumerate(stage):
            if m >> j & 1:
                peer[axis] = peer[axis] ^ mask
        peers.append((peer["dp"], peer["expert"]))
    return mine, peers


def dot_nn(a, b):
    return jnp.dot(a, b, preferred_element_type=jnp.float32)


def dot_nt(a, b):
    return lax.dot_general(a, b, (((1,), (1,)), ((), ())), preferred_element_type=jnp.float32)


def dot_tn(a, b):
    return lax.dot_general(a, b, (((0,), (0,)), ((), ())), preferred_element_type=jnp.float32)


GELU_A = 0.7978845608028654
GELU_B = GELU_A * 0.044715


def gelu_pair(h):
    square = h * h
    bend = jnp.tanh(h * (GELU_B * square + GELU_A))
    share = 0.5 * bend + 0.5
    slope = share + (0.5 * h) * (1.0 - bend * bend) * ((3.0 * GELU_B) * square + GELU_A)
    return h * share, slope


def remote(source, target, pair, at, device):
    return pltpu.make_async_remote_copy(
        src_ref=source, dst_ref=target, send_sem=pair.at[(0,) + at], recv_sem=pair.at[(1,) + at], device_id=device,
        device_id_type=MESH)


class Gather:

    def __init__(self, dp, ex, far, source, whole, sems):
        self.dp, self.ex, self.far, self.source, self.whole, self.sems = dp, ex, far, source, whole, sems
        self.rows = source.shape[0]

    def at(self, which):
        return self.whole.at[pl.ds(pl.multiple_of(which * self.rows, 16), self.rows)]

    def first(self, k):
        return remote(self.source, self.at(self.dp), self.sems, (0, k), (self.dp ^ (2 * k if k else 1), self.ex))

    def second(self, k):
        theirs = self.at(self.dp ^ (2 * k))
        return remote(theirs, theirs, self.sems, (1, k), (self.dp ^ 1, self.ex))

    def start(self):
        for k in list(range(1, self.far)) + [0]:
            self.first(k).start()

    def forward(self):
        for k in range(1, self.far):
            self.first(k).wait_recv()
            self.second(k).start()

    def finish(self):
        self.first(0).wait()
        for k in range(1, self.far):
            self.first(k).wait_send()
            self.second(k).wait()


class Scatter:

    def __init__(self, dp, ex, far, source, core_v, pre_v, chip_v, sems):
        self.dp, self.ex, self.far, self.source = dp, ex, far, source
        self.core_v, self.pre_v, self.chip_v, self.sems = core_v, pre_v, chip_v, sems
        self.rows = core_v.shape[1]

    def at(self, which):
        return self.source.at[pl.ds(pl.multiple_of(which * self.rows, 16), self.rows)]

    def core(self, k):
        return remote(self.at(self.dp ^ (2 * k + 1)), self.core_v.at[k], self.sems, (0, k), (self.dp ^ 1, self.ex))

    def chip(self, k):
        return remote(self.pre_v.at[k - 1], self.chip_v.at[k - 1], self.sems, (1, k), (self.dp ^ (2 * k), self.ex))

    def to_chips(self):
        for k in range(1, self.far):
            self.core(k).wait_recv()
            source = self.at(self.dp ^ (2 * k))

            def add(j, _):
                at = pl.ds(pl.multiple_of(j * 128, 128), 128)
                total = source[at, :].astype(jnp.float32) + self.core_v[k, at, :].astype(jnp.float32)
                self.pre_v[k - 1, at, :] = total.astype(jnp.bfloat16)
                return 0

            lax.fori_loop(0, self.rows // 128, add, 0)
            self.chip(k).start()

    def finish(self):
        self.core(0).wait_recv()
        for k in range(1, self.far):
            self.chip(k).wait_recv()
        source = self.at(self.dp)

        def add(j, _):
            at = pl.ds(pl.multiple_of(j * 128, 128), 128)
            total = source[at, :].astype(jnp.float32) + self.core_v[0, at, :].astype(jnp.float32)
            for k in range(1, self.far):
                total = total + self.chip_v[k - 1, at, :].astype(jnp.float32)
            self.core_v[0, at, :] = total.astype(jnp.bfloat16)
            return 0

        lax.fori_loop(0, self.rows // 128, add, 0)
        for k in range(self.far):
            self.core(k).wait_send()
            if k:
                self.chip(k).wait_send()


class Sums:

    def __init__(self, chunks, blocks, acc, got, out, scatter_sems, gather_sems, own_sems):
        self.chunks, self.blocks, self.acc, self.got, self.out = chunks, blocks, acc, got, out
        self.scatter_sems, self.gather_sems, self.own_sems = scatter_sems, gather_sems, own_sems
        self.offs = [[base] for base, _, _, _ in chunks]
        self.lens = [[rows] for _, rows, _, _ in chunks]
        self.land = [[base] for base, _, _, _ in chunks]
        self.copies = [None] * len(chunks)
        self.shift = [0] * len(chunks)
        self.stage = [0] * len(chunks)
        self.own = [None] * len(chunks)

    def scatter(self, c, i):
        base, _, order, _ = self.chunks[c]
        mine, peers = group_of(order[i])
        part = self.lens[c][i] >> len(order[i])
        source = self.acc if i else self.blocks
        self.copies[c] = []
        for m, peer in enumerate(peers, 1):
            give = pl.multiple_of(self.offs[c][i] + (mine ^ m) * part + self.shift[c], 16)
            self.copies[c].append(remote(
                source.at[pl.ds(give, part)], self.got.at[pl.ds(self.land[c][i] + (m - 1) * part, part)],
                self.scatter_sems, (c, i, m), peer))
            self.copies[c][-1].start()
        self.offs[c].append(self.offs[c][i] + mine * part)
        self.lens[c].append(part)
        self.land[c].append(self.land[c][i] + len(peers) * part)

    def gather(self, c, i):
        stages = len(self.chunks[c][2])
        _, peers = group_of(self.chunks[c][2][i])
        part = self.lens[c][i + 1]
        target = self.out.at[pl.ds(pl.multiple_of(self.offs[c][i + 1], 16), part)]
        source = target
        if i + 1 == stages:
            source = self.acc.at[pl.ds(pl.multiple_of(self.offs[c][i + 1] + self.shift[c], 16), part)]
            self.own[c] = pltpu.make_async_copy(source, target, self.own_sems.at[c])
            self.own[c].start()
        self.copies[c] = []
        for m, peer in enumerate(peers, 1):
            self.copies[c].append(remote(source, target, self.gather_sems, (c, i, m), peer))
            self.copies[c][-1].start()

    def start(self, phase):
        for c, chunk in enumerate(self.chunks):
            if chunk[3] == phase:
                self.scatter(c, 0)

    def advance(self, c):
        if not self.copies[c]:
            return
        base, _, order, _ = self.chunks[c]
        stages, s = len(order), self.stage[c]
        for copy in self.copies[c]:
            copy.wait()
        self.stage[c] += 1
        if s >= stages:
            i = 2 * stages - 1 - s
            self.copies[c] = None
            if s == stages:
                self.own[c].wait()
            if i > 0:
                self.gather(c, i - 1)
            return
        part = self.lens[c][s + 1]
        source = self.acc if s else self.blocks
        keep, begin = self.offs[c][s + 1], self.land[c][s]
        count = (1 << len(order[s])) - 1
        tile = part
        while tile > 128 or part % tile or tile % 16:
            tile -= 16
        move_in = self.shift[c]
        if s == 0:
            self.shift[c] = base // 2 - keep
        move_out = self.shift[c]

        def add(j, _):
            at = pl.ds(pl.multiple_of(keep + move_out + j * tile, 16), tile)
            come = pl.ds(pl.multiple_of(keep + move_in + j * tile, 16), tile)
            total = source[come, :].astype(jnp.float32)
            for m in range(count):
                other = pl.ds(pl.multiple_of(begin + m * part + j * tile, 16), tile)
                total = total + self.got[other, :].astype(jnp.float32)
            self.acc[at, :] = total.astype(jnp.bfloat16)
            return 0

        lax.fori_loop(0, part // tile, add, 0)
        if s + 1 < stages:
            self.scatter(c, s + 1)
        else:
            self.gather(c, s)

    def tick(self):
        for c in reversed(range(len(self.chunks))):
            self.advance(c)

    def finish(self):
        while any(self.copies):
            self.tick()


def sum_chunks(dp_size, ex_size, rows):
    core, xs, ys, zs = butterfly(dp_size, ex_size)
    yxz, xyz, zyx = [[core], ys, xs, zs], [[core], xs, ys, zs], [[core], zs, ys, xs]
    if dp_size * ex_size * 16 <= 512:
        return [(0, 1536, yxz, 0), (1536, 2048, yxz, 1), (3584, 1024, yxz, 2), (4608, 1024, xyz, 2), (5632, 512, zyx, 2)]
    third = rows // 3
    return [(0, third, yxz, 2), (third, third, xyz, 2), (2 * third, third, zyx, 2)]


def layer_kernel(dp_size, ex_size, kinds, cap,
                 lengths_s, chosen_ref, gatest_ref, keep_ref, gates_ref, tok_ref, cot_ref, gain1_ref, gain2_ref,
                 wqkv_hbm, wo_hbm, in_hbm, outw_hbm, fin_hbm, fout_hbm,
                 out_ref, dtok_ref, total_hbm, sum_ref, dwin_hbm, dwout_hbm,
                 back_hbm, ret_hbm, proj_hbm, prob_hbm, attt_hbm, normt_hbm,
                 token_st, grad_st, rows_v, grad_v, win_v, wout_v, icore_v, ipre_v, ichip_v, ocore_v, opre_v, ochip_v,
                 got_v, mixed_v, place_v, column_v, gain_v, count_v, small_v,
                 grad_sem, row_sem, back_sem, res_sem, win_sem, wout_sem, iscat_sem, oscat_sem, part_sem, join_sem, own_sem,
                 tiny_sem, local_sem, prob_sem):
    dp = lax.axis_index("dp")
    ex = lax.axis_index("expert")
    count, feat = tok_ref.shape
    shard = in_hbm.shape[0]
    hidden = win_v.shape[0]
    far = dp_size // 2
    slots = kinds * cap
    padded = token_st.shape[0]
    full, low = jnp.float32, jnp.bfloat16
    dma = pltpu.SemaphoreType.DMA
    half, wide, pairs, tiles = count // 2, feat // 2, feat // 128, hidden // 256

    barrier = pltpu.get_barrier_semaphore()
    for r in range(1, ex_size):
        pl.semaphore_signal(barrier, inc=1, device_id=(dp, ex ^ r), device_id_type=MESH)
    for k in range(1, dp_size):
        pl.semaphore_signal(barrier, inc=1, device_id=(dp ^ k, ex), device_id_type=MESH)

    def slot_rows(which):
        return pl.ds(pl.multiple_of(which * cap, 16), cap)

    def grad_copy(r):
        return remote(grad_st.at[slot_rows(2 + (ex ^ r))], grad_v.at[pl.ds(r * cap, cap)], grad_sem, (r,), (dp, ex ^ r))

    def row_copy(r):
        return remote(token_st.at[slot_rows(2 + (ex ^ r))], rows_v.at[pl.ds(r * cap, cap)], row_sem, (r,), (dp, ex ^ r))

    def result_copy(r):
        source, target = rows_v.at[pl.ds(r * cap, cap)], ret_hbm.at[slot_rows(2 + ex)]
        if r == 0:
            return pltpu.make_async_copy(source, target, local_sem.at[0])
        return remote(source, target, res_sem, (r,), (dp, ex ^ r))

    win = Gather(dp, ex, far, in_hbm, win_v, win_sem)
    wout = Gather(dp, ex, far, outw_hbm, wout_v, wout_sem)
    in_scatter = Scatter(dp, ex, far, win_v, icore_v, ipre_v, ichip_v, iscat_sem)
    out_scatter = Scatter(dp, ex, far, wout_v, ocore_v, opre_v, ochip_v, oscat_sem)

    def own_shards():
        return [pltpu.make_async_copy(outw_hbm, wout.at(dp), local_sem.at[1]),
                pltpu.make_async_copy(in_hbm, win.at(dp), local_sem.at[2])]

    def forward(wqkv_v, wo_v, norm_v, normt_v, proj_v, prob_v, attt_v, att_v, bias_v, sem):
        loads = [pltpu.make_async_copy(wqkv_hbm, wqkv_v, sem.at[0]), pltpu.make_async_copy(wo_hbm, wo_v, sem.at[1])]
        for copy in loads + own_shards():
            copy.start()

        kind = lax.broadcasted_iota(jnp.int32, (128, count), 0)
        first = chosen_ref[0:1, :]
        second = chosen_ref[1:2, :]
        hit_first = jnp.where(kind == first, 1.0, 0.0)
        hit_second = jnp.where(kind == second, 1.0, 0.0)
        hits = (hit_first + hit_second).astype(low)
        before = jnp.where(lax.broadcasted_iota(jnp.int32, (count, count), 0)
                           < lax.broadcasted_iota(jnp.int32, (count, count), 1), 1.0, 0.0).astype(low)
        ahead = dot_nn(hits, before)
        count_v[...] = dot_nt(jnp.ones((8, count), low), hits)
        place_v[0:1, :] = first.astype(full) * cap + jnp.sum(hit_first * ahead, axis=0, keepdims=True)
        place_v[1:2, :] = second.astype(full) * cap + jnp.sum(hit_second * ahead, axis=0, keepdims=True)

        def picks(which):
            slot = (which * cap + lax.broadcasted_iota(jnp.int32, (cap, count), 0)).astype(full)
            return slot == place_v[0:1, :], slot == place_v[1:2, :]

        def grad_rows(which):
            one, two = picks(which)
            gate = jnp.sum(jnp.where(one, gatest_ref[0:1, :], jnp.where(two, gatest_ref[1:2, :], 0.0)), axis=1,
                           keepdims=True)
            pick = jnp.where(one | two, 1.0, 0.0).astype(low)
            return (dot_nn(pick, cot_ref[...]) * gate).astype(low)

        pl.semaphore_wait(barrier, ex_size - 1 + dp_size - 1)
        wout.start()
        for r in reversed(range(ex_size)):
            if r:
                grad_st[slot_rows(2 + (ex ^ r)), :] = grad_rows(2 + (ex ^ r))
                grad_copy(r).start()
            else:
                grad_v[0:cap, :] = grad_rows(2 + ex)
        for which in range(2):
            grad_st[slot_rows(which), :] = grad_rows(which)
        if padded > slots:
            grad_st[slots:, :] = jnp.zeros((padded - slots, feat), low)
            token_st[slots:, :] = jnp.zeros((padded - slots, feat), low)

        spot = lax.broadcasted_iota(jnp.int32, (1, count), 1)
        document = jnp.zeros((1, count), full)
        end = lengths_s[0, 0]
        for j in range(1, lengths_s.shape[1] + 1):
            document = document + jnp.where(spot >= end, 1.0, 0.0)
            if j < lengths_s.shape[1]:
                end = end + lengths_s[0, j]
        place_v[2:3, :] = document
        place_v[3:4, :] = keep_ref[...].astype(full)
        place_v[4:8, :] = jnp.zeros((4, count), full)
        columns = place_v[...].T
        column_v[...] = columns

        def norm_rows(i, source, gain, target):
            at = pl.ds(pl.multiple_of(i * 64, 64), 64)
            whole = source[at, :].astype(full)
            centred = whole - jnp.mean(whole, axis=1, keepdims=True)
            scale = lax.rsqrt(jnp.mean(centred * centred, axis=1, keepdims=True) + 1e-05)
            target[at, :] = (centred * scale * gain).astype(low)
            return 0

        lax.fori_loop(0, count // 64, lambda i, _: norm_rows(i, tok_ref, gain1_ref[...][None], norm_v), 0)
        loads[0].wait()

        def project(n, _):
            at = pl.ds(pl.multiple_of(n * 256, 256), 256)
            proj_v[:, at] = dot_nn(norm_v[...], wqkv_v[:, at]).astype(low)
            return 0

        lax.fori_loop(0, 3 * feat // 256, project, 0)
        stores = [pltpu.make_async_copy(proj_v, proj_hbm, sem.at[2])]
        stores[-1].start()

        key = lax.broadcasted_iota(jnp.int32, (count, count), 0)
        query = lax.broadcasted_iota(jnp.int32, (count, count), 1)
        allowed = (columns[:, 2:3] == document) & (key <= query) & ((columns[:, 3:4] > 0.0) | (key == query))
        bias_v[...] = jnp.where(allowed, 0.0, -1e30)
        lower = lax.broadcasted_iota(jnp.int32, (count, 128), 1) < 64

        def head_pair(p, _):
            at = pl.multiple_of(p * 128, 128)
            q = proj_v[:, pl.ds(at, 128)]
            k = proj_v[:, pl.ds(pl.multiple_of(feat + p * 128, 128), 128)]
            vt = proj_v[:, pl.ds(pl.multiple_of(2 * feat + p * 128, 128), 128)].T
            for j in range(2):
                one = jnp.where(lower if j == 0 else jnp.logical_not(lower), k, jnp.zeros_like(k))
                for b in range(2):
                    reach, here = (b + 1) * half, slice(b * half, (b + 1) * half)
                    scores = dot_nt(one[0:reach], q[here]) * 0.125 + bias_v[0:reach, here]
                    powers = jnp.exp(scores - jnp.max(scores, axis=0, keepdims=True))
                    probs = (powers * (1.0 / jnp.sum(powers, axis=0, keepdims=True))).astype(low)
                    prob_v[2 * p + j, b * half:b * half + reach, :] = probs
                    attt_v[pl.ds(at + 64 * j, 64), here] = dot_nn(vt[64 * j:64 * j + 64, 0:reach], probs).astype(low)
            pltpu.make_async_copy(prob_v.at[pl.ds(2 * p, 2)], prob_hbm.at[pl.ds(2 * p, 2)], prob_sem.at[p]).start()
            return 0

        lax.fori_loop(0, pairs, head_pair, 0)
        win.start()
        stores.append(pltpu.make_async_copy(attt_v, attt_hbm, sem.at[3]))
        stores[-1].start()

        def turn(n, _):
            at = pl.ds(pl.multiple_of(n * 128, 128), 128)
            att_v[:, at] = attt_v[at, :].T
            return 0

        lax.fori_loop(0, pairs, turn, 0)
        loads[1].wait()

        def mix(n, _):
            at = pl.ds(pl.multiple_of(n * 256, 256), 256)
            mixed_v[:, at] = tok_ref[:, at].astype(full) + dot_nn(att_v[...], wo_v[:, at])
            return 0

        lax.fori_loop(0, feat // 256, mix, 0)
        lax.fori_loop(0, count // 64, lambda i, _: norm_rows(i, mixed_v, gain2_ref[...][None], att_v), 0)

        def token_rows(which):
            one, two = picks(which)
            return dot_nn(jnp.where(one | two, 1.0, 0.0).astype(low), att_v[...]).astype(low)

        for r in reversed(range(ex_size)):
            if r:
                token_st[slot_rows(2 + (ex ^ r)), :] = token_rows(2 + (ex ^ r))
                row_copy(r).start()
            else:
                rows_v[0:cap, :] = token_rows(2 + ex)
        for which in range(2):
            token_st[slot_rows(which), :] = token_rows(which)

        def turn_norm(n, _):
            at = pl.ds(pl.multiple_of(n * 128, 128), 128)
            normt_v[at, :] = norm_v[:, at].T
            return 0

        lax.fori_loop(0, pairs, turn_norm, 0)
        stores.append(pltpu.make_async_copy(normt_v, normt_hbm, sem.at[4]))
        stores[-1].start()
        for p in range(pairs):
            pltpu.make_async_copy(prob_v.at[pl.ds(2 * p, 2)], prob_hbm.at[pl.ds(2 * p, 2)], prob_sem.at[p]).wait()
        for copy in stores:
            copy.wait()

    heads = feat // 64
    pl.run_scoped(
        forward, pltpu.VMEM((feat, 3 * feat), low), pltpu.VMEM((feat, feat), low), pltpu.VMEM((count, feat), low),
        pltpu.VMEM((feat, count), low), pltpu.VMEM((count, 3 * feat), low), pltpu.VMEM((heads, count + half, half), low),
        pltpu.VMEM((feat, count), low), pltpu.VMEM((count, feat), low), pltpu.VMEM((count, count), full), dma((5,)))

    def expert(act_v, hg_v, fin_v, fout_v, facc_v, fst_v, rg_v, sem, load_sem):
        steps = fin_hbm.shape[0]
        per = steps // 2

        def frozen_load(i, slot):
            return (pltpu.make_async_copy(fin_hbm.at[i], fin_v.at[slot], load_sem.at[0, slot]),
                    pltpu.make_async_copy(fout_hbm.at[i], fout_v.at[slot], load_sem.at[1, slot]))

        def back_copy(r):
            source, target = rg_v.at[pl.ds(r * cap, cap)], back_hbm.at[slot_rows(2 + ex)]
            if r == 0:
                return pltpu.make_async_copy(source, target, sem.at[0])
            return remote(source, target, back_sem, (r,), (dp, ex ^ r))

        for copy in frozen_load(0, 0):
            copy.start()

        def frozen(i, _):
            slot = lax.rem(i, 2)
            for copy in frozen_load(i, slot):
                copy.wait()

            @pl.when(i + 1 < steps)
            def _():
                for copy in frozen_load(i + 1, 1 - slot):
                    copy.start()
            which = i // per
            up, down = fin_v[slot], fout_v[slot]
            active, slope = gelu_pair(dot_nt(token_st[slot_rows(which), :], up))
            slope_in = dot_nt(grad_st[slot_rows(which), :], down)
            result = dot_nn(active.astype(low), down)
            back = dot_nn((slope_in * slope).astype(low), up)
            fresh = lax.rem(i, per) == 0

            @pl.when(fresh)
            def _():
                facc_v[0, which] = result
                facc_v[1, which] = back

            @pl.when(jnp.logical_not(fresh))
            def _():
                facc_v[0, which] += result
                facc_v[1, which] += back
            return 0

        lax.fori_loop(0, steps, frozen, 0)
        stores = []
        for which in range(2):
            fst_v[0, pl.ds(which * cap, cap), :] = facc_v[0, which].astype(low)
            fst_v[1, pl.ds(which * cap, cap), :] = facc_v[1, which].astype(low)
        for n, target in enumerate((ret_hbm, back_hbm)):
            stores.append(pltpu.make_async_copy(fst_v.at[n], target.at[pl.ds(0, 2 * cap)], sem.at[1 + n]))
            stores[-1].start()
        wout.forward()
        for copy in own_shards():
            copy.wait()
        wout.finish()
        for r in range(1, ex_size):
            grad_copy(r).wait()

        def slope_tile(t, _):
            at = pl.ds(pl.multiple_of(t * 256, 256), 256)
            hg_v[:, at] = dot_nt(grad_v[...], wout_v[at, :]).astype(low)
            return 0

        lax.fori_loop(0, tiles, slope_tile, 0)
        win.forward()
        win.finish()
        order = list(reversed(range(ex_size)))
        for group in (order[:ex_size // 4], order[ex_size // 4:ex_size // 2], order[ex_size // 2:]):
            here = pl.ds(group[-1] * cap, len(group) * cap)
            for r in group:
                if r:
                    row_copy(r).wait_recv()

            def hidden_tile(t, _, here=here):
                at = pl.ds(pl.multiple_of(t * 256, 256), 256)
                active, slope = gelu_pair(dot_nt(rows_v[here, :], win_v[at, :]))
                act_v[here, at] = active.astype(low)
                hg_v[here, at] = (hg_v[here, at].astype(full) * slope).astype(low)
                return 0

            lax.fori_loop(0, tiles, hidden_tile, 0)

            def back_tile(n, _, here=here):
                at = pl.ds(pl.multiple_of(n * 256, 256), 256)
                rg_v[here, at] = dot_nn(hg_v[here, :], win_v[:, at]).astype(low)
                return 0

            lax.fori_loop(0, feat // 256, back_tile, 0)
            for r in group:
                back_copy(r).start()
        for r in range(1, ex_size):
            row_copy(r).wait_send()

        width = 256 if shard % 256 == 0 else 128

        def one_shard(which, units, rows, target):
            def tile(j, _):
                at = pl.ds(pl.multiple_of(which * shard + j * width, width), width)
                target[at, :] = dot_tn(units[:, at], rows[...]).astype(low)
                return 0

            lax.fori_loop(0, shard // width, tile, 0)

        def all_shards(scatter, units, rows):
            for k in range(1, far):
                one_shard(dp ^ (2 * k + 1), units, rows, scatter.source)
                scatter.core(k).start()
                one_shard(dp ^ (2 * k), units, rows, scatter.source)
            scatter.to_chips()
            one_shard(dp ^ 1, units, rows, scatter.source)
            scatter.core(0).start()
            one_shard(dp, units, rows, scatter.source)

        all_shards(in_scatter, hg_v, rows_v)

        def result_tile(n, _):
            at = pl.ds(pl.multiple_of(n * 256, 256), 256)
            rows_v[:, at] = dot_nn(act_v[...], wout_v[:, at]).astype(low)
            return 0

        lax.fori_loop(0, feat // 256, result_tile, 0)
        for r in reversed(range(ex_size)):
            result_copy(r).start()
        all_shards(out_scatter, act_v, grad_v)
        for copy in stores:
            copy.wait()
        for r in range(ex_size):
            back_copy(r).wait()

    span = fin_hbm.shape[1]
    rows_all = ex_size * cap
    pl.run_scoped(
        expert, pltpu.VMEM((rows_all, hidden), low), pltpu.VMEM((rows_all, hidden), low), pltpu.VMEM((2, span, feat), low),
        pltpu.VMEM((2, span, feat), low), pltpu.VMEM((2, 2, cap, feat), full), pltpu.VMEM((2, 2 * cap, feat), low),
        pltpu.VMEM((rows_all, feat), low), dma((3,)), dma((2, 2)))

    back_v, ret_v, branch_v, da_v = grad_st, token_st, grad_v.at[pl.ds(0, count)], grad_v.at[pl.ds(count, count)]

    def backward(prob_v, proj_v, turned_v, wo_v, pg_v, blocks_v, acc_v, g_v, mg_v, pick_v, dqt_v, sem):
        loads = [pltpu.make_async_copy(source, target, sem.at[i]) for i, (source, target) in enumerate([
            (back_hbm, back_v.at[pl.ds(0, slots)]), (attt_hbm, turned_v), (wo_hbm, wo_v), (prob_hbm, prob_v),
            (proj_hbm, proj_v)])]
        for copy in loads:
            copy.start()
        sums = Sums(sum_chunks(dp_size, ex_size, blocks_v.shape[0]), blocks_v, acc_v, got_v, total_hbm, part_sem, join_sem,
                    own_sem)

        def place_tile(n):
            at = pl.ds(pl.multiple_of(n * 128, 128), 128)
            slot = (n * 128 + lax.broadcasted_iota(jnp.int32, (count, 128), 1)).astype(full)
            return at, slot == column_v[:, 0:1], slot == column_v[:, 1:2]

        def pick_both(n, _):
            at, one, two = place_tile(n)
            pick_v[:, at] = jnp.where(one | two, 1.0, 0.0).astype(low)
            return 0

        lax.fori_loop(0, padded // 128, pick_both, 0)
        loads[0].wait()

        def collect(n, _):
            at = pl.ds(pl.multiple_of(n * 256, 256), 256)
            g_v[:, at] = dot_nn(pick_v[...], back_v[:, at])
            return 0

        lax.fori_loop(0, feat // 256, collect, 0)
        gain_v[...] = jnp.zeros_like(gain_v)
        gain_v[16:24, 0:128] = count_v[...]

        def norm_back(i, whole, gain, target):
            at = pl.ds(pl.multiple_of(i * 64, 64), 64)
            centred = whole - jnp.mean(whole, axis=1, keepdims=True)
            scale = lax.rsqrt(jnp.mean(centred * centred, axis=1, keepdims=True) + 1e-05)
            unit = centred * scale
            grad = g_v[at, :]
            weighted = grad * unit
            gain_v[target:target + 8, :] += jnp.sum(weighted.reshape(8, 8, feat), axis=0)
            scaled = grad * gain
            return at, scale * (scaled - jnp.mean(scaled, axis=1, keepdims=True)
                                - unit * jnp.mean(scaled * unit, axis=1, keepdims=True))

        def second_norm(i, _):
            at, part = norm_back(i, mixed_v[pl.ds(pl.multiple_of(i * 64, 64), 64), :], gain2_ref[...][None], 8)
            grad = cot_ref[at, :].astype(full) + part
            mg_v[at, :] = grad
            branch_v[at, :] = grad.astype(low)
            return 0

        lax.fori_loop(0, count // 64, second_norm, 0)
        loads[1].wait()

        def out_weight(b, _):
            at = pl.ds(pl.multiple_of(b * wide, 128), wide)
            blocks_v[pl.ds(pl.multiple_of(b * feat, 16), feat), :] = dot_nn(turned_v[...], branch_v[:, at]).astype(low)
            return 0

        lax.fori_loop(0, 2, out_weight, 0)
        loads.append(pltpu.make_async_copy(normt_hbm, turned_v, sem.at[5]))
        loads[5].start()
        sums.start(0)
        loads[2].wait()

        def attended_grad(n, _):
            at = pl.ds(pl.multiple_of(n * 256, 256), 256)
            da_v[:, at] = dot_nt(branch_v[...], wo_v[at, :]).astype(low)
            return 0

        lax.fori_loop(0, feat // 256, attended_grad, 0)
        loads[3].wait()
        loads[4].wait()
        lower = lax.broadcasted_iota(jnp.int32, (count, 128), 1) < 64

        def head_pair(p, _):
            at_q = pl.ds(pl.multiple_of(p * 128, 128), 128)
            at_k = pl.ds(pl.multiple_of(feat + p * 128, 128), 128)
            at_v = pl.ds(pl.multiple_of(2 * feat + p * 128, 128), 128)
            q, k, v, da = proj_v[:, at_q], proj_v[:, at_k], proj_v[:, at_v], da_v[:, at_q]
            kt = k.T
            key_near = key_far = value_near = value_far = 0.0
            for j in range(2):
                mask = lower if j == 0 else jnp.logical_not(lower)
                qj, vj, daj = [jnp.where(mask, w, jnp.zeros_like(w)) for w in (q, v, da)]
                for b in range(2):
                    reach, here = (b + 1) * half, slice(b * half, (b + 1) * half)
                    prob = prob_v[2 * p + j, b * half:b * half + reach, :]
                    whole = prob.astype(full)
                    grad = dot_nt(vj[0:reach], da[here])
                    score = (whole * (grad - jnp.sum(whole * grad, axis=0, keepdims=True))).astype(low)
                    dqt_v[64 * j:64 * j + 64, here] = dot_nn(kt[64 * j:64 * j + 64, 0:reach], score)
                    key_near += dot_nn(score[0:half], qj[here])
                    value_near += dot_nn(prob[0:half], daj[here])
                    if b:
                        key_far += dot_nn(score[half:], qj[here])
                        value_far += dot_nn(prob[half:], daj[here])
            pg_v[:, at_q] = (dqt_v[...].T * 0.125).astype(low)
            pg_v[0:half, at_k] = (key_near * 0.125).astype(low)
            pg_v[half:, at_k] = (key_far * 0.125).astype(low)
            pg_v[0:half, at_v] = value_near.astype(low)
            pg_v[half:, at_v] = value_far.astype(low)
            return 0

        for part in range(2):
            lax.fori_loop(part * pairs // 2, (part + 1) * pairs // 2, head_pair, 0)
            if part == 0:
                loads[5].wait()
                in_scatter.finish()
                ends = [pltpu.make_async_copy(icore_v.at[0], dwin_hbm, sem.at[7])]
                ends[-1].start()
                weights = [pltpu.make_async_copy(wqkv_hbm.at[:, pl.ds(c * feat, feat)], win_v.at[pl.ds(c * feat, feat)],
                                                 sem.at[10 + c]) for c in range(3)]
                for copy in weights:
                    copy.start()
            sums.tick()

            def weight_block(c, _, part=part):
                at = pl.ds(pl.multiple_of(c * feat + part * wide, 128), wide)
                into = pl.ds(pl.multiple_of(2 * feat + (3 * part + c) * feat, 16), feat)
                blocks_v[into, :] = dot_nn(turned_v[...], pg_v[:, at]).astype(low)
                return 0

            lax.fori_loop(0, 3, weight_block, 0)
            sums.start(1 + part)
        for copy in weights:
            copy.wait()

        def norm_grad(n, _):
            at = pl.ds(pl.multiple_of(n * 256, 256), 256)
            g_v[:, at] = sum(dot_nt(pg_v[:, c * feat:(c + 1) * feat],
                                    win_v[pl.ds(pl.multiple_of(c * feat + n * 256, 256), 256), :]) for c in range(3))
            return 0

        lax.fori_loop(0, feat // 256, norm_grad, 0)
        sums.tick()

        def first_norm(i, _):
            here = pl.ds(pl.multiple_of(i * 64, 64), 64)
            at, part = norm_back(i, tok_ref[here, :].astype(full), gain1_ref[...][None], 0)
            dtok_ref[at, :] = (mg_v[at, :] + part).astype(low)
            return 0

        lax.fori_loop(0, count // 64, first_norm, 0)

        order = sums.chunks[0][2]
        stages = len(order)
        slot_of = [stages + sum((1 << len(stage)) - 1 for stage in order[:i]) for i in range(stages)]
        for i in range(3):
            small_v[0, i:i + 1, :] = jnp.sum(gain_v[8 * i:8 * i + 8, :], axis=0, keepdims=True)
        small_v[0, 2:3, :] = gain_v[16:17, :]
        small_v[0, 3:8, :] = jnp.zeros((5, feat), full)

        def small_send(i):
            copies = []
            for m, peer in enumerate(group_of(order[i])[1], 1):
                copies.append(remote(small_v.at[i], small_v.at[slot_of[i] + m - 1], tiny_sem, (i, m), peer))
                copies[-1].start()
            return copies

        def small_add(i, copies):
            for copy in copies:
                copy.wait()
            mine, peers = group_of(order[i])
            total = jnp.zeros_like(sum_ref[...])
            for n in range(len(peers) + 1):
                term = small_v[i]
                for m in range(1, len(peers) + 1):
                    term = jnp.where(mine == n ^ m, small_v[slot_of[i] + m - 1], term)
                total = total + term
            if i + 1 < stages:
                small_v[i + 1] = total
                return small_send(i + 1)
            sum_ref[...] = total

        tiny = small_send(0)
        sums.tick()
        sums.tick()
        tiny = small_add(0, tiny)
        sums.tick()
        tiny = small_add(1, tiny)
        out_scatter.finish()
        ends.append(pltpu.make_async_copy(ocore_v.at[0], dwout_hbm, sem.at[8]))
        ends[-1].start()
        for r in range(ex_size):
            result_copy(r).wait()
        load = pltpu.make_async_copy(ret_hbm, ret_v.at[pl.ds(0, slots)], sem.at[9])
        load.start()
        sums.tick()
        tiny = small_add(2, tiny)
        load.wait()
        for turn in range(2):
            def pick_one(n, _, turn=turn):
                at, one, two = place_tile(n)
                pick_v[:, at] = jnp.where((one, two)[turn], 1.0, 0.0).astype(low)
                return 0

            lax.fori_loop(0, padded // 128, pick_one, 0)

            def deliver(n, _, turn=turn):
                at = pl.ds(pl.multiple_of(n * 256, 256), 256)
                term = dot_nn(pick_v[...], ret_v[:, at]) * gates_ref[:, turn:turn + 1]
                if turn == 0:
                    g_v[:, at] = term
                else:
                    out_ref[:, at] = (mixed_v[:, at] + (g_v[:, at] + term)).astype(low)
                return 0

            lax.fori_loop(0, feat // 256, deliver, 0)
            if turn == 0:
                sums.tick()
                small_add(3, tiny)
        sums.finish()
        for copy in ends:
            copy.wait()

    rows, steps = 8 * feat, 13
    pl.run_scoped(
        backward, pltpu.VMEM((heads, count + half, half), low), pltpu.VMEM((count, 3 * feat), low),
        pltpu.VMEM((feat, count), low), pltpu.VMEM((feat, feat), low), pltpu.VMEM((count, 3 * feat), low),
        pltpu.VMEM((rows, wide), low),
        pltpu.VMEM((rows // 2, wide), low), pltpu.VMEM((count, feat), full), pltpu.VMEM((count, feat), full),
        pltpu.VMEM((count, padded), low), pltpu.VMEM((128, count), full), dma((steps,)))


def layer(tokens, cotangent, chosen, gates, lengths, keep, gain1, gain2, wqkv, wo, in_shard, out_shard, fin, fout, kinds, cap,
          dp_size, ex_size):
    count, feat = tokens.shape
    shard = in_shard.shape[0]
    hidden = dp_size * shard
    far, slots = dp_size // 2, kinds * cap
    padded = (slots + 127) // 128 * 128
    heads, half = feat // 64, count // 2
    rows, wide = 8 * feat, feat // 2
    span = 768 if ex_size * cap <= 1024 else 384
    steps = 2 * hidden // span
    chunks, stages = len(sum_chunks(dp_size, ex_size, rows)), 4
    anyspace, vmem = pl.BlockSpec(memory_space=pl.ANY), pl.BlockSpec(memory_space=pltpu.VMEM)
    dma, shape, buffer = pltpu.SemaphoreType.DMA, jax.ShapeDtypeStruct, pltpu.VMEM
    full, low = jnp.float32, jnp.bfloat16
    scatter = [buffer((far, shard, feat), low), buffer((far - 1, shard, feat), low), buffer((far - 1, shard, feat), low)]
    return pl.pallas_call(
        functools.partial(layer_kernel, dp_size, ex_size, kinds, cap),
        out_shape=(shape((count, feat), low), shape((count, feat), low), shape((rows, wide), low), shape((8, feat), full),
                   shape((shard, feat), low), shape((shard, feat), low),
                   shape((slots, feat), low), shape((slots, feat), low), shape((count, 3 * feat), low),
                   shape((heads, count + half, half), low), shape((feat, count), low), shape((feat, count), low)),
        in_specs=[pl.BlockSpec(memory_space=pltpu.SMEM)] + [vmem] * 8 + [anyspace] * 6,
        out_specs=(vmem, vmem, anyspace, vmem) + (anyspace,) * 8,
        scratch_shapes=[
            buffer((padded, feat), low), buffer((padded, feat), low),
            buffer((ex_size * cap, feat), low), buffer((ex_size * cap, feat), low),
            buffer((hidden, feat), low), buffer((hidden, feat), low)] + scatter + scatter + [
            buffer((rows, wide), low), buffer((count, feat), full), buffer((8, count), full), buffer((count, 8), full),
            buffer((24, feat), full), buffer((8, 128), full), buffer((4 * stages, 8, feat), full),
            dma((2, ex_size)), dma((2, ex_size)), dma((2, ex_size)), dma((2, ex_size)),
            dma((2, 2, far)), dma((2, 2, far)), dma((2, 2, far)), dma((2, 2, far)),
            dma((2, chunks, stages, 4)), dma((2, chunks, stages, 4)), dma((chunks,)),
            dma((2, stages, 4)), dma((3,)), dma((feat // 128,)),
        ],
        compiler_params=pltpu.CompilerParams(collective_id=0, has_side_effects=True, vmem_limit_bytes=63 << 20),
        name="layer",
    )(lengths, chosen.T, gates.T, keep[None], gates, tokens, cotangent, gain1, gain2, wqkv, wo, in_shard, out_shard,
      fin.reshape(steps, span, feat), fout.reshape(steps, span, feat))


def finish_kernel(kinds, total_hbm, small_ref, out_in, dtok_in, dwin_in, dwout_in,
                  out_ref, dtok_ref, gain1_ref, qkv_hbm, wide_hbm, gain2_ref, dwin_ref, dwout_ref, count_ref,
                  block_v, whole_v, load_sem, store_sem):
    feat = small_ref.shape[1]
    wide = feat // 2
    loads = [pltpu.make_async_copy(total_hbm.at[pl.ds(b * feat, feat)], block_v.at[b], load_sem.at[b]) for b in range(8)]
    for copy in loads:
        copy.start()
    out_ref[...] = out_in[...]
    dtok_ref[...] = dtok_in[...]
    stores = []
    for b in range(8):
        loads[b].wait()

        def widen(j, _):
            at = pl.ds(pl.multiple_of(j * 64, 64), 64)
            whole_v[b, at, :] = block_v[b, at, :].astype(jnp.float32)
            return 0

        lax.fori_loop(0, feat // 64, widen, 0)
        part, c = (b - 2) // 3, (b - 2) % 3
        target = wide_hbm.at[:, pl.ds(b * wide, wide)] if b < 2 else qkv_hbm.at[:, pl.ds(c * feat + part * wide, wide)]
        stores.append(pltpu.make_async_copy(whole_v.at[b], target, store_sem.at[b]))
        stores[-1].start()
    for source, target in ((dwin_in, dwin_ref), (dwout_in, dwout_ref)):
        def widen(j, _):
            at = pl.ds(pl.multiple_of(j * 64, 64), 64)
            target[at, :] = source[at, :].astype(jnp.float32)
            return 0

        lax.fori_loop(0, source.shape[0] // 64, widen, 0)
    gain1_ref[...] = small_ref[0, :]
    gain2_ref[...] = small_ref[1, :]
    count_ref[...] = small_ref[2, 0:128]
    for copy in stores:
        copy.wait()


def finish(total, small, out, dtok, dwin, dwout, kinds):
    rows, wide = total.shape
    feat = 2 * wide
    anyspace, vmem = pl.BlockSpec(memory_space=pl.ANY), pl.BlockSpec(memory_space=pltpu.VMEM)
    shape, full, low = jax.ShapeDtypeStruct, jnp.float32, jnp.bfloat16
    return pl.pallas_call(
        functools.partial(finish_kernel, kinds),
        out_shape=(shape(out.shape, low), shape(dtok.shape, low), shape((feat,), full), shape((feat, 3 * feat), full),
                   shape((feat, feat), full), shape((feat,), full), shape(dwin.shape, full), shape(dwout.shape, full),
                   shape((128,), full)),
        in_specs=[anyspace] + [vmem] * 5,
        out_specs=(vmem, vmem, vmem, anyspace, anyspace, vmem, vmem, vmem, vmem),
        scratch_shapes=[pltpu.VMEM((8, feat, wide), low), pltpu.VMEM((8, feat, wide), full),
                        pltpu.SemaphoreType.DMA((8,)), pltpu.SemaphoreType.DMA((8,))],
        compiler_params=pltpu.CompilerParams(vmem_limit_bytes=48 << 20),
        name="finish",
    )(total, small, out, dtok, dwin, dwout)


FROZEN = 2


def body(
    tokens,
    cotangent,
    chosen,
    gates,
    lengths,
    keep_mask,
    gain1,
    w_qkv,
    w_o,
    gain2,
    frozen_in,
    frozen_out,
    w_in,
    w_out,
):
    row_count, feat_width = tokens.shape
    owners = lax.axis_size("expert")
    dp_size = lax.axis_size("dp")
    kind_count = FROZEN + owners
    slot_count = ((2 * row_count * 5 // (4 * kind_count) + 7) // 8 * 8 + 15) // 16 * 16
    output, tokens_grad, total, small_sum, d_w_in, d_w_out = layer(
        tokens, cotangent, chosen, gates, lengths, keep_mask, gain1, gain2, w_qkv, w_o, w_in[0], w_out[0], frozen_in,
        frozen_out, kind_count, slot_count, dp_size, owners)[:6]
    output, tokens_grad, gain1_sum, w_qkv_sum, w_o_sum, gain2_sum, d_w_in, d_w_out, counts = finish(
        total, small_sum, output, tokens_grad, d_w_in, d_w_out, kind_count)
    return (
        output,
        tokens_grad,
        gain1_sum,
        w_qkv_sum,
        w_o_sum,
        gain2_sum,
        d_w_in[None],
        d_w_out[None],
        counts[:kind_count],
    )


def solution(mesh):
    placed = (
        P(("dp", "expert"), None),
        P(("dp", "expert"), None),
        P(("dp", "expert"), None),
        P(("dp", "expert"), None),
        P(("dp", "expert"), None),
        P(("dp", "expert")),
        P(),
        P(),
        P(),
        P(),
        P(),
        P(),
        P("expert", "dp", None),
        P("expert", "dp", None),
    )
    return jax.shard_map(
        body,
        mesh=mesh,
        in_specs=placed,
        out_specs=(
            P(("dp", "expert"), None),
            P(("dp", "expert"), None),
            P(),
            P(),
            P(),
            P(),
            P("expert", "dp", None),
            P("expert", "dp", None),
            P(),
        ),
        check_vma=False,
    )
```

```python
import functools
import jax
import jax.numpy as jnp
from jax import lax
from jax.experimental import pallas as pl
from jax.experimental.pallas import tpu as pltpu
from jax.sharding import PartitionSpec as P

MESH = pl.DeviceIdType.MESH


def butterfly(dp_size, ex_size):
    core = ("dp", 1)
    xs = [("dp", 2 << k) for k in range((dp_size // 2).bit_length() - 1)]
    depth = 4 if ex_size % 4 == 0 else 1
    wide = ex_size // depth
    ys = [("expert", 1 << k) for k in range(wide.bit_length() - 1)]
    zs = [("expert", wide << k) for k in range(depth.bit_length() - 1)]
    return core, xs, ys, zs


def group_of(stage):
    place = {"dp": lax.axis_index("dp"), "expert": lax.axis_index("expert")}
    mine = sum(lax.rem(place[axis] // mask, 2) << j for j, (axis, mask) in enumerate(stage))
    peers = []
    for m in range(1, 1 << len(stage)):
        peer = dict(place)
        for j, (axis, mask) in enumerate(stage):
            if m >> j & 1:
                peer[axis] = peer[axis] ^ mask
        peers.append((peer["dp"], peer["expert"]))
    return mine, peers


def dot_nn(a, b):
    return jnp.dot(a, b, preferred_element_type=jnp.float32)


def dot_nt(a, b):
    return lax.dot_general(a, b, (((1,), (1,)), ((), ())), preferred_element_type=jnp.float32)


def dot_tn(a, b):
    return lax.dot_general(a, b, (((0,), (0,)), ((), ())), preferred_element_type=jnp.float32)


GELU_A = 0.7978845608028654
GELU_B = GELU_A * 0.044715


def gelu_pair(h):
    square = h * h
    bend = jnp.tanh(h * (GELU_B * square + GELU_A))
    share = 0.5 * bend + 0.5
    slope = share + (0.5 * h) * (1.0 - bend * bend) * ((3.0 * GELU_B) * square + GELU_A)
    return h * share, slope


def remote(source, target, pair, at, device):
    return pltpu.make_async_remote_copy(
        src_ref=source, dst_ref=target, send_sem=pair.at[(0,) + at], recv_sem=pair.at[(1,) + at], device_id=device,
        device_id_type=MESH)


class Gather:

    def __init__(self, dp, ex, far, source, whole, sems):
        self.dp, self.ex, self.far, self.source, self.whole, self.sems = dp, ex, far, source, whole, sems
        self.rows = source.shape[0]

    def at(self, which):
        return self.whole.at[pl.ds(pl.multiple_of(which * self.rows, 16), self.rows)]

    def first(self, k):
        return remote(self.source, self.at(self.dp), self.sems, (0, k), (self.dp ^ (2 * k if k else 1), self.ex))

    def second(self, k):
        theirs = self.at(self.dp ^ (2 * k))
        return remote(theirs, theirs, self.sems, (1, k), (self.dp ^ 1, self.ex))

    def start(self):
        for k in list(range(1, self.far)) + [0]:
            self.first(k).start()

    def forward(self):
        for k in range(1, self.far):
            self.first(k).wait_recv()
            self.second(k).start()

    def finish(self):
        self.first(0).wait()
        for k in range(1, self.far):
            self.first(k).wait_send()
            self.second(k).wait()


class Scatter:

    def __init__(self, dp, ex, far, source, core_v, pre_v, chip_v, sems):
        self.dp, self.ex, self.far, self.source = dp, ex, far, source
        self.core_v, self.pre_v, self.chip_v, self.sems = core_v, pre_v, chip_v, sems
        self.rows = core_v.shape[1]

    def at(self, which):
        return self.source.at[pl.ds(pl.multiple_of(which * self.rows, 16), self.rows)]

    def core(self, k):
        return remote(self.at(self.dp ^ (2 * k + 1)), self.core_v.at[k], self.sems, (0, k), (self.dp ^ 1, self.ex))

    def chip(self, k):
        return remote(self.pre_v.at[k - 1], self.chip_v.at[k - 1], self.sems, (1, k), (self.dp ^ (2 * k), self.ex))

    def to_chips(self):
        for k in range(1, self.far):
            self.core(k).wait_recv()
            source = self.at(self.dp ^ (2 * k))

            def add(j, _):
                at = pl.ds(pl.multiple_of(j * 128, 128), 128)
                total = source[at, :].astype(jnp.float32) + self.core_v[k, at, :].astype(jnp.float32)
                self.pre_v[k - 1, at, :] = total.astype(jnp.bfloat16)
                return 0

            lax.fori_loop(0, self.rows // 128, add, 0)
            self.chip(k).start()

    def finish(self):
        self.core(0).wait_recv()
        for k in range(1, self.far):
            self.chip(k).wait_recv()
        source = self.at(self.dp)

        def add(j, _):
            at = pl.ds(pl.multiple_of(j * 128, 128), 128)
            total = source[at, :].astype(jnp.float32) + self.core_v[0, at, :].astype(jnp.float32)
            for k in range(1, self.far):
                total = total + self.chip_v[k - 1, at, :].astype(jnp.float32)
            self.core_v[0, at, :] = total.astype(jnp.bfloat16)
            return 0

        lax.fori_loop(0, self.rows // 128, add, 0)
        for k in range(self.far):
            self.core(k).wait_send()
            if k:
                self.chip(k).wait_send()


class Sums:

    def __init__(self, chunks, blocks, acc, got, out, scatter_sems, gather_sems, own_sems):
        self.chunks, self.blocks, self.acc, self.got, self.out = chunks, blocks, acc, got, out
        self.scatter_sems, self.gather_sems, self.own_sems = scatter_sems, gather_sems, own_sems
        self.offs = [[base] for base, _, _, _ in chunks]
        self.lens = [[rows] for _, rows, _, _ in chunks]
        self.land = [[base] for base, _, _, _ in chunks]
        self.copies = [None] * len(chunks)
        self.shift = [0] * len(chunks)
        self.stage = [0] * len(chunks)
        self.own = [None] * len(chunks)

    def scatter(self, c, i):
        base, _, order, _ = self.chunks[c]
        mine, peers = group_of(order[i])
        part = self.lens[c][i] >> len(order[i])
        source = self.acc if i else self.blocks
        self.copies[c] = []
        for m, peer in enumerate(peers, 1):
            give = pl.multiple_of(self.offs[c][i] + (mine ^ m) * part + self.shift[c], 16)
            self.copies[c].append(remote(
                source.at[pl.ds(give, part)], self.got.at[pl.ds(self.land[c][i] + (m - 1) * part, part)],
                self.scatter_sems, (c, i, m), peer))
            self.copies[c][-1].start()
        self.offs[c].append(self.offs[c][i] + mine * part)
        self.lens[c].append(part)
        self.land[c].append(self.land[c][i] + len(peers) * part)

    def gather(self, c, i):
        stages = len(self.chunks[c][2])
        _, peers = group_of(self.chunks[c][2][i])
        part = self.lens[c][i + 1]
        target = self.out.at[pl.ds(pl.multiple_of(self.offs[c][i + 1], 16), part)]
        source = target
        if i + 1 == stages:
            source = self.acc.at[pl.ds(pl.multiple_of(self.offs[c][i + 1] + self.shift[c], 16), part)]
            self.own[c] = pltpu.make_async_copy(source, target, self.own_sems.at[c])
            self.own[c].start()
        self.copies[c] = []
        for m, peer in enumerate(peers, 1):
            self.copies[c].append(remote(source, target, self.gather_sems, (c, i, m), peer))
            self.copies[c][-1].start()

    def start(self, phase):
        for c, chunk in enumerate(self.chunks):
            if chunk[3] == phase:
                self.scatter(c, 0)

    def advance(self, c):
        if not self.copies[c]:
            return
        base, _, order, _ = self.chunks[c]
        stages, s = len(order), self.stage[c]
        for copy in self.copies[c]:
            copy.wait()
        self.stage[c] += 1
        if s >= stages:
            i = 2 * stages - 1 - s
            self.copies[c] = None
            if s == stages:
                self.own[c].wait()
            if i > 0:
                self.gather(c, i - 1)
            return
        part = self.lens[c][s + 1]
        source = self.acc if s else self.blocks
        keep, begin = self.offs[c][s + 1], self.land[c][s]
        count = (1 << len(order[s])) - 1
        tile = part
        while tile > 128 or part % tile or tile % 16:
            tile -= 16
        move_in = self.shift[c]
        if s == 0:
            self.shift[c] = base // 2 - keep
        move_out = self.shift[c]

        def add(j, _):
            at = pl.ds(pl.multiple_of(keep + move_out + j * tile, 16), tile)
            come = pl.ds(pl.multiple_of(keep + move_in + j * tile, 16), tile)
            total = source[come, :].astype(jnp.float32)
            for m in range(count):
                other = pl.ds(pl.multiple_of(begin + m * part + j * tile, 16), tile)
                total = total + self.got[other, :].astype(jnp.float32)
            self.acc[at, :] = total.astype(jnp.bfloat16)
            return 0

        lax.fori_loop(0, part // tile, add, 0)
        if s + 1 < stages:
            self.scatter(c, s + 1)
        else:
            self.gather(c, s)

    def tick(self):
        for c in reversed(range(len(self.chunks))):
            self.advance(c)

    def finish(self):
        while any(self.copies):
            for c in range(len(self.chunks)):
                self.advance(c)


def sum_chunks(dp_size, ex_size, rows):
    core, xs, ys, zs = butterfly(dp_size, ex_size)
    yxz, xyz, zyx = [[core], ys, xs, zs], [[core], xs, ys, zs], [[core], zs, ys, xs]
    if dp_size * ex_size * 16 <= 512:
        yq, xq, zq = [[core], ys, xs + zs[:1], zs[1:]], [[core], xs, ys + zs[:1], zs[1:]], [[core], zs[:1], ys + xs, zs[1:]]
        return [(0, 1536, yq, 0), (1536, 1024, xq, 1), (2560, 1024, yq, 1), (3584, 1024, yq, 2), (4608, 1024, xq, 2), (5632, 512, zq, 2)]
    third = rows // 3
    return [(0, third, yxz, 2), (third, third, xyz, 2), (2 * third, third, zyx, 2)]


def layer_kernel(dp_size, ex_size, kinds, cap,
                 lengths_s, chosen_ref, gatest_ref, keep_ref, tok_ref, cot_ref, gain1_ref, gain2_ref,
                 wqkv_hbm, wo_hbm, in_hbm, outw_hbm, fin_hbm, fout_hbm,
                 out_ref, dtok_ref, total_hbm, sum_ref, dwin_hbm, dwout_hbm,
                 back_hbm, ret_hbm, proj_hbm, prob_hbm, attt_hbm, normt_hbm,
                 token_st, grad_st, rows_v, grad_v, win_v, wout_v, icore_v, ipre_v, ichip_v, ocore_v, opre_v, ochip_v,
                 got_v, mixed_v, place_v, column_v, gain_v, count_v, small_v,
                 grad_sem, row_sem, back_sem, res_sem, win_sem, wout_sem, iscat_sem, oscat_sem, part_sem, join_sem, own_sem,
                 tiny_sem, local_sem, prob_sem):
    dp = lax.axis_index("dp")
    ex = lax.axis_index("expert")
    count, feat = tok_ref.shape
    shard = in_hbm.shape[0]
    hidden = win_v.shape[0]
    far = dp_size // 2
    slots = kinds * cap
    padded = token_st.shape[0]
    full, low = jnp.float32, jnp.bfloat16
    dma = pltpu.SemaphoreType.DMA
    half, wide, pairs, tiles = count // 2, feat // 2, feat // 128, hidden // 256

    barrier = pltpu.get_barrier_semaphore()
    for r in range(1, ex_size):
        pl.semaphore_signal(barrier, inc=1, device_id=(dp, ex ^ r), device_id_type=MESH)
    for k in range(1, dp_size):
        pl.semaphore_signal(barrier, inc=1, device_id=(dp ^ k, ex), device_id_type=MESH)

    def slot_rows(which):
        return pl.ds(pl.multiple_of(which * cap, 16), cap)

    def grad_copy(r):
        return remote(grad_st.at[slot_rows(2 + (ex ^ r))], grad_v.at[pl.ds(r * cap, cap)], grad_sem, (r,), (dp, ex ^ r))

    def row_copy(r):
        return remote(token_st.at[slot_rows(2 + (ex ^ r))], rows_v.at[pl.ds(r * cap, cap)], row_sem, (r,), (dp, ex ^ r))

    def result_copy(r):
        source, target = rows_v.at[pl.ds(r * cap, cap)], ret_hbm.at[slot_rows(2 + ex)]
        if r == 0:
            return pltpu.make_async_copy(source, target, local_sem.at[0])
        return remote(source, target, res_sem, (r,), (dp, ex ^ r))

    win = Gather(dp, ex, far, in_hbm, win_v, win_sem)
    wout = Gather(dp, ex, far, outw_hbm, wout_v, wout_sem)
    in_scatter = Scatter(dp, ex, far, win_v, icore_v, ipre_v, ichip_v, iscat_sem)
    out_scatter = Scatter(dp, ex, far, wout_v, ocore_v, opre_v, ochip_v, oscat_sem)

    def own_shards():
        return [pltpu.make_async_copy(outw_hbm, wout.at(dp), local_sem.at[1]),
                pltpu.make_async_copy(in_hbm, win.at(dp), local_sem.at[2])]

    def forward(wqkv_v, wo_v, norm_v, normt_v, proj_v, prob_v, attt_v, att_v, bias_v, sem):
        loads = [pltpu.make_async_copy(wqkv_hbm, wqkv_v, sem.at[0]), pltpu.make_async_copy(wo_hbm, wo_v, sem.at[1])]
        for copy in loads + own_shards():
            copy.start()

        kind = lax.broadcasted_iota(jnp.int32, (128, count), 0)
        first = chosen_ref[0:1, :]
        second = chosen_ref[1:2, :]
        hit_first = jnp.where(kind == first, 1.0, 0.0)
        hit_second = jnp.where(kind == second, 1.0, 0.0)
        hits = (hit_first + hit_second).astype(low)
        before = jnp.where(lax.broadcasted_iota(jnp.int32, (count, count), 0)
                           < lax.broadcasted_iota(jnp.int32, (count, count), 1), 1.0, 0.0).astype(low)
        ahead = dot_nn(hits, before)
        count_v[...] = dot_nt(jnp.ones((8, count), low), hits)
        place_v[0:1, :] = first.astype(full) * cap + jnp.sum(hit_first * ahead, axis=0, keepdims=True)
        place_v[1:2, :] = second.astype(full) * cap + jnp.sum(hit_second * ahead, axis=0, keepdims=True)

        def picks(which):
            slot = (which * cap + lax.broadcasted_iota(jnp.int32, (cap, count), 0)).astype(full)
            return slot == place_v[0:1, :], slot == place_v[1:2, :]

        def grad_rows(which):
            one, two = picks(which)
            gate = jnp.sum(jnp.where(one, gatest_ref[0:1, :], jnp.where(two, gatest_ref[1:2, :], 0.0)), axis=1,
                           keepdims=True)
            pick = jnp.where(one | two, 1.0, 0.0).astype(low)
            return (dot_nn(pick, cot_ref[...]) * gate).astype(low)

        pl.semaphore_wait(barrier, ex_size - 1 + dp_size - 1)
        wout.start()
        for r in reversed(range(ex_size)):
            if r:
                grad_st[slot_rows(2 + (ex ^ r)), :] = grad_rows(2 + (ex ^ r))
                grad_copy(r).start()
            else:
                grad_v[0:cap, :] = grad_rows(2 + ex)
        for which in range(2):
            grad_st[slot_rows(which), :] = grad_rows(which)
        if padded > slots:
            grad_st[slots:, :] = jnp.zeros((padded - slots, feat), low)
            token_st[slots:, :] = jnp.zeros((padded - slots, feat), low)

        spot = lax.broadcasted_iota(jnp.int32, (1, count), 1)
        document = jnp.zeros((1, count), full)
        end = lengths_s[0, 0]
        for j in range(1, lengths_s.shape[1] + 1):
            document = document + jnp.where(spot >= end, 1.0, 0.0)
            if j < lengths_s.shape[1]:
                end = end + lengths_s[0, j]
        place_v[2:3, :] = document
        place_v[3:4, :] = keep_ref[...].astype(full)
        place_v[4:6, :] = gatest_ref[...]
        place_v[6:8, :] = jnp.zeros((2, count), full)
        columns = place_v[...].T
        column_v[...] = columns

        def norm_rows(i, source, gain, target):
            at = pl.ds(pl.multiple_of(i * 64, 64), 64)
            whole = source[at, :].astype(full)
            centred = whole - jnp.mean(whole, axis=1, keepdims=True)
            scale = lax.rsqrt(jnp.mean(centred * centred, axis=1, keepdims=True) + 1e-05)
            target[at, :] = (centred * scale * gain).astype(low)
            return 0

        lax.fori_loop(0, count // 64, lambda i, _: norm_rows(i, tok_ref, gain1_ref[...][None], norm_v), 0)
        loads[0].wait()

        def project(n, _):
            at = pl.ds(pl.multiple_of(n * 256, 256), 256)
            proj_v[:, at] = dot_nn(norm_v[...], wqkv_v[:, at]).astype(low)
            return 0

        lax.fori_loop(0, 3 * feat // 256, project, 0)
        stores = [pltpu.make_async_copy(proj_v, proj_hbm, sem.at[2])]
        stores[-1].start()

        key = lax.broadcasted_iota(jnp.int32, (count, count), 0)
        query = lax.broadcasted_iota(jnp.int32, (count, count), 1)
        allowed = (columns[:, 2:3] == document) & (key <= query) & ((columns[:, 3:4] > 0.0) | (key == query))
        bias_v[...] = jnp.where(allowed, 0.0, -1e30)
        lower = lax.broadcasted_iota(jnp.int32, (count, 128), 1) < 64

        def head_pair(p, _):
            at = pl.multiple_of(p * 128, 128)
            q = proj_v[:, pl.ds(at, 128)]
            k = proj_v[:, pl.ds(pl.multiple_of(feat + p * 128, 128), 128)]
            vt = proj_v[:, pl.ds(pl.multiple_of(2 * feat + p * 128, 128), 128)].T
            for j in range(2):
                one = jnp.where(lower if j == 0 else jnp.logical_not(lower), k, jnp.zeros_like(k))
                for b in range(2):
                    reach, here = (b + 1) * half, slice(b * half, (b + 1) * half)
                    scores = dot_nt(one[0:reach], q[here]) * 0.125 + bias_v[0:reach, here]
                    powers = jnp.exp(scores - jnp.max(scores, axis=0, keepdims=True))
                    probs = (powers * (1.0 / jnp.sum(powers, axis=0, keepdims=True))).astype(low)
                    prob_v[2 * p + j, b * half:b * half + reach, :] = probs
                    attt_v[pl.ds(at + 64 * j, 64), here] = dot_nn(vt[64 * j:64 * j + 64, 0:reach], probs).astype(low)
            pltpu.make_async_copy(prob_v.at[pl.ds(2 * p, 2)], prob_hbm.at[pl.ds(2 * p, 2)], prob_sem.at[p]).start()
            return 0

        lax.fori_loop(0, pairs, head_pair, 0)
        win.start()
        stores.append(pltpu.make_async_copy(attt_v, attt_hbm, sem.at[3]))
        stores[-1].start()

        def turn(n, _):
            at = pl.ds(pl.multiple_of(n * 128, 128), 128)
            att_v[:, at] = attt_v[at, :].T
            return 0

        lax.fori_loop(0, pairs, turn, 0)
        loads[1].wait()

        def mix(n, _):
            at = pl.ds(pl.multiple_of(n * 256, 256), 256)
            mixed_v[:, at] = tok_ref[:, at].astype(full) + dot_nn(att_v[...], wo_v[:, at])
            return 0

        lax.fori_loop(0, feat // 256, mix, 0)
        lax.fori_loop(0, count // 64, lambda i, _: norm_rows(i, mixed_v, gain2_ref[...][None], att_v), 0)

        def token_rows(which):
            one, two = picks(which)
            return dot_nn(jnp.where(one | two, 1.0, 0.0).astype(low), att_v[...]).astype(low)

        for r in reversed(range(ex_size)):
            if r:
                token_st[slot_rows(2 + (ex ^ r)), :] = token_rows(2 + (ex ^ r))
                row_copy(r).start()
            else:
                rows_v[0:cap, :] = token_rows(2 + ex)
        for which in range(2):
            token_st[slot_rows(which), :] = token_rows(which)

        def turn_norm(n, _):
            at = pl.ds(pl.multiple_of(n * 128, 128), 128)
            normt_v[at, :] = norm_v[:, at].T
            return 0

        lax.fori_loop(0, pairs, turn_norm, 0)
        stores.append(pltpu.make_async_copy(normt_v, normt_hbm, sem.at[4]))
        stores[-1].start()
        for p in range(pairs):
            pltpu.make_async_copy(prob_v.at[pl.ds(2 * p, 2)], prob_hbm.at[pl.ds(2 * p, 2)], prob_sem.at[p]).wait()
        for copy in stores:
            copy.wait()

    heads = feat // 64
    pl.run_scoped(
        forward, pltpu.VMEM((feat, 3 * feat), low), pltpu.VMEM((feat, feat), low), pltpu.VMEM((count, feat), low),
        pltpu.VMEM((feat, count), low), pltpu.VMEM((count, 3 * feat), low), pltpu.VMEM((heads, count + half, half), low),
        pltpu.VMEM((feat, count), low), pltpu.VMEM((count, feat), low), pltpu.VMEM((count, count), full), dma((5,)))

    def expert(act_v, hg_v, fin_v, fout_v, facc_v, fst_v, rg_v, even_v, odd_v, sem, load_sem):
        steps = fin_hbm.shape[0]
        per = steps // 2

        def frozen_load(i, slot):
            return (pltpu.make_async_copy(fin_hbm.at[i], fin_v.at[slot], load_sem.at[0, slot]),
                    pltpu.make_async_copy(fout_hbm.at[i], fout_v.at[slot], load_sem.at[1, slot]))

        def back_copy(r):
            source, target = rg_v.at[pl.ds(r * cap, cap)], back_hbm.at[slot_rows(2 + ex)]
            if r == 0:
                return pltpu.make_async_copy(source, target, sem.at[0])
            return remote(source, target, back_sem, (r,), (dp, ex ^ r))

        for copy in frozen_load(0, 0):
            copy.start()

        def frozen(i, _):
            slot = lax.rem(i, 2)
            for copy in frozen_load(i, slot):
                copy.wait()

            @pl.when(i + 1 < steps)
            def _():
                for copy in frozen_load(i + 1, 1 - slot):
                    copy.start()
            which = i // per
            up, down = fin_v[slot], fout_v[slot]
            active, slope = gelu_pair(dot_nt(token_st[slot_rows(which), :], up))
            slope_in = dot_nt(grad_st[slot_rows(which), :], down)
            result = dot_nn(active.astype(low), down)
            back = dot_nn((slope_in * slope).astype(low), up)
            fresh = lax.rem(i, per) == 0

            @pl.when(fresh)
            def _():
                facc_v[0, which] = result
                facc_v[1, which] = back

            @pl.when(jnp.logical_not(fresh))
            def _():
                facc_v[0, which] += result
                facc_v[1, which] += back
            return 0

        lax.fori_loop(0, steps, frozen, 0)
        stores = []
        for which in range(2):
            fst_v[0, pl.ds(which * cap, cap), :] = facc_v[0, which].astype(low)
            fst_v[1, pl.ds(which * cap, cap), :] = facc_v[1, which].astype(low)
        for n, target in enumerate((ret_hbm, back_hbm)):
            stores.append(pltpu.make_async_copy(fst_v.at[n], target.at[pl.ds(0, 2 * cap)], sem.at[1 + n]))
            stores[-1].start()
        wout.forward()
        for copy in own_shards():
            copy.wait()
        wout.finish()
        for r in range(1, ex_size):
            grad_copy(r).wait()

        def slope_tile(t, _):
            at = pl.ds(pl.multiple_of(t * 256, 256), 256)
            hg_v[:, at] = dot_nt(grad_v[...], wout_v[at, :]).astype(low)
            return 0

        lax.fori_loop(0, tiles, slope_tile, 0)
        win.forward()
        win.finish()
        order = list(reversed(range(ex_size)))
        for group in (order[:ex_size // 4], order[ex_size // 4:ex_size // 2], order[ex_size // 2:]):
            here = pl.ds(group[-1] * cap, len(group) * cap)
            for r in group:
                if r:
                    row_copy(r).wait_recv()

            size = pl.ds(0, len(group) * cap)

            def units(t, target, here=here, size=size):
                at = pl.ds(pl.multiple_of(t * 256, 256), 256)
                target[size, :] = dot_nt(rows_v[here, :], win_v[at, :])

            def gelu_tile(t, source, here=here, size=size):
                at = pl.ds(pl.multiple_of(t * 256, 256), 256)
                active, slope = gelu_pair(source[size, :])
                act_v[here, at] = active.astype(low)
                hg_v[here, at] = (hg_v[here, at].astype(full) * slope).astype(low)

            units(0, even_v)

            def tile_pair(i, _):
                units(2 * i + 1, odd_v)
                gelu_tile(2 * i, even_v)
                units(lax.rem(2 * i + 2, tiles), even_v)
                gelu_tile(2 * i + 1, odd_v)
                return 0

            lax.fori_loop(0, tiles // 2, tile_pair, 0)

            def back_tile(n, _, here=here):
                at = pl.ds(pl.multiple_of(n * 256, 256), 256)
                rg_v[here, at] = dot_nn(hg_v[here, :], win_v[:, at]).astype(low)
                return 0

            lax.fori_loop(0, feat // 256, back_tile, 0)
            for r in group:
                back_copy(r).start()
        for r in range(1, ex_size):
            row_copy(r).wait_send()

        width = 256 if shard % 256 == 0 else 128

        def one_shard(which, units, rows, target):
            def tile(j, _):
                at = pl.ds(pl.multiple_of(which * shard + j * width, width), width)
                target[at, :] = dot_tn(units[:, at], rows[...]).astype(low)
                return 0

            lax.fori_loop(0, shard // width, tile, 0)

        def all_shards(scatter, units, rows):
            for k in range(1, far):
                one_shard(dp ^ (2 * k + 1), units, rows, scatter.source)
                scatter.core(k).start()
                one_shard(dp ^ (2 * k), units, rows, scatter.source)
            scatter.to_chips()
            one_shard(dp ^ 1, units, rows, scatter.source)
            scatter.core(0).start()
            one_shard(dp, units, rows, scatter.source)

        all_shards(in_scatter, hg_v, rows_v)

        def result_tile(n, _):
            at = pl.ds(pl.multiple_of(n * 256, 256), 256)
            rows_v[:, at] = dot_nn(act_v[...], wout_v[:, at]).astype(low)
            return 0

        lax.fori_loop(0, feat // 256, result_tile, 0)
        for r in reversed(range(ex_size)):
            result_copy(r).start()
        all_shards(out_scatter, act_v, grad_v)
        for copy in stores:
            copy.wait()
        for r in range(ex_size):
            back_copy(r).wait()

    span = fin_hbm.shape[1]
    rows_all = ex_size * cap
    pl.run_scoped(
        expert, pltpu.VMEM((rows_all, hidden), low), pltpu.VMEM((rows_all, hidden), low), pltpu.VMEM((2, span, feat), low),
        pltpu.VMEM((2, span, feat), low), pltpu.VMEM((2, 2, cap, feat), full), pltpu.VMEM((2, 2 * cap, feat), low),
        pltpu.VMEM((rows_all, feat), low), pltpu.VMEM((rows_all // 2, 256), full), pltpu.VMEM((rows_all // 2, 256), full),
        dma((3,)), dma((2, 2)))

    back_v, ret_v, branch_v, da_v = grad_st, token_st, grad_v.at[pl.ds(0, count)], grad_v.at[pl.ds(count, count)]

    def backward(prob_v, proj_v, turned_v, wo_v, pg_v, blocks_v, acc_v, g_v, mg_v, pick_v, dqt_v, sem):
        loads = [pltpu.make_async_copy(source, target, sem.at[i]) for i, (source, target) in enumerate([
            (back_hbm, back_v.at[pl.ds(0, slots)]), (attt_hbm, turned_v), (wo_hbm, wo_v), (prob_hbm, prob_v),
            (proj_hbm, proj_v)])]
        for copy in loads:
            copy.start()
        sums = Sums(sum_chunks(dp_size, ex_size, blocks_v.shape[0]), blocks_v, acc_v, got_v, total_hbm, part_sem, join_sem,
                    own_sem)

        def place_tile(n):
            at = pl.ds(pl.multiple_of(n * 128, 128), 128)
            slot = (n * 128 + lax.broadcasted_iota(jnp.int32, (count, 128), 1)).astype(full)
            return at, slot == column_v[:, 0:1], slot == column_v[:, 1:2]

        def pick_both(n, _):
            at, one, two = place_tile(n)
            pick_v[:, at] = jnp.where(one | two, 1.0, 0.0).astype(low)
            return 0

        lax.fori_loop(0, padded // 128, pick_both, 0)
        loads[0].wait()

        def collect(n, _):
            at = pl.ds(pl.multiple_of(n * 256, 256), 256)
            g_v[:, at] = dot_nn(pick_v[...], back_v[:, at])
            return 0

        lax.fori_loop(0, feat // 256, collect, 0)
        gain_v[...] = jnp.zeros_like(gain_v)
        gain_v[16:24, 0:128] = count_v[...]

        def norm_back(i, whole, gain, target):
            at = pl.ds(pl.multiple_of(i * 64, 64), 64)
            centred = whole - jnp.mean(whole, axis=1, keepdims=True)
            scale = lax.rsqrt(jnp.mean(centred * centred, axis=1, keepdims=True) + 1e-05)
            unit = centred * scale
            grad = g_v[at, :]
            weighted = grad * unit
            gain_v[target:target + 8, :] += jnp.sum(weighted.reshape(8, 8, feat), axis=0)
            scaled = grad * gain
            return at, scale * (scaled - jnp.mean(scaled, axis=1, keepdims=True)
                                - unit * jnp.mean(scaled * unit, axis=1, keepdims=True))

        def second_norm(i, _):
            at, part = norm_back(i, mixed_v[pl.ds(pl.multiple_of(i * 64, 64), 64), :], gain2_ref[...][None], 8)
            grad = cot_ref[at, :].astype(full) + part
            mg_v[at, :] = grad
            branch_v[at, :] = grad.astype(low)
            return 0

        lax.fori_loop(0, count // 64, second_norm, 0)
        loads[1].wait()

        def out_weight(b, _):
            at = pl.ds(pl.multiple_of(b * wide, 128), wide)
            blocks_v[pl.ds(pl.multiple_of(b * feat, 16), feat), :] = dot_nn(turned_v[...], branch_v[:, at]).astype(low)
            return 0

        lax.fori_loop(0, 2, out_weight, 0)
        loads.append(pltpu.make_async_copy(normt_hbm, turned_v, sem.at[5]))
        loads[5].start()
        sums.start(0)
        loads[2].wait()

        def attended_grad(n, _):
            at = pl.ds(pl.multiple_of(n * 256, 256), 256)
            da_v[:, at] = dot_nt(branch_v[...], wo_v[at, :]).astype(low)
            return 0

        lax.fori_loop(0, feat // 256, attended_grad, 0)
        loads[3].wait()
        loads[4].wait()
        lower = lax.broadcasted_iota(jnp.int32, (count, 128), 1) < 64

        def head_pair(p, _):
            at_q = pl.ds(pl.multiple_of(p * 128, 128), 128)
            at_k = pl.ds(pl.multiple_of(feat + p * 128, 128), 128)
            at_v = pl.ds(pl.multiple_of(2 * feat + p * 128, 128), 128)
            q, k, v, da = proj_v[:, at_q], proj_v[:, at_k], proj_v[:, at_v], da_v[:, at_q]
            kt = k.T
            key_near = key_far = value_near = value_far = 0.0
            for j in range(2):
                mask = lower if j == 0 else jnp.logical_not(lower)
                qj, vj, daj = [jnp.where(mask, w, jnp.zeros_like(w)) for w in (q, v, da)]
                for b in range(2):
                    reach, here = (b + 1) * half, slice(b * half, (b + 1) * half)
                    prob = prob_v[2 * p + j, b * half:b * half + reach, :]
                    whole = prob.astype(full)
                    grad = dot_nt(vj[0:reach], da[here])
                    score = (whole * (grad - jnp.sum(whole * grad, axis=0, keepdims=True))).astype(low)
                    dqt_v[64 * j:64 * j + 64, here] = dot_nn(kt[64 * j:64 * j + 64, 0:reach], score)
                    key_near += dot_nn(score[0:half], qj[here])
                    value_near += dot_nn(prob[0:half], daj[here])
                    if b:
                        key_far += dot_nn(score[half:], qj[here])
                        value_far += dot_nn(prob[half:], daj[here])
            pg_v[:, at_q] = (dqt_v[...].T * 0.125).astype(low)
            pg_v[0:half, at_k] = (key_near * 0.125).astype(low)
            pg_v[half:, at_k] = (key_far * 0.125).astype(low)
            pg_v[0:half, at_v] = value_near.astype(low)
            pg_v[half:, at_v] = value_far.astype(low)
            return 0

        for part in range(2):
            lax.fori_loop(part * pairs // 2, (part + 1) * pairs // 2, head_pair, 0)
            if part == 0:
                loads[5].wait()
                in_scatter.finish()
                ends = [pltpu.make_async_copy(icore_v.at[0], dwin_hbm, sem.at[7])]
                ends[-1].start()
                weights = [pltpu.make_async_copy(wqkv_hbm.at[:, pl.ds(c * feat, feat)], win_v.at[pl.ds(c * feat, feat)],
                                                 sem.at[10 + c]) for c in range(3)]
                for copy in weights:
                    copy.start()
            sums.tick()

            def weight_block(c, _, part=part):
                at = pl.ds(pl.multiple_of(c * feat + part * wide, 128), wide)
                into = pl.ds(pl.multiple_of(2 * feat + (3 * part + c) * feat, 16), feat)
                blocks_v[into, :] = dot_nn(turned_v[...], pg_v[:, at]).astype(low)
                return 0

            lax.fori_loop(0, 3, weight_block, 0)
            sums.start(1 + part)
        for copy in weights:
            copy.wait()

        def norm_grad(n, _):
            at = pl.ds(pl.multiple_of(n * 256, 256), 256)
            g_v[:, at] = sum(dot_nt(pg_v[:, c * feat:(c + 1) * feat],
                                    win_v[pl.ds(pl.multiple_of(c * feat + n * 256, 256), 256), :]) for c in range(3))
            return 0

        lax.fori_loop(0, feat // 256, norm_grad, 0)
        sums.tick()

        def first_norm(i, _):
            here = pl.ds(pl.multiple_of(i * 64, 64), 64)
            at, part = norm_back(i, tok_ref[here, :].astype(full), gain1_ref[...][None], 0)
            dtok_ref[at, :] = (mg_v[at, :] + part).astype(low)
            return 0

        lax.fori_loop(0, count // 64, first_norm, 0)

        core, xs, ys, zs = butterfly(dp_size, ex_size)
        order = [[core], ys, xs, zs]
        stages = len(order)
        slot_of = [stages + sum((1 << len(stage)) - 1 for stage in order[:i]) for i in range(stages)]
        for i in range(3):
            small_v[0, i:i + 1, :] = jnp.sum(gain_v[8 * i:8 * i + 8, :], axis=0, keepdims=True)
        small_v[0, 2:3, :] = gain_v[16:17, :]
        small_v[0, 3:8, :] = jnp.zeros((5, feat), full)

        def small_send(i):
            copies = []
            for m, peer in enumerate(group_of(order[i])[1], 1):
                copies.append(remote(small_v.at[i], small_v.at[slot_of[i] + m - 1], tiny_sem, (i, m), peer))
                copies[-1].start()
            return copies

        def small_add(i, copies):
            for copy in copies:
                copy.wait()
            mine, peers = group_of(order[i])
            total = jnp.zeros_like(sum_ref[...])
            for n in range(len(peers) + 1):
                term = small_v[i]
                for m in range(1, len(peers) + 1):
                    term = jnp.where(mine == n ^ m, small_v[slot_of[i] + m - 1], term)
                total = total + term
            if i + 1 < stages:
                small_v[i + 1] = total
                return small_send(i + 1)
            sum_ref[...] = total

        tiny = small_send(0)
        sums.tick()
        sums.tick()
        tiny = small_add(0, tiny)
        sums.tick()
        tiny = small_add(1, tiny)
        out_scatter.finish()
        ends.append(pltpu.make_async_copy(ocore_v.at[0], dwout_hbm, sem.at[8]))
        ends[-1].start()
        for r in range(ex_size):
            result_copy(r).wait()
        load = pltpu.make_async_copy(ret_hbm, ret_v.at[pl.ds(0, slots)], sem.at[9])
        load.start()
        sums.tick()
        tiny = small_add(2, tiny)
        load.wait()
        for turn in range(2):
            def pick_one(n, _, turn=turn):
                at, one, two = place_tile(n)
                pick_v[:, at] = jnp.where((one, two)[turn], 1.0, 0.0).astype(low)
                return 0

            lax.fori_loop(0, padded // 128, pick_one, 0)

            def deliver(n, _, turn=turn):
                at = pl.ds(pl.multiple_of(n * 256, 256), 256)
                term = dot_nn(pick_v[...], ret_v[:, at]) * column_v[:, 4 + turn:5 + turn]
                if turn == 0:
                    g_v[:, at] = term
                else:
                    out_ref[:, at] = (mixed_v[:, at] + (g_v[:, at] + term)).astype(low)
                return 0

            lax.fori_loop(0, feat // 256, deliver, 0)
            if turn == 0:
                sums.tick()
                small_add(3, tiny)
        sums.finish()
        for copy in ends:
            copy.wait()

    rows, steps = 8 * feat, 13
    pl.run_scoped(
        backward, pltpu.VMEM((heads, count + half, half), low), pltpu.VMEM((count, 3 * feat), low),
        pltpu.VMEM((feat, count), low), pltpu.VMEM((feat, feat), low), pltpu.VMEM((count, 3 * feat), low),
        pltpu.VMEM((rows, wide), low),
        pltpu.VMEM((rows // 2, wide), low), pltpu.VMEM((count, feat), full), pltpu.VMEM((count, feat), full),
        pltpu.VMEM((count, padded), low), pltpu.VMEM((128, count), full), dma((steps,)))


def layer(tokens, cotangent, chosen, gates, lengths, keep, gain1, gain2, wqkv, wo, in_shard, out_shard, fin, fout, kinds, cap,
          dp_size, ex_size):
    count, feat = tokens.shape
    shard = in_shard.shape[0]
    hidden = dp_size * shard
    far, slots = dp_size // 2, kinds * cap
    padded = (slots + 127) // 128 * 128
    heads, half = feat // 64, count // 2
    rows, wide = 8 * feat, feat // 2
    span = 768 if ex_size * cap <= 1024 else 384
    steps = 2 * hidden // span
    chunks, stages = len(sum_chunks(dp_size, ex_size, rows)), 4
    anyspace, vmem = pl.BlockSpec(memory_space=pl.ANY), pl.BlockSpec(memory_space=pltpu.VMEM)
    dma, shape, buffer = pltpu.SemaphoreType.DMA, jax.ShapeDtypeStruct, pltpu.VMEM
    full, low = jnp.float32, jnp.bfloat16
    scatter = [buffer((far, shard, feat), low), buffer((far - 1, shard, feat), low), buffer((far - 1, shard, feat), low)]
    return pl.pallas_call(
        functools.partial(layer_kernel, dp_size, ex_size, kinds, cap),
        out_shape=(shape((count, feat), low), shape((count, feat), low), shape((rows, wide), low), shape((8, feat), full),
                   shape((shard, feat), low), shape((shard, feat), low),
                   shape((slots, feat), low), shape((slots, feat), low), shape((count, 3 * feat), low),
                   shape((heads, count + half, half), low), shape((feat, count), low), shape((feat, count), low)),
        in_specs=[pl.BlockSpec(memory_space=pltpu.SMEM)] + [vmem] * 7 + [anyspace] * 6,
        out_specs=(vmem, vmem, anyspace, vmem) + (anyspace,) * 8,
        scratch_shapes=[
            buffer((padded, feat), low), buffer((padded, feat), low),
            buffer((ex_size * cap, feat), low), buffer((ex_size * cap, feat), low),
            buffer((hidden, feat), low), buffer((hidden, feat), low)] + scatter + scatter + [
            buffer((rows, wide), low), buffer((count, feat), full), buffer((8, count), full), buffer((count, 8), full),
            buffer((24, feat), full), buffer((8, 128), full), buffer((4 * stages, 8, feat), full),
            dma((2, ex_size)), dma((2, ex_size)), dma((2, ex_size)), dma((2, ex_size)),
            dma((2, 2, far)), dma((2, 2, far)), dma((2, 2, far)), dma((2, 2, far)),
            dma((2, chunks, stages, 4)), dma((2, chunks, stages, 4)), dma((chunks,)),
            dma((2, stages, 4)), dma((3,)), dma((feat // 128,)),
        ],
        compiler_params=pltpu.CompilerParams(collective_id=0, has_side_effects=True, vmem_limit_bytes=63 << 20),
        name="layer",
    )(lengths, chosen.T, gates.T, keep[None], tokens, cotangent, gain1, gain2, wqkv, wo, in_shard, out_shard,
      fin.reshape(steps, span, feat), fout.reshape(steps, span, feat))


def finish_kernel(total_hbm, small_hbm, out_in, dtok_in, dwin_in, dwout_in,
                  out_hbm, dtok_hbm, gain1_ref, qkv_hbm, wide_hbm, gain2_ref, dwin_hbm, dwout_hbm, count_ref,
                  block_v, whole_v, shard_v, shard_w, row_v, small_v, load_sem, store_sem):
    feat = small_v.shape[1]
    wide = feat // 2
    copy = pltpu.make_async_copy
    loads = [copy(total_hbm.at[pl.ds(b * feat, feat)], block_v.at[b], load_sem.at[b]) for b in range(8)]
    loads += [copy(source, shard_v.at[n], load_sem.at[8 + n]) for n, source in enumerate((dwin_in, dwout_in))]
    loads += [copy(source, row_v.at[n], load_sem.at[10 + n]) for n, source in enumerate((out_in, dtok_in))]
    loads.append(copy(small_hbm, small_v, load_sem.at[12]))
    for load in loads:
        load.start()
    stores = []

    def widen(source, target, rows):
        def tile(j, _):
            at = pl.ds(pl.multiple_of(j * 64, 64), 64)
            target[at, :] = source[at, :].astype(jnp.float32)
            return 0

        lax.fori_loop(0, rows // 64, tile, 0)

    def store(source, target):
        stores.append(copy(source, target, store_sem.at[len(stores)]))
        stores[-1].start()

    for b in range(8):
        loads[b].wait()
        widen(block_v.at[b], whole_v.at[b], feat)
        part, c = (b - 2) // 3, (b - 2) % 3
        store(whole_v.at[b],
              wide_hbm.at[:, pl.ds(b * wide, wide)] if b < 2 else qkv_hbm.at[:, pl.ds(c * feat + part * wide, wide)])
    for n, target in enumerate((dwin_hbm, dwout_hbm)):
        loads[8 + n].wait()
        widen(shard_v.at[n], shard_w.at[n], shard_v.shape[1])
        store(shard_w.at[n], target)
    for n, target in enumerate((out_hbm, dtok_hbm)):
        loads[10 + n].wait()
        store(row_v.at[n], target)
    loads[12].wait()
    gain1_ref[...] = small_v[0, :]
    gain2_ref[...] = small_v[1, :]
    count_ref[...] = small_v[2, 0:128]
    for load in stores:
        load.wait()


def finish(total, small, out, dtok, dwin, dwout):
    rows, wide = total.shape
    feat = 2 * wide
    anyspace, vmem = pl.BlockSpec(memory_space=pl.ANY), pl.BlockSpec(memory_space=pltpu.VMEM)
    shape, full, low, buffer = jax.ShapeDtypeStruct, jnp.float32, jnp.bfloat16, pltpu.VMEM
    return pl.pallas_call(
        finish_kernel,
        out_shape=(shape(out.shape, low), shape(dtok.shape, low), shape((feat,), full), shape((feat, 3 * feat), full),
                   shape((feat, feat), full), shape((feat,), full), shape(dwin.shape, full), shape(dwout.shape, full),
                   shape((128,), full)),
        in_specs=[anyspace] * 6,
        out_specs=(anyspace, anyspace, vmem, anyspace, anyspace, vmem, anyspace, anyspace, vmem),
        scratch_shapes=[buffer((8, feat, wide), low), buffer((8, feat, wide), full), buffer((2,) + dwin.shape, low),
                        buffer((2,) + dwin.shape, full), buffer((2,) + out.shape, low), buffer(small.shape, full),
                        pltpu.SemaphoreType.DMA((13,)), pltpu.SemaphoreType.DMA((12,))],
        compiler_params=pltpu.CompilerParams(vmem_limit_bytes=63 << 20),
        name="finish",
    )(total, small, out, dtok, dwin, dwout)


FROZEN = 2


def body(
    tokens,
    cotangent,
    chosen,
    gates,
    lengths,
    keep_mask,
    gain1,
    w_qkv,
    w_o,
    gain2,
    frozen_in,
    frozen_out,
    w_in,
    w_out,
):
    row_count, feat_width = tokens.shape
    owners = lax.axis_size("expert")
    dp_size = lax.axis_size("dp")
    kind_count = FROZEN + owners
    slot_count = ((2 * row_count * 5 // (4 * kind_count) + 7) // 8 * 8 + 15) // 16 * 16
    output, tokens_grad, total, small_sum, d_w_in, d_w_out = layer(
        tokens, cotangent, chosen, gates, lengths, keep_mask, gain1, gain2, w_qkv, w_o, w_in[0], w_out[0], frozen_in,
        frozen_out, kind_count, slot_count, dp_size, owners)[:6]
    output, tokens_grad, gain1_sum, w_qkv_sum, w_o_sum, gain2_sum, d_w_in, d_w_out, counts = finish(
        total, small_sum, output, tokens_grad, d_w_in, d_w_out)
    return (
        output,
        tokens_grad,
        gain1_sum,
        w_qkv_sum,
        w_o_sum,
        gain2_sum,
        d_w_in[None],
        d_w_out[None],
        counts[:kind_count],
    )


def solution(mesh):
    placed = (
        P(("dp", "expert"), None),
        P(("dp", "expert"), None),
        P(("dp", "expert"), None),
        P(("dp", "expert"), None),
        P(("dp", "expert"), None),
        P(("dp", "expert")),
        P(),
        P(),
        P(),
        P(),
        P(),
        P(),
        P("expert", "dp", None),
        P("expert", "dp", None),
    )
    return jax.shard_map(
        body,
        mesh=mesh,
        in_specs=placed,
        out_specs=(
            P(("dp", "expert"), None),
            P(("dp", "expert"), None),
            P(),
            P(),
            P(),
            P(),
            P("expert", "dp", None),
            P("expert", "dp", None),
            P(),
        ),
        check_vma=False,
    )
```

```python
import functools
import jax
import jax.numpy as jnp
from jax import lax
from jax.experimental import pallas as pl
from jax.experimental.pallas import tpu as pltpu
from jax.sharding import PartitionSpec as P

MESH = pl.DeviceIdType.MESH


def butterfly(dp_size, ex_size):
    core = ("dp", 1)
    xs = [("dp", 2 << k) for k in range((dp_size // 2).bit_length() - 1)]
    depth = 4 if ex_size % 4 == 0 else 1
    wide = ex_size // depth
    ys = [("expert", 1 << k) for k in range(wide.bit_length() - 1)]
    zs = [("expert", wide << k) for k in range(depth.bit_length() - 1)]
    return core, xs, ys, zs


def group_of(stage):
    place = {"dp": lax.axis_index("dp"), "expert": lax.axis_index("expert")}
    mine = sum(lax.rem(place[axis] // mask, 2) << j for j, (axis, mask) in enumerate(stage))
    peers = []
    for m in range(1, 1 << len(stage)):
        peer = dict(place)
        for j, (axis, mask) in enumerate(stage):
            if m >> j & 1:
                peer[axis] = peer[axis] ^ mask
        peers.append((peer["dp"], peer["expert"]))
    return mine, peers


def dot_nn(a, b):
    return jnp.dot(a, b, preferred_element_type=jnp.float32)


def dot_nt(a, b):
    return lax.dot_general(a, b, (((1,), (1,)), ((), ())), preferred_element_type=jnp.float32)


def dot_tn(a, b):
    return lax.dot_general(a, b, (((0,), (0,)), ((), ())), preferred_element_type=jnp.float32)


GELU_A = 0.7978845608028654
GELU_B = GELU_A * 0.044715


def gelu_pair(h):
    square = h * h
    bend = jnp.tanh(h * (GELU_B * square + GELU_A))
    share = 0.5 * bend + 0.5
    slope = share + (0.5 * h) * (1.0 - bend * bend) * ((3.0 * GELU_B) * square + GELU_A)
    return h * share, slope


def remote(source, target, pair, at, device):
    return pltpu.make_async_remote_copy(
        src_ref=source, dst_ref=target, send_sem=pair.at[(0,) + at], recv_sem=pair.at[(1,) + at], device_id=device,
        device_id_type=MESH)


class Gather:

    def __init__(self, dp, ex, far, source, whole, sems):
        self.dp, self.ex, self.far, self.source, self.whole, self.sems = dp, ex, far, source, whole, sems
        self.rows = source.shape[0]

    def at(self, which):
        return self.whole.at[pl.ds(pl.multiple_of(which * self.rows, 16), self.rows)]

    def first(self, k):
        return remote(self.source, self.at(self.dp), self.sems, (0, k), (self.dp ^ (2 * k if k else 1), self.ex))

    def second(self, k):
        theirs = self.at(self.dp ^ (2 * k))
        return remote(theirs, theirs, self.sems, (1, k), (self.dp ^ 1, self.ex))

    def start(self):
        for k in list(range(1, self.far)) + [0]:
            self.first(k).start()

    def forward(self):
        for k in range(1, self.far):
            self.first(k).wait_recv()
            self.second(k).start()

    def finish(self):
        self.first(0).wait()
        for k in range(1, self.far):
            self.first(k).wait_send()
            self.second(k).wait()


class Scatter:

    def __init__(self, dp, ex, far, source, core_v, pre_v, chip_v, sems):
        self.dp, self.ex, self.far, self.source = dp, ex, far, source
        self.core_v, self.pre_v, self.chip_v, self.sems = core_v, pre_v, chip_v, sems
        self.rows = core_v.shape[1]

    def at(self, which):
        return self.source.at[pl.ds(pl.multiple_of(which * self.rows, 16), self.rows)]

    def core(self, k):
        return remote(self.at(self.dp ^ (2 * k + 1)), self.core_v.at[k], self.sems, (0, k), (self.dp ^ 1, self.ex))

    def chip(self, k):
        return remote(self.pre_v.at[k - 1], self.chip_v.at[k - 1], self.sems, (1, k), (self.dp ^ (2 * k), self.ex))

    def to_chips(self):
        for k in range(1, self.far):
            self.core(k).wait_recv()
            source = self.at(self.dp ^ (2 * k))

            def add(j, _):
                at = pl.ds(pl.multiple_of(j * 128, 128), 128)
                total = source[at, :].astype(jnp.float32) + self.core_v[k, at, :].astype(jnp.float32)
                self.pre_v[k - 1, at, :] = total.astype(jnp.bfloat16)
                return 0

            lax.fori_loop(0, self.rows // 128, add, 0)
            self.chip(k).start()

    def finish(self):
        self.core(0).wait_recv()
        for k in range(1, self.far):
            self.chip(k).wait_recv()
        source = self.at(self.dp)

        def add(j, _):
            at = pl.ds(pl.multiple_of(j * 128, 128), 128)
            total = source[at, :].astype(jnp.float32) + self.core_v[0, at, :].astype(jnp.float32)
            for k in range(1, self.far):
                total = total + self.chip_v[k - 1, at, :].astype(jnp.float32)
            self.core_v[0, at, :] = total.astype(jnp.bfloat16)
            return 0

        lax.fori_loop(0, self.rows // 128, add, 0)
        for k in range(self.far):
            self.core(k).wait_send()
            if k:
                self.chip(k).wait_send()


class Sums:

    def __init__(self, chunks, blocks, acc, got, out, scatter_sems, gather_sems, own_sems):
        self.chunks, self.blocks, self.acc, self.got, self.out = chunks, blocks, acc, got, out
        self.scatter_sems, self.gather_sems, self.own_sems = scatter_sems, gather_sems, own_sems
        self.offs = [[base] for base, _, _, _ in chunks]
        self.lens = [[rows] for _, rows, _, _ in chunks]
        self.land = [[base] for base, _, _, _ in chunks]
        self.copies = [None] * len(chunks)
        self.shift = [0] * len(chunks)
        self.stage = [0] * len(chunks)
        self.own = [None] * len(chunks)

    def scatter(self, c, i):
        base, _, order, _ = self.chunks[c]
        mine, peers = group_of(order[i])
        part = self.lens[c][i] >> len(order[i])
        source = self.acc if i else self.blocks
        self.copies[c] = []
        for m, peer in enumerate(peers, 1):
            give = pl.multiple_of(self.offs[c][i] + (mine ^ m) * part + self.shift[c], 16)
            self.copies[c].append(remote(
                source.at[pl.ds(give, part)], self.got.at[pl.ds(self.land[c][i] + (m - 1) * part, part)],
                self.scatter_sems, (c, i, m), peer))
            self.copies[c][-1].start()
        self.offs[c].append(self.offs[c][i] + mine * part)
        self.lens[c].append(part)
        self.land[c].append(self.land[c][i] + len(peers) * part)

    def gather(self, c, i):
        stages = len(self.chunks[c][2])
        _, peers = group_of(self.chunks[c][2][i])
        part = self.lens[c][i + 1]
        target = self.out.at[pl.ds(pl.multiple_of(self.offs[c][i + 1], 16), part)]
        source = target
        if i + 1 == stages:
            source = self.acc.at[pl.ds(pl.multiple_of(self.offs[c][i + 1] + self.shift[c], 16), part)]
            self.own[c] = pltpu.make_async_copy(source, target, self.own_sems.at[c])
            self.own[c].start()
        self.copies[c] = []
        for m, peer in enumerate(peers, 1):
            self.copies[c].append(remote(source, target, self.gather_sems, (c, i, m), peer))
            self.copies[c][-1].start()

    def start(self, phase):
        for c, chunk in enumerate(self.chunks):
            if chunk[3] == phase:
                self.scatter(c, 0)

    def advance(self, c):
        if not self.copies[c]:
            return
        base, _, order, _ = self.chunks[c]
        stages, s = len(order), self.stage[c]
        for copy in self.copies[c]:
            copy.wait()
        self.stage[c] += 1
        if s >= stages:
            i = 2 * stages - 1 - s
            self.copies[c] = None
            if s == stages:
                self.own[c].wait()
            if i > 0:
                self.gather(c, i - 1)
            return
        part = self.lens[c][s + 1]
        source = self.acc if s else self.blocks
        keep, begin = self.offs[c][s + 1], self.land[c][s]
        count = (1 << len(order[s])) - 1
        tile = part
        while tile > 128 or part % tile or tile % 16:
            tile -= 16
        move_in = self.shift[c]
        if s == 0:
            self.shift[c] = base // 2 - keep
        move_out = self.shift[c]

        def add(j, _):
            at = pl.ds(pl.multiple_of(keep + move_out + j * tile, 16), tile)
            come = pl.ds(pl.multiple_of(keep + move_in + j * tile, 16), tile)
            total = source[come, :].astype(jnp.float32)
            for m in range(count):
                other = pl.ds(pl.multiple_of(begin + m * part + j * tile, 16), tile)
                total = total + self.got[other, :].astype(jnp.float32)
            self.acc[at, :] = total.astype(jnp.bfloat16)
            return 0

        lax.fori_loop(0, part // tile, add, 0)
        if s + 1 < stages:
            self.scatter(c, s + 1)
        else:
            self.gather(c, s)

    def tick(self):
        for c in reversed(range(len(self.chunks))):
            self.advance(c)

    def finish(self):
        while any(self.copies):
            for c in range(len(self.chunks)):
                self.advance(c)


def sum_chunks(dp_size, ex_size, rows):
    core, xs, ys, zs = butterfly(dp_size, ex_size)
    yxz, xyz, zyx = [[core], ys, xs, zs], [[core], xs, ys, zs], [[core], zs, ys, xs]
    if dp_size * ex_size * 16 <= 512:
        yq, xq, zq = [[core], ys, xs + zs[:1], zs[1:]], [[core], xs, ys + zs[:1], zs[1:]], [[core], zs[:1], ys + xs, zs[1:]]
        return [(0, 1536, yq, 0), (1536, 1024, xq, 1), (2560, 1024, yq, 1), (3584, 1024, yq, 2), (4608, 1024, xq, 2), (5632, 512, zq, 2)]
    third = rows // 3
    return [(0, third, yxz, 2), (third, third, xyz, 2), (2 * third, third, zyx, 2)]


def layer_kernel(dp_size, ex_size, kinds, cap,
                 lengths_s, chosen_ref, gatest_ref, keep_ref, tok_ref, cot_ref, gain1_ref, gain2_ref,
                 wqkv_hbm, wo_hbm, in_hbm, outw_hbm, fin_hbm, fout_hbm,
                 out_ref, dtok_ref, total_hbm, sum_ref, dwin_hbm, dwout_hbm,
                 back_hbm, ret_hbm, proj_hbm, prob_hbm, attt_hbm, normt_hbm,
                 token_st, grad_st, rows_v, grad_v, win_v, wout_v, icore_v, ipre_v, ichip_v, ocore_v, opre_v, ochip_v,
                 got_v, mixed_v, place_v, column_v, gain_v, count_v, small_v,
                 grad_sem, row_sem, back_sem, res_sem, win_sem, wout_sem, iscat_sem, oscat_sem, part_sem, join_sem, own_sem,
                 tiny_sem, local_sem, prob_sem):
    dp = lax.axis_index("dp")
    ex = lax.axis_index("expert")
    count, feat = tok_ref.shape
    shard = in_hbm.shape[0]
    hidden = win_v.shape[0]
    far = dp_size // 2
    slots = kinds * cap
    padded = token_st.shape[0]
    full, low = jnp.float32, jnp.bfloat16
    dma = pltpu.SemaphoreType.DMA
    half, wide, pairs, tiles = count // 2, feat // 2, feat // 128, hidden // 256

    barrier = pltpu.get_barrier_semaphore()
    for r in range(1, ex_size):
        pl.semaphore_signal(barrier, inc=1, device_id=(dp, ex ^ r), device_id_type=MESH)
    for k in range(1, dp_size):
        pl.semaphore_signal(barrier, inc=1, device_id=(dp ^ k, ex), device_id_type=MESH)

    def slot_rows(which):
        return pl.ds(pl.multiple_of(which * cap, 16), cap)

    def grad_copy(r):
        return remote(grad_st.at[slot_rows(2 + (ex ^ r))], grad_v.at[pl.ds(r * cap, cap)], grad_sem, (r,), (dp, ex ^ r))

    def row_copy(r):
        return remote(token_st.at[slot_rows(2 + (ex ^ r))], rows_v.at[pl.ds(r * cap, cap)], row_sem, (r,), (dp, ex ^ r))

    def result_copy(r):
        source, target = rows_v.at[pl.ds(r * cap, cap)], ret_hbm.at[slot_rows(2 + ex)]
        if r == 0:
            return pltpu.make_async_copy(source, target, local_sem.at[0])
        return remote(source, target, res_sem, (r,), (dp, ex ^ r))

    win = Gather(dp, ex, far, in_hbm, win_v, win_sem)
    wout = Gather(dp, ex, far, outw_hbm, wout_v, wout_sem)
    in_scatter = Scatter(dp, ex, far, win_v, icore_v, ipre_v, ichip_v, iscat_sem)
    out_scatter = Scatter(dp, ex, far, wout_v, ocore_v, opre_v, ochip_v, oscat_sem)

    def own_shards():
        return [pltpu.make_async_copy(outw_hbm, wout.at(dp), local_sem.at[1]),
                pltpu.make_async_copy(in_hbm, win.at(dp), local_sem.at[2])]

    def forward(wqkv_v, wo_v, norm_v, normt_v, proj_v, prob_v, attt_v, att_v, bias_v, sem):
        loads = [pltpu.make_async_copy(wqkv_hbm, wqkv_v, sem.at[0]), pltpu.make_async_copy(wo_hbm, wo_v, sem.at[1])]
        for copy in loads + own_shards():
            copy.start()

        kind = lax.broadcasted_iota(jnp.int32, (128, count), 0)
        first = chosen_ref[0:1, :]
        second = chosen_ref[1:2, :]
        hit_first = jnp.where(kind == first, 1.0, 0.0)
        hit_second = jnp.where(kind == second, 1.0, 0.0)
        hits = (hit_first + hit_second).astype(low)
        before = jnp.where(lax.broadcasted_iota(jnp.int32, (count, count), 0)
                           < lax.broadcasted_iota(jnp.int32, (count, count), 1), 1.0, 0.0).astype(low)
        ahead = dot_nn(hits, before)
        count_v[...] = dot_nt(jnp.ones((8, count), low), hits)
        place_v[0:1, :] = first.astype(full) * cap + jnp.sum(hit_first * ahead, axis=0, keepdims=True)
        place_v[1:2, :] = second.astype(full) * cap + jnp.sum(hit_second * ahead, axis=0, keepdims=True)

        def picks(which):
            slot = (which * cap + lax.broadcasted_iota(jnp.int32, (cap, count), 0)).astype(full)
            return slot == place_v[0:1, :], slot == place_v[1:2, :]

        def grad_rows(which):
            one, two = picks(which)
            gate = jnp.sum(jnp.where(one, gatest_ref[0:1, :], jnp.where(two, gatest_ref[1:2, :], 0.0)), axis=1,
                           keepdims=True)
            pick = jnp.where(one | two, 1.0, 0.0).astype(low)
            return (dot_nn(pick, cot_ref[...]) * gate).astype(low)

        pl.semaphore_wait(barrier, ex_size - 1 + dp_size - 1)
        wout.start()
        for r in reversed(range(ex_size)):
            if r:
                grad_st[slot_rows(2 + (ex ^ r)), :] = grad_rows(2 + (ex ^ r))
                grad_copy(r).start()
            else:
                grad_v[0:cap, :] = grad_rows(2 + ex)
        for which in range(2):
            grad_st[slot_rows(which), :] = grad_rows(which)
        if padded > slots:
            grad_st[slots:, :] = jnp.zeros((padded - slots, feat), low)
            token_st[slots:, :] = jnp.zeros((padded - slots, feat), low)

        spot = lax.broadcasted_iota(jnp.int32, (1, count), 1)
        document = jnp.zeros((1, count), full)
        end = lengths_s[0, 0]
        for j in range(1, lengths_s.shape[1] + 1):
            document = document + jnp.where(spot >= end, 1.0, 0.0)
            if j < lengths_s.shape[1]:
                end = end + lengths_s[0, j]
        place_v[2:3, :] = document
        place_v[3:4, :] = keep_ref[...].astype(full)
        place_v[4:6, :] = gatest_ref[...]
        place_v[6:8, :] = jnp.zeros((2, count), full)
        columns = place_v[...].T
        column_v[...] = columns

        def norm_rows(i, source, gain, target):
            at = pl.ds(pl.multiple_of(i * 64, 64), 64)
            whole = source[at, :].astype(full)
            centred = whole - jnp.mean(whole, axis=1, keepdims=True)
            scale = lax.rsqrt(jnp.mean(centred * centred, axis=1, keepdims=True) + 1e-05)
            target[at, :] = (centred * scale * gain).astype(low)
            return 0

        lax.fori_loop(0, count // 64, lambda i, _: norm_rows(i, tok_ref, gain1_ref[...][None], norm_v), 0)
        loads[0].wait()

        def project(n, _):
            at = pl.ds(pl.multiple_of(n * 256, 256), 256)
            proj_v[:, at] = dot_nn(norm_v[...], wqkv_v[:, at]).astype(low)
            return 0

        lax.fori_loop(0, 3 * feat // 256, project, 0)
        stores = [pltpu.make_async_copy(proj_v, proj_hbm, sem.at[2])]
        stores[-1].start()

        key = lax.broadcasted_iota(jnp.int32, (count, count), 0)
        query = lax.broadcasted_iota(jnp.int32, (count, count), 1)
        allowed = (columns[:, 2:3] == document) & (key <= query) & ((columns[:, 3:4] > 0.0) | (key == query))
        bias_v[...] = jnp.where(allowed, 0.0, -1e30)
        lower = lax.broadcasted_iota(jnp.int32, (count, 128), 1) < 64

        def head_pair(p, _):
            at = pl.multiple_of(p * 128, 128)
            q = proj_v[:, pl.ds(at, 128)]
            k = proj_v[:, pl.ds(pl.multiple_of(feat + p * 128, 128), 128)]
            vt = proj_v[:, pl.ds(pl.multiple_of(2 * feat + p * 128, 128), 128)].T
            for j in range(2):
                one = jnp.where(lower if j == 0 else jnp.logical_not(lower), k, jnp.zeros_like(k))
                for b in range(2):
                    reach, here = (b + 1) * half, slice(b * half, (b + 1) * half)
                    scores = dot_nt(one[0:reach], q[here]) * 0.125 + bias_v[0:reach, here]
                    powers = jnp.exp(scores - jnp.max(scores, axis=0, keepdims=True))
                    probs = (powers * (1.0 / jnp.sum(powers, axis=0, keepdims=True))).astype(low)
                    prob_v[2 * p + j, b * half:b * half + reach, :] = probs
                    attt_v[pl.ds(at + 64 * j, 64), here] = dot_nn(vt[64 * j:64 * j + 64, 0:reach], probs).astype(low)
            pltpu.make_async_copy(prob_v.at[pl.ds(2 * p, 2)], prob_hbm.at[pl.ds(2 * p, 2)], prob_sem.at[p]).start()
            return 0

        lax.fori_loop(0, pairs, head_pair, 0)
        win.start()
        stores.append(pltpu.make_async_copy(attt_v, attt_hbm, sem.at[3]))
        stores[-1].start()

        def turn(n, _):
            at = pl.ds(pl.multiple_of(n * 128, 128), 128)
            att_v[:, at] = attt_v[at, :].T
            return 0

        lax.fori_loop(0, pairs, turn, 0)
        loads[1].wait()

        def mix(n, _):
            at = pl.ds(pl.multiple_of(n * 256, 256), 256)
            mixed_v[:, at] = tok_ref[:, at].astype(full) + dot_nn(att_v[...], wo_v[:, at])
            return 0

        lax.fori_loop(0, feat // 256, mix, 0)
        lax.fori_loop(0, count // 64, lambda i, _: norm_rows(i, mixed_v, gain2_ref[...][None], att_v), 0)

        def token_rows(which):
            one, two = picks(which)
            return dot_nn(jnp.where(one | two, 1.0, 0.0).astype(low), att_v[...]).astype(low)

        for r in reversed(range(ex_size)):
            if r:
                token_st[slot_rows(2 + (ex ^ r)), :] = token_rows(2 + (ex ^ r))
                row_copy(r).start()
            else:
                rows_v[0:cap, :] = token_rows(2 + ex)
        for which in range(2):
            token_st[slot_rows(which), :] = token_rows(which)

        def turn_norm(n, _):
            at = pl.ds(pl.multiple_of(n * 128, 128), 128)
            normt_v[at, :] = norm_v[:, at].T
            return 0

        lax.fori_loop(0, pairs, turn_norm, 0)
        stores.append(pltpu.make_async_copy(normt_v, normt_hbm, sem.at[4]))
        stores[-1].start()
        for p in range(pairs):
            pltpu.make_async_copy(prob_v.at[pl.ds(2 * p, 2)], prob_hbm.at[pl.ds(2 * p, 2)], prob_sem.at[p]).wait()
        for copy in stores:
            copy.wait()

    heads = feat // 64
    pl.run_scoped(
        forward, pltpu.VMEM((feat, 3 * feat), low), pltpu.VMEM((feat, feat), low), pltpu.VMEM((count, feat), low),
        pltpu.VMEM((feat, count), low), pltpu.VMEM((count, 3 * feat), low), pltpu.VMEM((heads, count + half, half), low),
        pltpu.VMEM((feat, count), low), pltpu.VMEM((count, feat), low), pltpu.VMEM((count, count), full), dma((5,)))

    def expert(act_v, hg_v, fin_v, fout_v, facc_v, fst_v, rg_v, even_v, odd_v, sem, load_sem):
        steps = fin_hbm.shape[0]
        per = steps // 2

        def frozen_load(i, slot):
            return (pltpu.make_async_copy(fin_hbm.at[i], fin_v.at[slot], load_sem.at[0, slot]),
                    pltpu.make_async_copy(fout_hbm.at[i], fout_v.at[slot], load_sem.at[1, slot]))

        def back_copy(r):
            source, target = rg_v.at[pl.ds(r * cap, cap)], back_hbm.at[slot_rows(2 + ex)]
            if r == 0:
                return pltpu.make_async_copy(source, target, sem.at[0])
            return remote(source, target, back_sem, (r,), (dp, ex ^ r))

        for copy in frozen_load(0, 0):
            copy.start()

        def frozen(i, _):
            slot = lax.rem(i, 2)
            for copy in frozen_load(i, slot):
                copy.wait()

            @pl.when(i + 1 < steps)
            def _():
                for copy in frozen_load(i + 1, 1 - slot):
                    copy.start()
            which = i // per
            up, down = fin_v[slot], fout_v[slot]
            active, slope = gelu_pair(dot_nt(token_st[slot_rows(which), :], up))
            slope_in = dot_nt(grad_st[slot_rows(which), :], down)
            result = dot_nn(active.astype(low), down)
            back = dot_nn((slope_in * slope).astype(low), up)
            fresh = lax.rem(i, per) == 0

            @pl.when(fresh)
            def _():
                facc_v[0, which] = result
                facc_v[1, which] = back

            @pl.when(jnp.logical_not(fresh))
            def _():
                facc_v[0, which] += result
                facc_v[1, which] += back
            return 0

        lax.fori_loop(0, steps, frozen, 0)
        stores = []
        for which in range(2):
            fst_v[0, pl.ds(which * cap, cap), :] = facc_v[0, which].astype(low)
            fst_v[1, pl.ds(which * cap, cap), :] = facc_v[1, which].astype(low)
        for n, target in enumerate((ret_hbm, back_hbm)):
            stores.append(pltpu.make_async_copy(fst_v.at[n], target.at[pl.ds(0, 2 * cap)], sem.at[1 + n]))
            stores[-1].start()
        wout.forward()
        for copy in own_shards():
            copy.wait()
        wout.finish()
        for r in range(1, ex_size):
            grad_copy(r).wait()

        def slope_tile(t, _):
            at = pl.ds(pl.multiple_of(t * 256, 256), 256)
            hg_v[:, at] = dot_nt(grad_v[...], wout_v[at, :]).astype(low)
            return 0

        lax.fori_loop(0, tiles, slope_tile, 0)
        win.forward()
        win.finish()
        order = list(reversed(range(ex_size)))
        for group in (order[:ex_size // 4], order[ex_size // 4:ex_size // 2], order[ex_size // 2:]):
            here = pl.ds(group[-1] * cap, len(group) * cap)
            for r in group:
                if r:
                    row_copy(r).wait_recv()

            size = pl.ds(0, len(group) * cap)

            def units(t, target, here=here, size=size):
                at = pl.ds(pl.multiple_of(t * 256, 256), 256)
                target[size, :] = dot_nt(rows_v[here, :], win_v[at, :])

            def gelu_tile(t, source, here=here, size=size):
                at = pl.ds(pl.multiple_of(t * 256, 256), 256)
                active, slope = gelu_pair(source[size, :])
                act_v[here, at] = active.astype(low)
                hg_v[here, at] = (hg_v[here, at].astype(full) * slope).astype(low)

            units(0, even_v)

            def tile_pair(i, _):
                units(2 * i + 1, odd_v)
                gelu_tile(2 * i, even_v)
                units(lax.rem(2 * i + 2, tiles), even_v)
                gelu_tile(2 * i + 1, odd_v)
                return 0

            lax.fori_loop(0, tiles // 2, tile_pair, 0)

            def back_tile(n, _, here=here):
                at = pl.ds(pl.multiple_of(n * 256, 256), 256)
                rg_v[here, at] = dot_nn(hg_v[here, :], win_v[:, at]).astype(low)
                return 0

            lax.fori_loop(0, feat // 256, back_tile, 0)
            for r in group:
                back_copy(r).start()
        for r in range(1, ex_size):
            row_copy(r).wait_send()

        width = 256 if shard % 256 == 0 else 128

        def one_shard(which, units, rows, target):
            def tile(j, _):
                at = pl.ds(pl.multiple_of(which * shard + j * width, width), width)
                target[at, :] = dot_tn(units[:, at], rows[...]).astype(low)
                return 0

            lax.fori_loop(0, shard // width, tile, 0)

        def all_shards(scatter, units, rows):
            for k in range(1, far):
                one_shard(dp ^ (2 * k + 1), units, rows, scatter.source)
                scatter.core(k).start()
                one_shard(dp ^ (2 * k), units, rows, scatter.source)
            scatter.to_chips()
            one_shard(dp ^ 1, units, rows, scatter.source)
            scatter.core(0).start()
            one_shard(dp, units, rows, scatter.source)

        all_shards(in_scatter, hg_v, rows_v)

        def result_tile(n, _):
            at = pl.ds(pl.multiple_of(n * 256, 256), 256)
            rows_v[:, at] = dot_nn(act_v[...], wout_v[:, at]).astype(low)
            return 0

        lax.fori_loop(0, feat // 256, result_tile, 0)
        all_shards(out_scatter, act_v, grad_v)
        for r in reversed(range(ex_size)):
            result_copy(r).start()
        for copy in stores:
            copy.wait()
        for r in range(ex_size):
            back_copy(r).wait()

    span = fin_hbm.shape[1]
    rows_all = ex_size * cap
    pl.run_scoped(
        expert, pltpu.VMEM((rows_all, hidden), low), pltpu.VMEM((rows_all, hidden), low), pltpu.VMEM((2, span, feat), low),
        pltpu.VMEM((2, span, feat), low), pltpu.VMEM((2, 2, cap, feat), full), pltpu.VMEM((2, 2 * cap, feat), low),
        pltpu.VMEM((rows_all, feat), low), pltpu.VMEM((rows_all // 2, 256), full), pltpu.VMEM((rows_all // 2, 256), full),
        dma((3,)), dma((2, 2)))

    back_v, ret_v, branch_v, da_v = grad_st, token_st, grad_v.at[pl.ds(0, count)], grad_v.at[pl.ds(count, count)]

    def backward(prob_v, proj_v, turned_v, wo_v, pg_v, blocks_v, acc_v, g_v, mg_v, pick_v, dqt_v, sem):
        loads = [pltpu.make_async_copy(source, target, sem.at[i]) for i, (source, target) in enumerate([
            (back_hbm, back_v.at[pl.ds(0, slots)]), (attt_hbm, turned_v), (wo_hbm, wo_v), (prob_hbm, prob_v),
            (proj_hbm, proj_v)])]
        for copy in loads:
            copy.start()
        sums = Sums(sum_chunks(dp_size, ex_size, blocks_v.shape[0]), blocks_v, acc_v, got_v, total_hbm, part_sem, join_sem,
                    own_sem)

        def place_tile(n):
            at = pl.ds(pl.multiple_of(n * 128, 128), 128)
            slot = (n * 128 + lax.broadcasted_iota(jnp.int32, (count, 128), 1)).astype(full)
            return at, slot == column_v[:, 0:1], slot == column_v[:, 1:2]

        def pick_both(n, _):
            at, one, two = place_tile(n)
            pick_v[:, at] = jnp.where(one | two, 1.0, 0.0).astype(low)
            return 0

        lax.fori_loop(0, padded // 128, pick_both, 0)
        loads[0].wait()

        def collect(n, _):
            at = pl.ds(pl.multiple_of(n * 256, 256), 256)
            g_v[:, at] = dot_nn(pick_v[...], back_v[:, at])
            return 0

        lax.fori_loop(0, feat // 256, collect, 0)
        gain_v[...] = jnp.zeros_like(gain_v)
        gain_v[16:24, 0:128] = count_v[...]

        def norm_back(i, whole, gain, target):
            at = pl.ds(pl.multiple_of(i * 64, 64), 64)
            centred = whole - jnp.mean(whole, axis=1, keepdims=True)
            scale = lax.rsqrt(jnp.mean(centred * centred, axis=1, keepdims=True) + 1e-05)
            unit = centred * scale
            grad = g_v[at, :]
            weighted = grad * unit
            gain_v[target:target + 8, :] += jnp.sum(weighted.reshape(8, 8, feat), axis=0)
            scaled = grad * gain
            return at, scale * (scaled - jnp.mean(scaled, axis=1, keepdims=True)
                                - unit * jnp.mean(scaled * unit, axis=1, keepdims=True))

        def second_norm(i, _):
            at, part = norm_back(i, mixed_v[pl.ds(pl.multiple_of(i * 64, 64), 64), :], gain2_ref[...][None], 8)
            grad = cot_ref[at, :].astype(full) + part
            mg_v[at, :] = grad
            branch_v[at, :] = grad.astype(low)
            return 0

        lax.fori_loop(0, count // 64, second_norm, 0)
        loads[1].wait()

        def out_weight(b, _):
            at = pl.ds(pl.multiple_of(b * wide, 128), wide)
            blocks_v[pl.ds(pl.multiple_of(b * feat, 16), feat), :] = dot_nn(turned_v[...], branch_v[:, at]).astype(low)
            return 0

        lax.fori_loop(0, 2, out_weight, 0)
        loads.append(pltpu.make_async_copy(normt_hbm, turned_v, sem.at[5]))
        loads[5].start()
        sums.start(0)
        loads[2].wait()

        def attended_grad(n, _):
            at = pl.ds(pl.multiple_of(n * 256, 256), 256)
            da_v[:, at] = dot_nt(branch_v[...], wo_v[at, :]).astype(low)
            return 0

        lax.fori_loop(0, feat // 256, attended_grad, 0)
        loads[3].wait()
        loads[4].wait()
        lower = lax.broadcasted_iota(jnp.int32, (count, 128), 1) < 64

        def head_pair(p, _):
            at_q = pl.ds(pl.multiple_of(p * 128, 128), 128)
            at_k = pl.ds(pl.multiple_of(feat + p * 128, 128), 128)
            at_v = pl.ds(pl.multiple_of(2 * feat + p * 128, 128), 128)
            q, k, v, da = proj_v[:, at_q], proj_v[:, at_k], proj_v[:, at_v], da_v[:, at_q]
            kt = k.T
            key_near = key_far = value_near = value_far = 0.0
            for j in range(2):
                mask = lower if j == 0 else jnp.logical_not(lower)
                qj, vj, daj = [jnp.where(mask, w, jnp.zeros_like(w)) for w in (q, v, da)]
                for b in range(2):
                    reach, here = (b + 1) * half, slice(b * half, (b + 1) * half)
                    prob = prob_v[2 * p + j, b * half:b * half + reach, :]
                    whole = prob.astype(full)
                    grad = dot_nt(vj[0:reach], da[here])
                    score = (whole * (grad - jnp.sum(whole * grad, axis=0, keepdims=True))).astype(low)
                    dqt_v[64 * j:64 * j + 64, here] = dot_nn(kt[64 * j:64 * j + 64, 0:reach], score)
                    key_near += dot_nn(score[0:half], qj[here])
                    value_near += dot_nn(prob[0:half], daj[here])
                    if b:
                        key_far += dot_nn(score[half:], qj[here])
                        value_far += dot_nn(prob[half:], daj[here])
            pg_v[:, at_q] = (dqt_v[...].T * 0.125).astype(low)
            pg_v[0:half, at_k] = (key_near * 0.125).astype(low)
            pg_v[half:, at_k] = (key_far * 0.125).astype(low)
            pg_v[0:half, at_v] = value_near.astype(low)
            pg_v[half:, at_v] = value_far.astype(low)
            return 0

        for part in range(2):
            lax.fori_loop(part * pairs // 2, (part + 1) * pairs // 2, head_pair, 0)
            if part == 0:
                loads[5].wait()
                in_scatter.finish()
                ends = [pltpu.make_async_copy(icore_v.at[0], dwin_hbm, sem.at[7])]
                ends[-1].start()
                weights = [pltpu.make_async_copy(wqkv_hbm.at[:, pl.ds(c * feat, feat)], win_v.at[pl.ds(c * feat, feat)],
                                                 sem.at[10 + c]) for c in range(3)]
                for copy in weights:
                    copy.start()
            sums.tick()

            def weight_block(c, _, part=part):
                at = pl.ds(pl.multiple_of(c * feat + part * wide, 128), wide)
                into = pl.ds(pl.multiple_of(2 * feat + (3 * part + c) * feat, 16), feat)
                blocks_v[into, :] = dot_nn(turned_v[...], pg_v[:, at]).astype(low)
                return 0

            lax.fori_loop(0, 3, weight_block, 0)
            sums.start(1 + part)
        for copy in weights:
            copy.wait()

        def norm_grad(n, _):
            at = pl.ds(pl.multiple_of(n * 256, 256), 256)
            g_v[:, at] = sum(dot_nt(pg_v[:, c * feat:(c + 1) * feat],
                                    win_v[pl.ds(pl.multiple_of(c * feat + n * 256, 256), 256), :]) for c in range(3))
            return 0

        lax.fori_loop(0, feat // 256, norm_grad, 0)
        sums.tick()

        def first_norm(i, _):
            here = pl.ds(pl.multiple_of(i * 64, 64), 64)
            at, part = norm_back(i, tok_ref[here, :].astype(full), gain1_ref[...][None], 0)
            dtok_ref[at, :] = (mg_v[at, :] + part).astype(low)
            return 0

        lax.fori_loop(0, count // 64, first_norm, 0)

        core, xs, ys, zs = butterfly(dp_size, ex_size)
        order = [[core], ys, xs, zs]
        stages = len(order)
        slot_of = [stages + sum((1 << len(stage)) - 1 for stage in order[:i]) for i in range(stages)]
        for i in range(3):
            small_v[0, i:i + 1, :] = jnp.sum(gain_v[8 * i:8 * i + 8, :], axis=0, keepdims=True)
        small_v[0, 2:3, :] = gain_v[16:17, :]
        small_v[0, 3:8, :] = jnp.zeros((5, feat), full)

        def small_send(i):
            copies = []
            for m, peer in enumerate(group_of(order[i])[1], 1):
                copies.append(remote(small_v.at[i], small_v.at[slot_of[i] + m - 1], tiny_sem, (i, m), peer))
                copies[-1].start()
            return copies

        def small_add(i, copies):
            for copy in copies:
                copy.wait()
            mine, peers = group_of(order[i])
            total = jnp.zeros_like(sum_ref[...])
            for n in range(len(peers) + 1):
                term = small_v[i]
                for m in range(1, len(peers) + 1):
                    term = jnp.where(mine == n ^ m, small_v[slot_of[i] + m - 1], term)
                total = total + term
            if i + 1 < stages:
                small_v[i + 1] = total
                return small_send(i + 1)
            sum_ref[...] = total

        tiny = small_send(0)
        sums.tick()
        sums.tick()
        tiny = small_add(0, tiny)
        out_scatter.finish()
        ends.append(pltpu.make_async_copy(ocore_v.at[0], dwout_hbm, sem.at[8]))
        ends[-1].start()
        for r in range(ex_size):
            result_copy(r).wait()
        load = pltpu.make_async_copy(ret_hbm, ret_v.at[pl.ds(0, slots)], sem.at[9])
        load.start()
        sums.tick()
        tiny = small_add(1, tiny)
        load.wait()
        for turn in range(2):
            def pick_one(n, _, turn=turn):
                at, one, two = place_tile(n)
                pick_v[:, at] = jnp.where((one, two)[turn], 1.0, 0.0).astype(low)
                return 0

            lax.fori_loop(0, padded // 128, pick_one, 0)

            def deliver(n, _, turn=turn):
                at = pl.ds(pl.multiple_of(n * 256, 256), 256)
                term = dot_nn(pick_v[...], ret_v[:, at]) * column_v[:, 4 + turn:5 + turn]
                if turn == 0:
                    g_v[:, at] = term
                else:
                    out_ref[:, at] = (mixed_v[:, at] + (g_v[:, at] + term)).astype(low)
                return 0

            lax.fori_loop(0, feat // 256, deliver, 0)
            sums.tick()
            tiny = small_add(2 + turn, tiny)
        sums.finish()
        for copy in ends:
            copy.wait()

    rows, steps = 8 * feat, 13
    pl.run_scoped(
        backward, pltpu.VMEM((heads, count + half, half), low), pltpu.VMEM((count, 3 * feat), low),
        pltpu.VMEM((feat, count), low), pltpu.VMEM((feat, feat), low), pltpu.VMEM((count, 3 * feat), low),
        pltpu.VMEM((rows, wide), low),
        pltpu.VMEM((rows // 2, wide), low), pltpu.VMEM((count, feat), full), pltpu.VMEM((count, feat), full),
        pltpu.VMEM((count, padded), low), pltpu.VMEM((128, count), full), dma((steps,)))


def layer(tokens, cotangent, chosen, gates, lengths, keep, gain1, gain2, wqkv, wo, in_shard, out_shard, fin, fout, kinds, cap,
          dp_size, ex_size):
    count, feat = tokens.shape
    shard = in_shard.shape[0]
    hidden = dp_size * shard
    far, slots = dp_size // 2, kinds * cap
    padded = (slots + 127) // 128 * 128
    heads, half = feat // 64, count // 2
    rows, wide = 8 * feat, feat // 2
    span = 768 if ex_size * cap <= 1024 else 384
    steps = 2 * hidden // span
    chunks, stages = len(sum_chunks(dp_size, ex_size, rows)), 4
    anyspace, vmem = pl.BlockSpec(memory_space=pl.ANY), pl.BlockSpec(memory_space=pltpu.VMEM)
    dma, shape, buffer = pltpu.SemaphoreType.DMA, jax.ShapeDtypeStruct, pltpu.VMEM
    full, low = jnp.float32, jnp.bfloat16
    scatter = [buffer((far, shard, feat), low), buffer((far - 1, shard, feat), low), buffer((far - 1, shard, feat), low)]
    return pl.pallas_call(
        functools.partial(layer_kernel, dp_size, ex_size, kinds, cap),
        out_shape=(shape((count, feat), low), shape((count, feat), low), shape((rows, wide), low), shape((8, feat), full),
                   shape((shard, feat), low), shape((shard, feat), low),
                   shape((slots, feat), low), shape((slots, feat), low), shape((count, 3 * feat), low),
                   shape((heads, count + half, half), low), shape((feat, count), low), shape((feat, count), low)),
        in_specs=[pl.BlockSpec(memory_space=pltpu.SMEM)] + [vmem] * 7 + [anyspace] * 6,
        out_specs=(vmem, vmem, anyspace, vmem) + (anyspace,) * 8,
        scratch_shapes=[
            buffer((padded, feat), low), buffer((padded, feat), low),
            buffer((ex_size * cap, feat), low), buffer((ex_size * cap, feat), low),
            buffer((hidden, feat), low), buffer((hidden, feat), low)] + scatter + scatter + [
            buffer((rows, wide), low), buffer((count, feat), full), buffer((8, count), full), buffer((count, 8), full),
            buffer((24, feat), full), buffer((8, 128), full), buffer((4 * stages, 8, feat), full),
            dma((2, ex_size)), dma((2, ex_size)), dma((2, ex_size)), dma((2, ex_size)),
            dma((2, 2, far)), dma((2, 2, far)), dma((2, 2, far)), dma((2, 2, far)),
            dma((2, chunks, stages, 4)), dma((2, chunks, stages, 4)), dma((chunks,)),
            dma((2, stages, 4)), dma((3,)), dma((feat // 128,)),
        ],
        compiler_params=pltpu.CompilerParams(collective_id=0, has_side_effects=True, vmem_limit_bytes=63 << 20),
        name="layer",
    )(lengths, chosen.T, gates.T, keep[None], tokens, cotangent, gain1, gain2, wqkv, wo, in_shard, out_shard,
      fin.reshape(steps, span, feat), fout.reshape(steps, span, feat))


def finish_kernel(total_hbm, small_hbm, out_in, dtok_in, dwin_in, dwout_in,
                  out_hbm, dtok_hbm, gain1_ref, qkv_hbm, wide_hbm, gain2_ref, dwin_hbm, dwout_hbm, count_ref,
                  block_v, whole_v, shard_v, shard_w, row_v, small_v, load_sem, store_sem):
    feat = small_v.shape[1]
    wide = feat // 2
    copy = pltpu.make_async_copy
    loads = [copy(total_hbm.at[pl.ds(b * feat, feat)], block_v.at[b], load_sem.at[b]) for b in range(8)]
    loads += [copy(source, shard_v.at[n], load_sem.at[8 + n]) for n, source in enumerate((dwin_in, dwout_in))]
    loads += [copy(source, row_v.at[n], load_sem.at[10 + n]) for n, source in enumerate((out_in, dtok_in))]
    loads.append(copy(small_hbm, small_v, load_sem.at[12]))
    for load in loads:
        load.start()
    stores = []

    def widen(source, target, rows):
        def tile(j, _):
            at = pl.ds(pl.multiple_of(j * 64, 64), 64)
            target[at, :] = source[at, :].astype(jnp.float32)
            return 0

        lax.fori_loop(0, rows // 64, tile, 0)

    def store(source, target):
        stores.append(copy(source, target, store_sem.at[len(stores)]))
        stores[-1].start()

    for b in range(8):
        loads[b].wait()
        widen(block_v.at[b], whole_v.at[b], feat)
        part, c = (b - 2) // 3, (b - 2) % 3
        store(whole_v.at[b],
              wide_hbm.at[:, pl.ds(b * wide, wide)] if b < 2 else qkv_hbm.at[:, pl.ds(c * feat + part * wide, wide)])
    for n, target in enumerate((dwin_hbm, dwout_hbm)):
        loads[8 + n].wait()
        widen(shard_v.at[n], shard_w.at[n], shard_v.shape[1])
        store(shard_w.at[n], target)
    for n, target in enumerate((out_hbm, dtok_hbm)):
        loads[10 + n].wait()
        store(row_v.at[n], target)
    loads[12].wait()
    gain1_ref[...] = small_v[0, :]
    gain2_ref[...] = small_v[1, :]
    count_ref[...] = small_v[2, 0:128]
    for load in stores:
        load.wait()


def finish(total, small, out, dtok, dwin, dwout):
    rows, wide = total.shape
    feat = 2 * wide
    anyspace, vmem = pl.BlockSpec(memory_space=pl.ANY), pl.BlockSpec(memory_space=pltpu.VMEM)
    shape, full, low, buffer = jax.ShapeDtypeStruct, jnp.float32, jnp.bfloat16, pltpu.VMEM
    return pl.pallas_call(
        finish_kernel,
        out_shape=(shape(out.shape, low), shape(dtok.shape, low), shape((feat,), full), shape((feat, 3 * feat), full),
                   shape((feat, feat), full), shape((feat,), full), shape(dwin.shape, full), shape(dwout.shape, full),
                   shape((128,), full)),
        in_specs=[anyspace] * 6,
        out_specs=(anyspace, anyspace, vmem, anyspace, anyspace, vmem, anyspace, anyspace, vmem),
        scratch_shapes=[buffer((8, feat, wide), low), buffer((8, feat, wide), full), buffer((2,) + dwin.shape, low),
                        buffer((2,) + dwin.shape, full), buffer((2,) + out.shape, low), buffer(small.shape, full),
                        pltpu.SemaphoreType.DMA((13,)), pltpu.SemaphoreType.DMA((12,))],
        compiler_params=pltpu.CompilerParams(vmem_limit_bytes=63 << 20),
        name="finish",
    )(total, small, out, dtok, dwin, dwout)


FROZEN = 2


def body(
    tokens,
    cotangent,
    chosen,
    gates,
    lengths,
    keep_mask,
    gain1,
    w_qkv,
    w_o,
    gain2,
    frozen_in,
    frozen_out,
    w_in,
    w_out,
):
    row_count, feat_width = tokens.shape
    owners = lax.axis_size("expert")
    dp_size = lax.axis_size("dp")
    kind_count = FROZEN + owners
    slot_count = ((2 * row_count * 5 // (4 * kind_count) + 7) // 8 * 8 + 15) // 16 * 16
    output, tokens_grad, total, small_sum, d_w_in, d_w_out = layer(
        tokens, cotangent, chosen, gates, lengths, keep_mask, gain1, gain2, w_qkv, w_o, w_in[0], w_out[0], frozen_in,
        frozen_out, kind_count, slot_count, dp_size, owners)[:6]
    output, tokens_grad, gain1_sum, w_qkv_sum, w_o_sum, gain2_sum, d_w_in, d_w_out, counts = finish(
        total, small_sum, output, tokens_grad, d_w_in, d_w_out)
    return (
        output,
        tokens_grad,
        gain1_sum,
        w_qkv_sum,
        w_o_sum,
        gain2_sum,
        d_w_in[None],
        d_w_out[None],
        counts[:kind_count],
    )


def solution(mesh):
    placed = (
        P(("dp", "expert"), None),
        P(("dp", "expert"), None),
        P(("dp", "expert"), None),
        P(("dp", "expert"), None),
        P(("dp", "expert"), None),
        P(("dp", "expert")),
        P(),
        P(),
        P(),
        P(),
        P(),
        P(),
        P("expert", "dp", None),
        P("expert", "dp", None),
    )
    return jax.shard_map(
        body,
        mesh=mesh,
        in_specs=placed,
        out_specs=(
            P(("dp", "expert"), None),
            P(("dp", "expert"), None),
            P(),
            P(),
            P(),
            P(),
            P("expert", "dp", None),
            P("expert", "dp", None),
            P(),
        ),
        check_vma=False,
    )
```
